32 devices in a mesh: elem: 16 (over z, y, core), range: 2 (over x).
Axes of the slice: x: 2, y: 2, z: 4, core: 2. Of those that a mesh axis runs over, the one named last changes fastest.
Arguments:
- echoes: bfloat16 [2, 512, 128, 256], P(None, 'elem', None, 'range'), may hold values from -6 to 6
- replica: bfloat16 [2, 64], replicated, may hold values from -0.5 to 0.5
- beam_weights: bfloat16 [2, 64, 512], replicated, as said below
- steering: float32 [2, 128, 64], P(None, 'elem'), may hold values from -0.5 to 0.5
Outputs:
- adapted: float32 [2, 128, 256], P(None, 'elem', 'range')
The draws below stay inside these ranges and needn't reach their ends.
Inputs may be any that keep to these rules, and one draw needn't show every extreme that they name: `beam_weights`: coefficients for 64 beams over all 512 elements.
All inputs are finite; a program needn't handle non-finite values.
Results may differ from the reference program's by a relative error of at most 0.0086.
Values may be sent and summed in bfloat16 or wider, within the bound.
No kernel may reach another device: no remote copies, remote signals or barrier semaphores. Data moves between devices by JAX's collectives and lax.ppermute only.
A program may use at most 64 MiB of HBM per device.

```python
import jax
import jax.numpy as jnp
from jax import lax

ELEMENTS = 512
PULSES = 128
BEAMS = 64
TAPS = 64
RG_DEV = 128
GATES = 256
N_RANGE = 2


def draw_beam_weights(key, part):
    first_key, second_key = jax.random.split(jax.random.fold_in(key, 7), 2)
    common = jax.random.normal(first_key, (2, 1, ELEMENTS), jnp.float32)
    individual = jax.random.normal(second_key, (2, BEAMS, ELEMENTS), jnp.float32)
    values = (common + 0.6 * individual) / jnp.sqrt(jnp.float32(ELEMENTS))
    return values.astype(jnp.bfloat16)


def level_of(stream_key, dims, cuts, low, high):
    loudness, own = 1.0, jax.random.fold_in(stream_key, 6)
    for axis_at, blocks in cuts:
        draws = jnp.exp(jax.random.uniform(jax.random.fold_in(own, axis_at), (blocks,), jnp.float32, low / len(cuts), high / len(cuts)))
        loudness = loudness * jnp.repeat(draws, dims[axis_at] // blocks).reshape([-1 if axis == axis_at else 1 for axis in range(len(dims))])
    return loudness


def scatter_about(key, shape, scale, limit, cuts=(), held_as=jnp.bfloat16):
    level = level_of(key, shape, cuts, -0.22, 0.18) if cuts else 1.0
    entries = jax.random.normal(key, shape, jnp.float32) * scale * level
    return jnp.minimum(jnp.maximum(entries, -limit), limit).astype(held_as)


def setup_inputs(seed: int = 0) -> dict:
    keys = jax.random.split(jax.random.key(seed), 5)
    echoes = scatter_about(keys[0], (2, ELEMENTS, PULSES, GATES), 1.0, 6.0, ((1, 16), (3, 2)))
    replica = scatter_about(keys[1], (2, TAPS), (2 * TAPS) ** -0.5, 0.5)
    beam_weights = draw_beam_weights(jax.random.fold_in(keys[4], 71), 0)
    steering = scatter_about(keys[3], (2, PULSES, BEAMS), 0.09, 0.5, ((1, 16),), jnp.float32)
    return dict(echoes=echoes, replica=replica, beam_weights=beam_weights, steering=steering)


load_ratio = 0.1
epsilon = 1e-06

def correlation_matrix(tap_values, gate_count):
    tap_count = tap_values.shape[0]
    span_width = gate_count + tap_count - 1
    padded_taps = jnp.concatenate([tap_values, jnp.zeros((span_width + 1 - tap_count,), tap_values.dtype)])
    tiled_rows = jnp.tile(padded_taps, gate_count)[:gate_count * span_width].reshape(gate_count, span_width)
    return tiled_rows.T

def pulse_kernel(replica, gate_count):
    real_part = correlation_matrix(replica[0], gate_count)
    imag_part = correlation_matrix(replica[1], gate_count)
    return jnp.stack([jnp.stack([real_part, imag_part]), jnp.stack([-imag_part, real_part])])

def doppler_kernel(pulses):
    bin_index = jnp.arange(pulses, dtype=jnp.int32)
    pulse_index = jnp.arange(pulses, dtype=jnp.int32)
    phase_index = bin_index[:, None] * pulse_index[None, :] % pulses
    phase_angle = 2.0 * jnp.pi * phase_index.astype(jnp.float32) / pulses
    scale = 1.0 / jnp.sqrt(jnp.float32(pulses))
    cosine = jnp.cos(phase_angle) * scale
    sine = jnp.sin(phase_angle) * scale
    table = jnp.stack([jnp.stack([cosine, -sine]), jnp.stack([sine, cosine])])
    return table.astype(jnp.bfloat16)

def beam_kernel(beam_weights):
    weight_re = beam_weights[0]
    weight_im = beam_weights[1]
    return jnp.stack([jnp.stack([weight_re, weight_im]), jnp.stack([-weight_im, weight_re])])

def adapt(gram_sum, steering, formed):
    beams = formed.shape[2]
    cov_re = gram_sum[:, :beams, :beams] + gram_sum[:, beams:, beams:]
    cov_im = gram_sum[:, beams:, :beams] - gram_sum[:, :beams, beams:]
    loading = load_ratio * jnp.trace(cov_re, axis1=1, axis2=2) / beams + epsilon
    upper = jnp.concatenate([cov_re, -cov_im], axis=2)
    lower = jnp.concatenate([cov_im, cov_re], axis=2)
    system = jnp.concatenate([upper, lower], axis=1)
    system = system + loading[:, None, None] * jnp.eye(2 * beams, dtype=jnp.float32)[None]
    factor = jnp.linalg.cholesky(system)
    right_side = jnp.concatenate([steering[0], steering[1]], axis=-1)
    solved = jax.scipy.linalg.cho_solve((factor, True), right_side[..., None])[..., 0]
    response = lax.optimization_barrier(jnp.sum(right_side * solved, axis=-1))
    weights = solved / response[:, None]
    weight_re = weights[:, :beams]
    weight_im = weights[:, beams:]
    beam_re = formed[:, 0].astype(jnp.float32)
    beam_im = formed[:, 1].astype(jnp.float32)
    high = lax.Precision.HIGHEST
    out_re = jnp.einsum('db,dbr->dr', weight_re, beam_re, precision=high) + jnp.einsum('db,dbr->dr', weight_im, beam_im, precision=high)
    out_im = jnp.einsum('db,dbr->dr', weight_re, beam_im, precision=high) - jnp.einsum('db,dbr->dr', weight_im, beam_re, precision=high)
    return jnp.stack([out_re, out_im])

def reference(echoes, replica, beam_weights, steering):
    pulse_table = pulse_kernel(replica, RG_DEV).astype(jnp.float32)
    tail_zeros = jnp.zeros((2, ELEMENTS, PULSES, TAPS - 1), jnp.bfloat16)
    padded = jnp.concatenate([echoes, tail_zeros], axis=3)

    def compress_block(first_gate):
        segment = lax.dynamic_slice_in_dim(padded, first_gate, RG_DEV + TAPS - 1, 3).astype(jnp.float32)
        return jnp.einsum('cepj,cojr->oepr', segment, pulse_table).astype(jnp.bfloat16)
    block_starts = jnp.arange(N_RANGE, dtype=jnp.int32) * RG_DEV
    compressed_blocks = lax.map(compress_block, block_starts)
    compressed = jnp.moveaxis(compressed_blocks, 0, 3).reshape(2, ELEMENTS, PULSES, GATES)
    dft_table = doppler_kernel(PULSES).astype(jnp.float32)
    doppler = jnp.einsum('cepr,codp->oedr', compressed.astype(jnp.float32), dft_table).astype(jnp.bfloat16)
    beam_table = beam_kernel(beam_weights).astype(jnp.float32)
    formed = jnp.einsum('cedr,cobe->dobr', doppler.astype(jnp.float32), beam_table).astype(jnp.bfloat16)
    stacked = formed.reshape(PULSES, 2 * BEAMS, GATES).astype(jnp.float32)
    gram_sum = jnp.einsum('dbr,dcr->dbc', stacked, stacked, precision=lax.Precision.HIGHEST) / GATES
    return adapt(gram_sum, steering, formed)
```

```python
import functools

import jax
import jax.numpy as jnp
import numpy as np
from jax import lax
from jax.experimental import pallas as pl
from jax.experimental.pallas import tpu as pltpu
from jax.sharding import PartitionSpec as P

load_ratio = 0.1
epsilon = 1e-06
VMEM_BYTES = 56 << 20


def shifted(value, axis, steps):
    count = lax.axis_size(axis)
    first, last = (max(0, -steps), min(count, count - steps))
    return lax.ppermute(value, axis, [(source, source + steps) for source in range(first, last)])


def correlation_matrix(tap_values, gate_count):
    tap_count = tap_values.shape[0]
    span_width = gate_count + tap_count - 1
    padded_taps = jnp.concatenate(
        [tap_values, jnp.zeros((span_width + 1 - tap_count,), tap_values.dtype)]
    )
    tiled_rows = jnp.tile(padded_taps, gate_count)[: gate_count * span_width].reshape(
        gate_count, span_width
    )
    return tiled_rows.T


def pulse_kernel(replica, gate_count):
    real_part = correlation_matrix(replica[0], gate_count)
    imag_part = correlation_matrix(replica[1], gate_count)
    return jnp.stack([jnp.stack([real_part, imag_part]), jnp.stack([-imag_part, real_part])])


def doppler_table(pulses):
    index = np.arange(pulses, dtype=np.int64)
    phase_index = (index[:, None] * index[None, :]) % pulses
    phase_angle = np.float32(2.0 * np.pi) * phase_index.astype(np.float32) / np.float32(pulses)
    scale = np.float32(1.0) / np.sqrt(np.float32(pulses))
    cosine = np.cos(phase_angle) * scale
    sine = np.sin(phase_angle) * scale
    table = np.stack([np.stack([cosine, -sine]), np.stack([sine, cosine])])
    return table.astype(jnp.bfloat16)


def beam_kernel(beam_weights):
    weight_re = beam_weights[0]
    weight_im = beam_weights[1]
    return jnp.stack([jnp.stack([weight_re, weight_im]), jnp.stack([-weight_im, weight_re])])


def adapt(gram_sum, steering, formed):
    beams = formed.shape[2]
    cov_re = gram_sum[:, :beams, :beams] + gram_sum[:, beams:, beams:]
    cov_im = gram_sum[:, beams:, :beams] - gram_sum[:, :beams, beams:]
    loading = load_ratio * jnp.trace(cov_re, axis1=1, axis2=2) / beams + epsilon
    upper = jnp.concatenate([cov_re, -cov_im], axis=2)
    lower = jnp.concatenate([cov_im, cov_re], axis=2)
    system = jnp.concatenate([upper, lower], axis=1)
    system = system + loading[:, None, None] * jnp.eye(2 * beams, dtype=jnp.float32)[None]
    factor = jnp.linalg.cholesky(system)
    right_side = jnp.concatenate([steering[0], steering[1]], axis=-1)
    solved = jax.scipy.linalg.cho_solve((factor, True), right_side[..., None])[..., 0]
    response = jnp.sum(right_side * solved, axis=-1)
    weights = solved / response[:, None]
    weight_re = weights[:, :beams]
    weight_im = weights[:, beams:]
    beam_re = formed[:, 0].astype(jnp.float32)
    beam_im = formed[:, 1].astype(jnp.float32)
    high = lax.Precision.HIGHEST
    out_re = jnp.einsum("db,dbr->dr", weight_re, beam_re, precision=high) + jnp.einsum(
        "db,dbr->dr", weight_im, beam_im, precision=high
    )
    out_im = jnp.einsum("db,dbr->dr", weight_re, beam_im, precision=high) - jnp.einsum(
        "db,dbr->dr", weight_im, beam_re, precision=high
    )
    return jnp.stack([out_re, out_im])


def on_device_general(echoes, replica, beam_weights, steering):
    pulses = echoes.shape[2]
    gate_count = echoes.shape[3]
    tap_count = replica.shape[1]
    following = shifted(echoes[:, :, :, : tap_count - 1], "range", -1)
    padded = jnp.concatenate([echoes, following], axis=3)
    compressed = jnp.einsum(
        "cepj,cojr->oepr",
        padded,
        pulse_kernel(replica, gate_count),
        preferred_element_type=jnp.float32,
    ).astype(jnp.bfloat16)
    doppler = jnp.einsum(
        "cepr,codp->oedr",
        compressed,
        jnp.asarray(doppler_table(pulses)),
        preferred_element_type=jnp.float32,
    ).astype(jnp.bfloat16)
    kernel_full = beam_kernel(beam_weights)
    own_bins = pulses // lax.axis_size("elem")
    beam_sums = jnp.einsum(
        "cedr,cobe->dobr",
        lax.all_to_all(doppler, "elem", split_axis=2, concat_axis=1, tiled=True),
        kernel_full,
        preferred_element_type=jnp.float32,
    )
    formed = beam_sums.astype(jnp.bfloat16)
    beams = formed.shape[2]
    stacked = formed.reshape(own_bins, 2 * beams, gate_count)
    partial_gram = jnp.einsum("dbr,dcr->dbc", stacked, stacked, preferred_element_type=jnp.float32)
    gram_sum = lax.psum(partial_gram, "range") / (gate_count * lax.axis_size("range"))
    return adapt(gram_sum, steering, formed)


def whole_vmem(count):
    return [pl.BlockSpec(memory_space=pltpu.VMEM)] * count


def spectra_body(table_ref, echo_ref, out_ref):
    table = table_ref[...]
    owners = out_ref.shape[0]
    gates = echo_ref.shape[3]
    for pair in range(echo_ref.shape[1] // 2):
        even, odd = 2 * pair, 2 * pair + 1
        samples = jnp.concatenate(
            [
                jnp.concatenate([echo_ref[0, even], echo_ref[0, odd]], axis=1),
                jnp.concatenate([echo_ref[1, even], echo_ref[1, odd]], axis=1),
            ],
            axis=0,
        )
        bins = jnp.dot(table, samples, preferred_element_type=jnp.float32)
        bins = bins.reshape(owners, bins.shape[0] // owners, 2 * gates)
        rows = jnp.concatenate([bins[:, :, :gates], bins[:, :, gates:]], axis=1)
        out_ref[:, pair] = rows.astype(jnp.bfloat16)


def spectra(echoes, devices, block=8):
    _, elements, pulses, gates = echoes.shape
    bins = pulses // devices
    table = doppler_table(pulses)
    table = table.transpose(2, 1, 0, 3).reshape(devices, bins, 2, 2 * pulses)
    table = table.transpose(0, 2, 1, 3).reshape(2 * pulses, 2 * pulses)
    return pl.pallas_call(
        spectra_body,
        grid=(elements // block,),
        in_specs=[
            pl.BlockSpec((2 * pulses, 2 * pulses), lambda i: (0, 0)),
            pl.BlockSpec((2, block, pulses, gates), lambda i: (0, i, 0, 0)),
        ],
        out_specs=pl.BlockSpec((devices, block // 2, 4 * bins, gates), lambda i: (0, i, 0, 0)),
        out_shape=jax.ShapeDtypeStruct((devices, elements // 2, 4 * bins, gates), jnp.bfloat16),
        compiler_params=pltpu.CompilerParams(vmem_limit_bytes=VMEM_BYTES),
        name="spectra",
    )(jnp.asarray(table), echoes)


def spread_body(weight_ref, out_ref, *, bins):
    beams = weight_ref.shape[1]
    elements = weight_ref.shape[2]
    group = 128
    width = group * 2 * bins
    lane = lax.broadcasted_iota(jnp.int32, (group, width), 1)
    row = lax.broadcasted_iota(jnp.int32, (group, width), 0)
    repeat = jnp.where(lane // (2 * bins) == row, 1.0, 0.0).astype(jnp.bfloat16)
    col = lax.broadcasted_iota(jnp.int32, (beams, width), 1)
    is_real = (col // bins) % 2 == 0
    own = col % bins
    for at in range(elements // group):
        span = slice(at * group, (at + 1) * group)
        real = jnp.dot(weight_ref[0, :, span], repeat, preferred_element_type=jnp.float32)
        imag = jnp.dot(weight_ref[1, :, span], repeat, preferred_element_type=jnp.float32)
        to_real = jnp.where(is_real, real, -imag)
        to_imag = jnp.where(is_real, imag, real)
        for d in range(bins):
            here = slice(at * width, (at + 1) * width)
            base = d * 2 * beams
            out_ref[base : base + beams, here] = jnp.where(own == d, to_real, 0.0).astype(jnp.bfloat16)
            out_ref[base + beams : base + 2 * beams, here] = jnp.where(own == d, to_imag, 0.0).astype(
                jnp.bfloat16
            )


def spread(beam_weights, bins):
    _, beams, elements = beam_weights.shape
    return pl.pallas_call(
        functools.partial(spread_body, bins=bins),
        in_specs=whole_vmem(1),
        out_specs=whole_vmem(1)[0],
        out_shape=jax.ShapeDtypeStruct((bins * 2 * beams, elements * 2 * bins), jnp.bfloat16),
        compiler_params=pltpu.CompilerParams(vmem_limit_bytes=VMEM_BYTES),
        name="spread",
    )(beam_weights)


def split(value):
    high = value.astype(jnp.bfloat16)
    return high, (value - high.astype(jnp.float32)).astype(jnp.bfloat16)


NT = (((1,), (1,)), ((), ()))


def eliminate(systems, rows):
    count = len(systems)
    beams = 8 * len(systems[0])
    lane = lax.broadcasted_iota(jnp.int32, (8, 2 * beams), 1)
    sub = lax.broadcasted_iota(jnp.int32, (8, 2 * beams), 0)
    shape = (8, 2 * beams)
    for k in range(beams):
        block, inside = divmod(k, 8)
        for n in range(count):
            a = systems[n]
            pivot_row = jnp.broadcast_to(a[block][inside : inside + 1, :], shape)
            pivot = jnp.broadcast_to(pivot_row[:, k : k + 1], shape)
            inverse = 1.0 / pivot
            is_re = lane == k
            is_im = lane == beams + k
            unit = jnp.where(is_re, 1.0, jnp.where(is_im, 0.0, pivot_row))
            turned = pltpu.roll(unit, beams, 1)
            turned = jnp.where(lane < beams, -turned, turned)
            scaled = unit * inverse
            turned = turned * inverse
            for v in range(block, len(a) + 1):
                part = rows[n] if v == len(a) else a[v]
                re = jnp.broadcast_to(part[:, k : k + 1], shape)
                im = jnp.broadcast_to(part[:, beams + k : beams + k + 1], shape)
                kept = jnp.where(is_re | is_im, 0.0, part)
                new = kept - re * scaled - im * turned
                if v == block:
                    new = jnp.where(sub > inside, new, part)
                if v == len(a):
                    rows[n] = new
                else:
                    a[v] = new
    return rows


def beams_body(side_ref, spectra_ref, spread_ref, pulse_ref, steer_ref, own_ref, send_ref):
    bins = steer_ref.shape[0]
    total = spread_ref.shape[0]
    beams = total // (2 * bins)
    ranges = spectra_ref.shape[1]
    gates = ranges * spectra_ref.shape[4]
    width = spectra_ref.shape[0] * spectra_ref.shape[2] * spectra_ref.shape[3]
    received = jnp.concatenate(
        [spectra_ref[:, j].reshape(width, gates // ranges) for j in range(ranges)], axis=1
    )
    sums = jnp.dot(spread_ref[...], received, preferred_element_type=jnp.float32)
    wide = jnp.concatenate(
        [
            jnp.concatenate(
                [sums[d * 2 * beams : d * 2 * beams + beams], sums[d * 2 * beams + beams : (d + 1) * 2 * beams]],
                axis=1,
            )
            for d in range(bins)
        ],
        axis=0,
    )
    high, low = split(wide)
    pulse = pulse_ref[...]
    formed = jnp.dot(high, pulse, preferred_element_type=jnp.float32) + jnp.dot(
        low, pulse, preferred_element_type=jnp.float32
    )
    sub = lax.broadcasted_iota(jnp.int32, (beams, 2 * beams), 0)
    lane = lax.broadcasted_iota(jnp.int32, (beams, 2 * beams), 1)
    systems, rows, both = [], [], []
    for d in range(bins):
        real = formed[d * beams : (d + 1) * beams, :gates]
        imag = formed[d * beams : (d + 1) * beams, gates:]
        top = jnp.concatenate([real, imag], axis=1)
        whole = jnp.concatenate([top, jnp.concatenate([-imag, real], axis=1)], axis=0)
        g_high, g_low = split(whole)
        both.append((g_high, g_low))
        cov = lax.dot_general(g_high[:beams], g_high, NT, preferred_element_type=jnp.float32)
        cov = cov + lax.dot_general(g_high[:beams], g_low, NT, preferred_element_type=jnp.float32)
        cov = cov + lax.dot_general(g_low[:beams], g_high, NT, preferred_element_type=jnp.float32)
        cov = cov * (1.0 / gates)
        on_diagonal = sub == lane
        trace = jnp.sum(jnp.where(on_diagonal, cov, 0.0), axis=(0, 1), keepdims=True)
        loading = load_ratio * trace / beams + epsilon
        cov = jnp.where(on_diagonal, cov + loading, cov)
        systems.append([cov[8 * v : 8 * v + 8] for v in range(beams // 8)])
        rows.append(jnp.broadcast_to(steer_ref[d : d + 1, :], (8, 2 * beams)))
    rows = eliminate(systems, rows)
    own_side = side_ref[0] == 0
    half = gates // ranges
    for d in range(bins):
        conj = -rows[d]
        steer = jnp.broadcast_to(steer_ref[d : d + 1, :], (8, 2 * beams))
        response = jnp.sum(conj * steer, axis=1, keepdims=True)
        weight = conj / response
        w_high, w_low = split(weight)
        g_high, g_low = both[d]
        out = jnp.dot(w_high, g_high, preferred_element_type=jnp.float32)
        out = out + jnp.dot(w_high, g_low, preferred_element_type=jnp.float32)
        out = out + jnp.dot(w_low, g_high, preferred_element_type=jnp.float32)
        for part in range(2):
            first = out[:1, part * gates : part * gates + half]
            second = out[:1, part * gates + half : (part + 1) * gates]
            own_ref[part, d : d + 1, :] = jnp.where(own_side, first, second)
            send_ref[part, d : d + 1, :] = jnp.where(own_side, second, first)


def on_device_owned(echoes, replica, beam_weights, steering):
    elems, ranges = lax.axis_size("elem"), lax.axis_size("range")
    devices = elems * ranges
    _, own_elements, pulses, gate_count = echoes.shape
    bins = pulses // devices
    beams = beam_weights.shape[1]
    gates = gate_count * ranges
    side = lax.axis_index("range")
    bound = lax.all_to_all(spectra(echoes, devices), ("elem", "range"), 0, 0, tiled=True)
    bound = bound.reshape(elems, ranges, own_elements // 2, 4 * bins, gate_count)
    pulse = pulse_kernel(replica, gates)[:, :, :gates]
    pulse = pulse.transpose(0, 2, 1, 3).reshape(2 * gates, 2 * gates)
    own_steering = lax.dynamic_slice_in_dim(steering, side * bins, bins, 1)
    steer_row = jnp.concatenate([own_steering[0], -own_steering[1]], axis=1)
    shape = jax.ShapeDtypeStruct((2, bins, gate_count), jnp.float32)
    own, send = pl.pallas_call(
        beams_body,
        in_specs=[pl.BlockSpec(memory_space=pltpu.SMEM)] + whole_vmem(4),
        out_specs=whole_vmem(2),
        out_shape=[shape, shape],
        compiler_params=pltpu.CompilerParams(vmem_limit_bytes=VMEM_BYTES),
        name="beams",
    )(side.reshape(1).astype(jnp.int32), bound, spread(beam_weights, bins), pulse, steer_row)
    other = lax.ppermute(send, "range", [(0, 1), (1, 0)])
    first = jnp.where(side == 0, own, other)
    second = jnp.where(side == 0, other, own)
    return jnp.concatenate([first, second], axis=1)


def on_device(echoes, replica, beam_weights, steering):
    elems, ranges = lax.axis_size("elem"), lax.axis_size("range")
    pulses, gate_count = echoes.shape[2:]
    beams, elements = beam_weights.shape[1:]
    owned = (
        ranges == 2
        and pulses == 4 * elems * ranges
        and gate_count % 128 == 0
        and beams == 64
        and elements % 128 == 0
        and echoes.shape[1] % 8 == 0
        and replica.shape[1] <= gate_count
    )
    run = on_device_owned if owned else on_device_general
    return run(echoes, replica, beam_weights, steering)


def solution(mesh):
    return jax.shard_map(
        on_device,
        mesh=mesh,
        in_specs=(P(None, "elem", None, "range"), P(), P(), P(None, "elem", None)),
        out_specs=P(None, "elem", "range"),
        check_vma=False,
    )
```

```python
import functools

import jax
import jax.numpy as jnp
import numpy as np
from jax import lax
from jax.experimental import pallas as pl
from jax.experimental.pallas import tpu as pltpu
from jax.sharding import PartitionSpec as P

load_ratio = 0.1
epsilon = 1e-06
SPECTRA_VMEM = 56 << 20
SMALL_VMEM = 14 << 20
BEAMS_VMEM = 24 << 20


def shifted(value, axis, steps):
    count = lax.axis_size(axis)
    first, last = (max(0, -steps), min(count, count - steps))
    return lax.ppermute(value, axis, [(source, source + steps) for source in range(first, last)])


def correlation_matrix(tap_values, gate_count):
    tap_count = tap_values.shape[0]
    span_width = gate_count + tap_count - 1
    padded_taps = jnp.concatenate(
        [tap_values, jnp.zeros((span_width + 1 - tap_count,), tap_values.dtype)]
    )
    tiled_rows = jnp.tile(padded_taps, gate_count)[: gate_count * span_width].reshape(
        gate_count, span_width
    )
    return tiled_rows.T


def pulse_kernel(replica, gate_count):
    real_part = correlation_matrix(replica[0], gate_count)
    imag_part = correlation_matrix(replica[1], gate_count)
    return jnp.stack([jnp.stack([real_part, imag_part]), jnp.stack([-imag_part, real_part])])


def doppler_table(pulses):
    index = np.arange(pulses, dtype=np.int64)
    phase_index = (index[:, None] * index[None, :]) % pulses
    phase_angle = np.float32(2.0 * np.pi) * phase_index.astype(np.float32) / np.float32(pulses)
    scale = np.float32(1.0) / np.sqrt(np.float32(pulses))
    cosine = np.cos(phase_angle) * scale
    sine = np.sin(phase_angle) * scale
    table = np.stack([np.stack([cosine, -sine]), np.stack([sine, cosine])])
    return table.astype(jnp.bfloat16)


def beam_kernel(beam_weights):
    weight_re = beam_weights[0]
    weight_im = beam_weights[1]
    return jnp.stack([jnp.stack([weight_re, weight_im]), jnp.stack([-weight_im, weight_re])])


def adapt(gram_sum, steering, formed):
    beams = formed.shape[2]
    cov_re = gram_sum[:, :beams, :beams] + gram_sum[:, beams:, beams:]
    cov_im = gram_sum[:, beams:, :beams] - gram_sum[:, :beams, beams:]
    loading = load_ratio * jnp.trace(cov_re, axis1=1, axis2=2) / beams + epsilon
    upper = jnp.concatenate([cov_re, -cov_im], axis=2)
    lower = jnp.concatenate([cov_im, cov_re], axis=2)
    system = jnp.concatenate([upper, lower], axis=1)
    system = system + loading[:, None, None] * jnp.eye(2 * beams, dtype=jnp.float32)[None]
    factor = jnp.linalg.cholesky(system)
    right_side = jnp.concatenate([steering[0], steering[1]], axis=-1)
    solved = jax.scipy.linalg.cho_solve((factor, True), right_side[..., None])[..., 0]
    response = jnp.sum(right_side * solved, axis=-1)
    weights = solved / response[:, None]
    weight_re = weights[:, :beams]
    weight_im = weights[:, beams:]
    beam_re = formed[:, 0].astype(jnp.float32)
    beam_im = formed[:, 1].astype(jnp.float32)
    high = lax.Precision.HIGHEST
    out_re = jnp.einsum("db,dbr->dr", weight_re, beam_re, precision=high) + jnp.einsum(
        "db,dbr->dr", weight_im, beam_im, precision=high
    )
    out_im = jnp.einsum("db,dbr->dr", weight_re, beam_im, precision=high) - jnp.einsum(
        "db,dbr->dr", weight_im, beam_re, precision=high
    )
    return jnp.stack([out_re, out_im])


def on_device_general(echoes, replica, beam_weights, steering):
    pulses = echoes.shape[2]
    gate_count = echoes.shape[3]
    tap_count = replica.shape[1]
    following = shifted(echoes[:, :, :, : tap_count - 1], "range", -1)
    padded = jnp.concatenate([echoes, following], axis=3)
    compressed = jnp.einsum(
        "cepj,cojr->oepr",
        padded,
        pulse_kernel(replica, gate_count),
        preferred_element_type=jnp.float32,
    ).astype(jnp.bfloat16)
    doppler = jnp.einsum(
        "cepr,codp->oedr",
        compressed,
        jnp.asarray(doppler_table(pulses)),
        preferred_element_type=jnp.float32,
    ).astype(jnp.bfloat16)
    kernel_full = beam_kernel(beam_weights)
    own_bins = pulses // lax.axis_size("elem")
    beam_sums = jnp.einsum(
        "cedr,cobe->dobr",
        lax.all_to_all(doppler, "elem", split_axis=2, concat_axis=1, tiled=True),
        kernel_full,
        preferred_element_type=jnp.float32,
    )
    formed = beam_sums.astype(jnp.bfloat16)
    beams = formed.shape[2]
    stacked = formed.reshape(own_bins, 2 * beams, gate_count)
    partial_gram = jnp.einsum("dbr,dcr->dbc", stacked, stacked, preferred_element_type=jnp.float32)
    gram_sum = lax.psum(partial_gram, "range") / (gate_count * lax.axis_size("range"))
    return adapt(gram_sum, steering, formed)


def whole_vmem(count):
    return [pl.BlockSpec(memory_space=pltpu.VMEM)] * count


def spectra_body(table_ref, echo_ref, out_ref):
    table = table_ref[...]
    owners = out_ref.shape[0]
    gates = echo_ref.shape[3]
    for pair in range(echo_ref.shape[1] // 2):
        even, odd = 2 * pair, 2 * pair + 1
        samples = jnp.concatenate(
            [
                jnp.concatenate([echo_ref[0, even], echo_ref[0, odd]], axis=1),
                jnp.concatenate([echo_ref[1, even], echo_ref[1, odd]], axis=1),
            ],
            axis=0,
        )
        bins = jnp.dot(table, samples, preferred_element_type=jnp.float32)
        bins = bins.reshape(owners, bins.shape[0] // owners, 2 * gates)
        rows = jnp.concatenate([bins[:, :, :gates], bins[:, :, gates:]], axis=1)
        out_ref[:, pair] = rows.astype(jnp.bfloat16)


def spectra(echoes, owners, block=8):
    _, elements, pulses, gates = echoes.shape
    devices = len(owners)
    bins = pulses // devices
    table = doppler_table(pulses)
    table = table.transpose(2, 1, 0, 3).reshape(devices, bins, 2, 2 * pulses)[np.asarray(owners)]
    table = table.transpose(0, 2, 1, 3).reshape(2 * pulses, 2 * pulses)
    return pl.pallas_call(
        spectra_body,
        grid=(elements // block,),
        in_specs=[
            pl.BlockSpec((2 * pulses, 2 * pulses), lambda i: (0, 0)),
            pl.BlockSpec((2, block, pulses, gates), lambda i: (0, i, 0, 0)),
        ],
        out_specs=pl.BlockSpec((devices, block // 2, 4 * bins, gates), lambda i: (0, i, 0, 0)),
        out_shape=jax.ShapeDtypeStruct((devices, elements // 2, 4 * bins, gates), jnp.bfloat16),
        compiler_params=pltpu.CompilerParams(vmem_limit_bytes=SPECTRA_VMEM),
        name="spectra",
    )(jnp.asarray(table), echoes)


def spread_body(weight_ref, out_ref, *, bins):
    beams = weight_ref.shape[1]
    elements = weight_ref.shape[2]
    group = 128
    width = group * 2 * bins
    lane = lax.broadcasted_iota(jnp.int32, (group, width), 1)
    row = lax.broadcasted_iota(jnp.int32, (group, width), 0)
    repeat = jnp.where(lane // (2 * bins) == row, 1.0, 0.0).astype(jnp.bfloat16)
    col = lax.broadcasted_iota(jnp.int32, (beams, width), 1)
    is_real = (col // bins) % 2 == 0
    for at in range(elements // group):
        span = slice(at * group, (at + 1) * group)
        here = slice(at * width, (at + 1) * width)
        real = jnp.dot(weight_ref[0, :, span], repeat, preferred_element_type=jnp.float32)
        imag = jnp.dot(weight_ref[1, :, span], repeat, preferred_element_type=jnp.float32)
        out_ref[:beams, here] = jnp.where(is_real, real, -imag).astype(jnp.bfloat16)
        out_ref[beams:, here] = jnp.where(is_real, imag, real).astype(jnp.bfloat16)


def spread(beam_weights, bins):
    _, beams, elements = beam_weights.shape
    return pl.pallas_call(
        functools.partial(spread_body, bins=bins),
        in_specs=whole_vmem(1),
        out_specs=whole_vmem(1)[0],
        out_shape=jax.ShapeDtypeStruct((2 * beams, elements * 2 * bins), jnp.bfloat16),
        compiler_params=pltpu.CompilerParams(vmem_limit_bytes=SMALL_VMEM),
        name="spread",
    )(beam_weights)


def partial_body(half_ref, spectra_ref, spread_ref, out_ref, *, bins):
    elems, ranges = spectra_ref.shape[:2]
    rows = spectra_ref.shape[3] * spectra_ref.shape[4]
    half = half_ref[0]
    received = jnp.concatenate(
        [
            jnp.concatenate(
                [spectra_ref[n, j, half].reshape(rows, spectra_ref.shape[5]) for n in range(elems)], axis=0
            )
            for j in range(ranges)
        ],
        axis=1,
    )
    weights = spread_ref[...]
    own = lax.broadcasted_iota(jnp.int32, weights.shape, 1) % bins
    for d in range(bins):
        here = jnp.where(own == d, weights, jnp.zeros_like(weights))
        out_ref[d] = jnp.dot(here, received, preferred_element_type=jnp.float32).astype(out_ref.dtype)


def partial_sums(half, bound, spread_weights, bins, dtype):
    shape = (bins, spread_weights.shape[0], bound.shape[1] * bound.shape[5])
    return pl.pallas_call(
        functools.partial(partial_body, bins=bins),
        in_specs=[pl.BlockSpec(memory_space=pltpu.SMEM)] + whole_vmem(2),
        out_specs=whole_vmem(1)[0],
        out_shape=jax.ShapeDtypeStruct(shape, dtype),
        compiler_params=pltpu.CompilerParams(vmem_limit_bytes=BEAMS_VMEM),
        name="partial_sums",
    )(half.reshape(1).astype(jnp.int32), bound, spread_weights)


def split(value):
    high = value.astype(jnp.bfloat16)
    return high, (value - high.astype(jnp.float32)).astype(jnp.bfloat16)


NT = (((1,), (1,)), ((), ()))


def c_mul(a, b):
    return a[0] * b[0] - a[1] * b[1], a[0] * b[1] + a[1] * b[0]
def c_mulc(a, b):
    return a[0] * b[0] + a[1] * b[1], a[1] * b[0] - a[0] * b[1]
def conj(a): return a[0], -a[1]
def c_add(a, b): return a[0] + b[0], a[1] + b[1]
def c_sub(a, b): return a[0] - b[0], a[1] - b[1]
def scale(a, r): return a[0] * r, a[1] * r

def inverse_pair(m):
    a, b, d = m
    r = 1.0 / (a * d - (b[0] * b[0] + b[1] * b[1]))
    return d * r, (-b[0] * r, -b[1] * r), a * r

def inverse_four(e):
    ea, eb, ed = inverse_pair((e[0][0][0], e[0][1], e[1][1][0]))
    f = [[e[0][2], e[0][3]], [e[1][2], e[1][3]]]
    t = [[None, None], [None, None]]
    for l in range(2):
        t[0][l] = c_add(scale(f[0][l], ea), c_mul(eb, f[1][l]))
        t[1][l] = c_add(c_mulc(f[0][l], eb), scale(f[1][l], ed))
    def herm(l, m):
        return c_add(c_mulc(t[0][m], f[0][l]), c_mulc(t[1][m], f[1][l]))
    def herm_re(l):
        return (t[0][l][0]*f[0][l][0] + t[0][l][1]*f[0][l][1]) + (t[1][l][0]*f[1][l][0] + t[1][l][1]*f[1][l][1])
    s = (e[2][2][0] - herm_re(0), c_sub(e[2][3], herm(0, 1)), e[3][3][0] - herm_re(1))
    sa, sb, sd = inverse_pair(s)
    u = [[None, None], [None, None]]
    for j in range(2):
        x = c_add(scale(t[j][0], sa), c_mulc(t[j][1], sb))
        y = c_add(c_mul(t[j][0], sb), scale(t[j][1], sd))
        u[j][0] = (-x[0], -x[1]); u[j][1] = (-y[0], -y[1])
    def corr(j, m):
        return c_add(c_mulc(u[j][0], t[m][0]), c_mulc(u[j][1], t[m][1]))
    zero = jnp.zeros_like(ea)
    p00 = ea - corr(0, 0)[0]; p11 = ed - corr(1, 1)[0]
    p01 = c_sub(eb, corr(0, 1))
    inv = [[None]*4 for _ in range(4)]
    inv[0][0] = (p00, None); inv[1][1] = (p11, None); inv[0][1] = p01
    inv[2][2] = (sa, None); inv[3][3] = (sd, None); inv[2][3] = sb
    for j in range(2):
        for l in range(2): inv[j][2+l] = u[j][l]
    for j in range(4):
        for l in range(j): inv[j][l] = conj(inv[l][j])
    return inv


def eliminate(rows, beams, lookahead=True):
    shape = rows[0].shape
    lane = lax.broadcasted_iota(jnp.int32, shape, 1)
    upper = lax.broadcasted_iota(jnp.int32, shape, 0) < 4
    sign = jnp.where(lane < beams, -1.0, 1.0)
    def turn(x): return pltpu.roll(x, beams, 1) * sign
    def col(x, k): return jnp.broadcast_to(x[:, k:k+1], shape)
    rows = list(rows)
    for k in range(0, beams, 4):
        inside = ((lane >= k) & (lane < k + 4)) | ((lane >= beams + k) & (lane < beams + k + 4))
        r = []
        for q in (k // 2, k // 2 + 1):
            x = rows[q]
            y = pltpu.roll(x, 4, 0)
            r += [jnp.where(upper, x, y), jnp.where(upper, y, x)]
        e = [[None]*4 for _ in range(4)]
        for j in range(4):
            for l in range(j, 4):
                e[j][l] = (col(r[j], k+l), col(r[j], beams+k+l) if l > j else None)
        inv = inverse_four(e)
        unit = [jnp.where(lane == k+l, 1.0, jnp.where(inside, 0.0, r[l])) for l in range(4)]
        turned = [turn(x) for x in unit]
        b, bt = [], []
        for j in range(4):
            acc, tacc = unit[j] * inv[j][j][0], turned[j] * inv[j][j][0]
            for l in range(4):
                if l != j:
                    acc = acc + (unit[l] * inv[j][l][0] + turned[l] * inv[j][l][1])
                    tacc = tacc + (turned[l] * inv[j][l][0] - unit[l] * inv[j][l][1])
            b.append(acc)
            bt.append(tacc)
        for i in range(k//2+2, beams//2+1):
            x = rows[i]
            acc = jnp.where(inside, 0.0, x)
            for l in range(4):
                acc = acc - (col(x, k+l) * b[l] + col(x, beams+k+l) * bt[l])
            rows[i] = acc
    return rows[beams//2]


def beams_body(side_ref, near_ref, far_ref, pulse_ref, steer_ref, own_ref, send_ref, rows_ref):
    bins, total, gates = near_ref.shape
    beams = total // 2
    ranges = gates // own_ref.shape[2]
    sums = [near_ref[d] + far_ref[d].astype(jnp.float32) for d in range(bins)]
    wide = jnp.concatenate(
        [jnp.concatenate([value[:beams], value[beams:]], axis=1) for value in sums], axis=0
    )
    high, low = split(wide)
    pulse = pulse_ref[...]
    formed = jnp.dot(high, pulse, preferred_element_type=jnp.float32) + jnp.dot(
        low, pulse, preferred_element_type=jnp.float32
    )
    sub = lax.broadcasted_iota(jnp.int32, (beams, 2 * beams), 0)
    lane = lax.broadcasted_iota(jnp.int32, (beams, 2 * beams), 1)
    both = []
    for d in range(bins):
        real = formed[d * beams : (d + 1) * beams, :gates]
        imag = formed[d * beams : (d + 1) * beams, gates:]
        top = jnp.concatenate([real, imag], axis=1)
        whole = jnp.concatenate([top, jnp.concatenate([-imag, real], axis=1)], axis=0)
        g_high, g_low = split(whole)
        both.append((g_high, g_low))
        cov = lax.dot_general(g_high[:beams], g_high, NT, preferred_element_type=jnp.float32)
        cov = cov + lax.dot_general(g_high[:beams], g_low, NT, preferred_element_type=jnp.float32)
        cov = cov + lax.dot_general(g_low[:beams], g_high, NT, preferred_element_type=jnp.float32)
        cov = cov * (1.0 / gates)
        on_diagonal = sub == lane
        trace = jnp.sum(jnp.where(on_diagonal, cov, 0.0), axis=(0, 1), keepdims=True)
        loading = load_ratio * trace / beams + epsilon
        cov = jnp.where(on_diagonal, cov + loading, cov)
        rows_ref[pl.ds(d, beams, stride=bins), :] = cov
    steer = steer_ref[...]
    rows = [rows_ref[8 * q : 8 * q + 8] for q in range(beams // 2)]
    rows.append(jnp.concatenate([steer, steer], axis=0))
    conj = -eliminate(rows, beams)[:bins]
    response = jnp.sum(conj * steer, axis=1, keepdims=True)
    weight = conj / response
    w_high, w_low = split(weight)
    first_side = side_ref[0] == 0
    half = gates // ranges
    row = lax.broadcasted_iota(jnp.int32, (bins, half), 0)
    outs = [jnp.zeros((bins, half), jnp.float32)] * (2 * ranges)
    for d in range(bins):
        g_high, g_low = both[d]
        out = jnp.dot(w_high, g_high, preferred_element_type=jnp.float32)
        out = out + jnp.dot(w_high, g_low, preferred_element_type=jnp.float32)
        out = out + jnp.dot(w_low, g_high, preferred_element_type=jnp.float32)
        outs = [
            jnp.where(row == d, out[:, n * half : (n + 1) * half], kept) for n, kept in enumerate(outs)
        ]
    nothing = jnp.zeros((bins, half), jnp.float32)
    for part in range(2):
        first, second = outs[2 * part : 2 * part + 2]
        own_ref[part] = jnp.concatenate(
            [jnp.where(first_side, first, nothing), jnp.where(first_side, nothing, second)], axis=0
        )
        send_ref[part] = jnp.concatenate(
            [jnp.where(first_side, second, nothing), jnp.where(first_side, nothing, first)], axis=0
        )


def on_device_owned(echoes, replica, beam_weights, steering):
    elems, ranges = lax.axis_size("elem"), lax.axis_size("range")
    devices = elems * ranges
    _, own_elements, pulses, gate_count = echoes.shape
    bins = pulses // devices
    elements = beam_weights.shape[2]
    gates = gate_count * ranges
    side = lax.axis_index("range")
    half = lax.axis_index("elem") // (elems // 2)
    group = devices // 2
    owners = [part * group + member for member in range(group) for part in range(2)]
    sent = spectra(echoes, owners).reshape(group, 2, own_elements // 2, 4 * bins, gate_count)
    bound = lax.all_to_all(
        sent,
        ("elem", "range"),
        0,
        0,
        tiled=True,
        axis_index_groups=[list(range(group)), list(range(group, devices))],
    )
    bound = bound.reshape(elems // 2, ranges, 2, own_elements // 2, 4 * bins, gate_count)
    here = lax.dynamic_slice_in_dim(beam_weights, half * (elements // 2), elements // 2, 2)
    spread_weights = spread(here, bins)
    crossing = partial_sums(1 - half, bound, spread_weights, bins, jnp.bfloat16)
    far = lax.ppermute(crossing, "elem", [(n, (n + elems // 2) % elems) for n in range(elems)])
    near = partial_sums(half, bound, spread_weights, bins, jnp.float32)
    pulse = pulse_kernel(replica, gates)[:, :, :gates]
    pulse = pulse.transpose(0, 2, 1, 3).reshape(2 * gates, 2 * gates)
    own_steering = lax.dynamic_slice_in_dim(steering, side * bins, bins, 1)
    steer_row = jnp.concatenate([own_steering[0], -own_steering[1]], axis=1)
    shape = jax.ShapeDtypeStruct((2, 2 * bins, gate_count), jnp.float32)
    own, send = pl.pallas_call(
        beams_body,
        in_specs=[pl.BlockSpec(memory_space=pltpu.SMEM)] + whole_vmem(4),
        out_specs=whole_vmem(2),
        out_shape=[shape, shape],
        scratch_shapes=[pltpu.VMEM((bins * beam_weights.shape[1], 2 * beam_weights.shape[1]), jnp.float32)],
        compiler_params=pltpu.CompilerParams(vmem_limit_bytes=BEAMS_VMEM),
        name="beams",
    )(side.reshape(1).astype(jnp.int32), near, far, pulse, steer_row)
    return own + lax.ppermute(send, "range", [(0, 1), (1, 0)])


def on_device(echoes, replica, beam_weights, steering):
    elems, ranges = lax.axis_size("elem"), lax.axis_size("range")
    pulses, gate_count = echoes.shape[2:]
    beams, elements = beam_weights.shape[1:]
    owned = (
        ranges == 2
        and pulses == 4 * elems * ranges
        and gate_count % 128 == 0
        and beams == 64
        and elems % 2 == 0
        and elements % 256 == 0
        and echoes.shape[1] % 8 == 0
        and replica.shape[1] <= gate_count
    )
    run = on_device_owned if owned else on_device_general
    return run(echoes, replica, beam_weights, steering)


def solution(mesh):
    return jax.shard_map(
        on_device,
        mesh=mesh,
        in_specs=(P(None, "elem", None, "range"), P(), P(), P(None, "elem", None)),
        out_specs=P(None, "elem", "range"),
        check_vma=False,
    )
```

```python
import functools

import jax
import jax.numpy as jnp
import numpy as np
from jax import lax
from jax.experimental import pallas as pl
from jax.experimental.pallas import tpu as pltpu
from jax.sharding import PartitionSpec as P

load_ratio = 0.1
epsilon = 1e-06
SPECTRA_VMEM = 56 << 20
STEPS = 4
SMALL_VMEM = 14 << 20
BEAMS_VMEM = 24 << 20


def shifted(value, axis, steps):
    count = lax.axis_size(axis)
    first, last = (max(0, -steps), min(count, count - steps))
    return lax.ppermute(value, axis, [(source, source + steps) for source in range(first, last)])


def correlation_matrix(tap_values, gate_count):
    tap_count = tap_values.shape[0]
    span_width = gate_count + tap_count - 1
    padded_taps = jnp.concatenate(
        [tap_values, jnp.zeros((span_width + 1 - tap_count,), tap_values.dtype)]
    )
    tiled_rows = jnp.tile(padded_taps, gate_count)[: gate_count * span_width].reshape(
        gate_count, span_width
    )
    return tiled_rows.T


def pulse_kernel(replica, gate_count):
    real_part = correlation_matrix(replica[0], gate_count)
    imag_part = correlation_matrix(replica[1], gate_count)
    return jnp.stack([jnp.stack([real_part, imag_part]), jnp.stack([-imag_part, real_part])])


def doppler_table(pulses):
    index = np.arange(pulses, dtype=np.int64)
    phase_index = (index[:, None] * index[None, :]) % pulses
    phase_angle = np.float32(2.0 * np.pi) * phase_index.astype(np.float32) / np.float32(pulses)
    scale = np.float32(1.0) / np.sqrt(np.float32(pulses))
    cosine = np.cos(phase_angle) * scale
    sine = np.sin(phase_angle) * scale
    table = np.stack([np.stack([cosine, -sine]), np.stack([sine, cosine])])
    return table.astype(jnp.bfloat16)


def beam_kernel(beam_weights):
    weight_re = beam_weights[0]
    weight_im = beam_weights[1]
    return jnp.stack([jnp.stack([weight_re, weight_im]), jnp.stack([-weight_im, weight_re])])


def adapt(gram_sum, steering, formed):
    beams = formed.shape[2]
    cov_re = gram_sum[:, :beams, :beams] + gram_sum[:, beams:, beams:]
    cov_im = gram_sum[:, beams:, :beams] - gram_sum[:, :beams, beams:]
    loading = load_ratio * jnp.trace(cov_re, axis1=1, axis2=2) / beams + epsilon
    upper = jnp.concatenate([cov_re, -cov_im], axis=2)
    lower = jnp.concatenate([cov_im, cov_re], axis=2)
    system = jnp.concatenate([upper, lower], axis=1)
    system = system + loading[:, None, None] * jnp.eye(2 * beams, dtype=jnp.float32)[None]
    factor = jnp.linalg.cholesky(system)
    right_side = jnp.concatenate([steering[0], steering[1]], axis=-1)
    solved = jax.scipy.linalg.cho_solve((factor, True), right_side[..., None])[..., 0]
    response = jnp.sum(right_side * solved, axis=-1)
    weights = solved / response[:, None]
    weight_re = weights[:, :beams]
    weight_im = weights[:, beams:]
    beam_re = formed[:, 0].astype(jnp.float32)
    beam_im = formed[:, 1].astype(jnp.float32)
    high = lax.Precision.HIGHEST
    out_re = jnp.einsum("db,dbr->dr", weight_re, beam_re, precision=high) + jnp.einsum(
        "db,dbr->dr", weight_im, beam_im, precision=high
    )
    out_im = jnp.einsum("db,dbr->dr", weight_re, beam_im, precision=high) - jnp.einsum(
        "db,dbr->dr", weight_im, beam_re, precision=high
    )
    return jnp.stack([out_re, out_im])


def on_device_general(echoes, replica, beam_weights, steering):
    pulses = echoes.shape[2]
    gate_count = echoes.shape[3]
    tap_count = replica.shape[1]
    following = shifted(echoes[:, :, :, : tap_count - 1], "range", -1)
    padded = jnp.concatenate([echoes, following], axis=3)
    compressed = jnp.einsum(
        "cepj,cojr->oepr",
        padded,
        pulse_kernel(replica, gate_count),
        preferred_element_type=jnp.float32,
    ).astype(jnp.bfloat16)
    doppler = jnp.einsum(
        "cepr,codp->oedr",
        compressed,
        jnp.asarray(doppler_table(pulses)),
        preferred_element_type=jnp.float32,
    ).astype(jnp.bfloat16)
    kernel_full = beam_kernel(beam_weights)
    own_bins = pulses // lax.axis_size("elem")
    beam_sums = jnp.einsum(
        "cedr,cobe->dobr",
        lax.all_to_all(doppler, "elem", split_axis=2, concat_axis=1, tiled=True),
        kernel_full,
        preferred_element_type=jnp.float32,
    )
    formed = beam_sums.astype(jnp.bfloat16)
    beams = formed.shape[2]
    stacked = formed.reshape(own_bins, 2 * beams, gate_count)
    partial_gram = jnp.einsum("dbr,dcr->dbc", stacked, stacked, preferred_element_type=jnp.float32)
    gram_sum = lax.psum(partial_gram, "range") / (gate_count * lax.axis_size("range"))
    return adapt(gram_sum, steering, formed)


def whole_vmem(count):
    return [pl.BlockSpec(memory_space=pltpu.VMEM)] * count


def spectra_body(half_ref, table_hbm, echo_hbm, out_hbm, table_ref, echo_ref, out_ref, table_sem, in_sem, out_sem):
    members = out_ref.shape[0]
    gates = echo_ref.shape[3]
    steps = in_sem.shape[0]
    block = echo_ref.shape[1] // steps
    pairs = block // 2
    fetch_table = pltpu.make_async_copy(table_hbm.at[half_ref[0]], table_ref, table_sem)
    fetches = [
        pltpu.make_async_copy(
            echo_hbm.at[:, pl.ds(step * block, block)],
            echo_ref.at[:, pl.ds(step * block, block)],
            in_sem.at[step],
        )
        for step in range(steps)
    ]
    stores = [
        pltpu.make_async_copy(
            out_ref.at[:, pl.ds(step * pairs, pairs)],
            out_hbm.at[:, pl.ds(step * pairs, pairs)],
            out_sem.at[step],
        )
        for step in range(steps)
    ]
    fetch_table.start()
    for fetch in fetches:
        fetch.start()
    fetch_table.wait()
    table = table_ref[...]
    for step in range(steps):
        fetches[step].wait()
        for pair in range(step * pairs, (step + 1) * pairs):
            even, odd = 2 * pair, 2 * pair + 1
            samples = jnp.concatenate(
                [
                    jnp.concatenate([echo_ref[0, even], echo_ref[0, odd]], axis=1),
                    jnp.concatenate([echo_ref[1, even], echo_ref[1, odd]], axis=1),
                ],
                axis=0,
            )
            bins = jnp.dot(table, samples, preferred_element_type=jnp.float32)
            bins = bins.reshape(members, bins.shape[0] // members, 2 * gates)
            rows = jnp.concatenate([bins[:, :, :gates], bins[:, :, gates:]], axis=1)
            out_ref[:, pair] = rows.astype(jnp.bfloat16)
        stores[step].start()
    for store in stores:
        store.wait()


def spectra(half, echoes, devices, steps=STEPS):
    _, elements, pulses, gates = echoes.shape
    bins = pulses // devices
    members = devices // 2
    table = doppler_table(pulses)
    table = table.transpose(2, 1, 0, 3).reshape(devices, bins, 2, 2 * pulses)
    table = table.transpose(0, 2, 1, 3).reshape(2, pulses, 2 * pulses)
    shape = (members, elements // 2, 4 * bins, gates)
    return pl.pallas_call(
        spectra_body,
        in_specs=[pl.BlockSpec(memory_space=pltpu.SMEM)] + [pl.BlockSpec(memory_space=pl.ANY)] * 2,
        out_specs=pl.BlockSpec(memory_space=pl.ANY),
        out_shape=jax.ShapeDtypeStruct(shape, jnp.bfloat16),
        scratch_shapes=[
            pltpu.VMEM((pulses, 2 * pulses), jnp.bfloat16),
            pltpu.VMEM(echoes.shape, jnp.bfloat16),
            pltpu.VMEM(shape, jnp.bfloat16),
            pltpu.SemaphoreType.DMA(()),
            pltpu.SemaphoreType.DMA((steps,)),
            pltpu.SemaphoreType.DMA((steps,)),
        ],
        compiler_params=pltpu.CompilerParams(vmem_limit_bytes=SPECTRA_VMEM),
        name="spectra",
    )(half.reshape(1).astype(jnp.int32), jnp.asarray(table), echoes)


def spread_body(weight_ref, out_ref, *, bins):
    beams = weight_ref.shape[1]
    elements = weight_ref.shape[2]
    group = 128
    width = group * 2 * bins
    lane = lax.broadcasted_iota(jnp.int32, (group, width), 1)
    row = lax.broadcasted_iota(jnp.int32, (group, width), 0)
    repeat = jnp.where(lane // (2 * bins) == row, 1.0, 0.0).astype(jnp.bfloat16)
    col = lax.broadcasted_iota(jnp.int32, (beams, width), 1)
    is_real = (col // bins) % 2 == 0
    for at in range(elements // group):
        span = slice(at * group, (at + 1) * group)
        here = slice(at * width, (at + 1) * width)
        real = jnp.dot(weight_ref[0, :, span], repeat, preferred_element_type=jnp.float32)
        imag = jnp.dot(weight_ref[1, :, span], repeat, preferred_element_type=jnp.float32)
        out_ref[:beams, here] = jnp.where(is_real, real, -imag).astype(jnp.bfloat16)
        out_ref[beams:, here] = jnp.where(is_real, imag, real).astype(jnp.bfloat16)


def spread(beam_weights, bins):
    _, beams, elements = beam_weights.shape
    return pl.pallas_call(
        functools.partial(spread_body, bins=bins),
        in_specs=whole_vmem(1),
        out_specs=whole_vmem(1)[0],
        out_shape=jax.ShapeDtypeStruct((2 * beams, elements * 2 * bins), jnp.bfloat16),
        compiler_params=pltpu.CompilerParams(vmem_limit_bytes=SMALL_VMEM),
        name="spread",
    )(beam_weights)


def partial_body(spectra_ref, spread_ref, out_ref, *, bins):
    elems, ranges = spectra_ref.shape[:2]
    rows = spectra_ref.shape[2] * spectra_ref.shape[3]
    received = jnp.concatenate(
        [
            jnp.concatenate(
                [spectra_ref[n, j].reshape(rows, spectra_ref.shape[4]) for n in range(elems)], axis=0
            )
            for j in range(ranges)
        ],
        axis=1,
    )
    weights = spread_ref[...]
    own = lax.broadcasted_iota(jnp.int32, weights.shape, 1) % bins
    for d in range(bins):
        here = jnp.where(own == d, weights, jnp.zeros_like(weights))
        out_ref[d] = jnp.dot(here, received, preferred_element_type=jnp.float32).astype(out_ref.dtype)


def partial_sums(bound, spread_weights, bins, dtype):
    shape = (bins, spread_weights.shape[0], bound.shape[1] * bound.shape[4])
    return pl.pallas_call(
        functools.partial(partial_body, bins=bins),
        in_specs=whole_vmem(2),
        out_specs=whole_vmem(1)[0],
        out_shape=jax.ShapeDtypeStruct(shape, dtype),
        compiler_params=pltpu.CompilerParams(vmem_limit_bytes=BEAMS_VMEM),
        name="partial_sums",
    )(bound, spread_weights)


def split(value):
    high = value.astype(jnp.bfloat16)
    return high, (value - high.astype(jnp.float32)).astype(jnp.bfloat16)


NT = (((1,), (1,)), ((), ()))


def c_mul(a, b):
    return a[0] * b[0] - a[1] * b[1], a[0] * b[1] + a[1] * b[0]
def c_mulc(a, b):
    return a[0] * b[0] + a[1] * b[1], a[1] * b[0] - a[0] * b[1]
def conj(a): return a[0], -a[1]
def c_add(a, b): return a[0] + b[0], a[1] + b[1]
def c_sub(a, b): return a[0] - b[0], a[1] - b[1]
def scale(a, r): return a[0] * r, a[1] * r

def inverse_pair(m):
    a, b, d = m
    r = 1.0 / (a * d - (b[0] * b[0] + b[1] * b[1]))
    return d * r, (-b[0] * r, -b[1] * r), a * r

def inverse_four(e):
    ea, eb, ed = inverse_pair((e[0][0][0], e[0][1], e[1][1][0]))
    f = [[e[0][2], e[0][3]], [e[1][2], e[1][3]]]
    t = [[None, None], [None, None]]
    for l in range(2):
        t[0][l] = c_add(scale(f[0][l], ea), c_mul(eb, f[1][l]))
        t[1][l] = c_add(c_mulc(f[0][l], eb), scale(f[1][l], ed))
    def herm(l, m):
        return c_add(c_mulc(t[0][m], f[0][l]), c_mulc(t[1][m], f[1][l]))
    def herm_re(l):
        return (t[0][l][0]*f[0][l][0] + t[0][l][1]*f[0][l][1]) + (t[1][l][0]*f[1][l][0] + t[1][l][1]*f[1][l][1])
    s = (e[2][2][0] - herm_re(0), c_sub(e[2][3], herm(0, 1)), e[3][3][0] - herm_re(1))
    sa, sb, sd = inverse_pair(s)
    u = [[None, None], [None, None]]
    for j in range(2):
        x = c_add(scale(t[j][0], sa), c_mulc(t[j][1], sb))
        y = c_add(c_mul(t[j][0], sb), scale(t[j][1], sd))
        u[j][0] = (-x[0], -x[1]); u[j][1] = (-y[0], -y[1])
    def corr(j, m):
        return c_add(c_mulc(u[j][0], t[m][0]), c_mulc(u[j][1], t[m][1]))
    zero = jnp.zeros_like(ea)
    p00 = ea - corr(0, 0)[0]; p11 = ed - corr(1, 1)[0]
    p01 = c_sub(eb, corr(0, 1))
    inv = [[None]*4 for _ in range(4)]
    inv[0][0] = (p00, None); inv[1][1] = (p11, None); inv[0][1] = p01
    inv[2][2] = (sa, None); inv[3][3] = (sd, None); inv[2][3] = sb
    for j in range(2):
        for l in range(2): inv[j][2+l] = u[j][l]
    for j in range(4):
        for l in range(j): inv[j][l] = conj(inv[l][j])
    return inv


def eliminate(rows, beams, lookahead=True):
    shape = rows[0].shape
    lane = lax.broadcasted_iota(jnp.int32, shape, 1)
    upper = lax.broadcasted_iota(jnp.int32, shape, 0) < 4
    sign = jnp.where(lane < beams, -1.0, 1.0)
    def turn(x): return pltpu.roll(x, beams, 1) * sign
    def col(x, k): return jnp.broadcast_to(x[:, k:k+1], shape)
    rows = list(rows)
    for k in range(0, beams, 4):
        inside = ((lane >= k) & (lane < k + 4)) | ((lane >= beams + k) & (lane < beams + k + 4))
        r = []
        for q in (k // 2, k // 2 + 1):
            x = rows[q]
            y = pltpu.roll(x, 4, 0)
            r += [jnp.where(upper, x, y), jnp.where(upper, y, x)]
        e = [[None]*4 for _ in range(4)]
        for j in range(4):
            for l in range(j, 4):
                e[j][l] = (col(r[j], k+l), col(r[j], beams+k+l) if l > j else None)
        inv = inverse_four(e)
        unit = [jnp.where(lane == k+l, 1.0, jnp.where(inside, 0.0, r[l])) for l in range(4)]
        turned = [turn(x) for x in unit]
        b, bt = [], []
        for j in range(4):
            acc, tacc = unit[j] * inv[j][j][0], turned[j] * inv[j][j][0]
            for l in range(4):
                if l != j:
                    acc = acc + (unit[l] * inv[j][l][0] + turned[l] * inv[j][l][1])
                    tacc = tacc + (turned[l] * inv[j][l][0] - unit[l] * inv[j][l][1])
            b.append(acc)
            bt.append(tacc)
        for i in range(k//2+2, beams//2+1):
            x = rows[i]
            acc = jnp.where(inside, 0.0, x)
            for l in range(4):
                acc = acc - (col(x, k+l) * b[l] + col(x, beams+k+l) * bt[l])
            rows[i] = acc
    return rows[beams//2]


def beams_body(side_ref, near_ref, far_ref, pulse_ref, steer_ref, own_ref, send_ref, rows_ref):
    bins, total, gates = near_ref.shape
    beams = total // 2
    ranges = gates // own_ref.shape[2]
    sums = [near_ref[d] + far_ref[d].astype(jnp.float32) for d in range(bins)]
    wide = jnp.concatenate(
        [jnp.concatenate([value[:beams], value[beams:]], axis=1) for value in sums], axis=0
    )
    high, low = split(wide)
    pulse = pulse_ref[...]
    formed = jnp.dot(high, pulse, preferred_element_type=jnp.float32) + jnp.dot(
        low, pulse, preferred_element_type=jnp.float32
    )
    sub = lax.broadcasted_iota(jnp.int32, (beams, 2 * beams), 0)
    lane = lax.broadcasted_iota(jnp.int32, (beams, 2 * beams), 1)
    both = []
    for d in range(bins):
        real = formed[d * beams : (d + 1) * beams, :gates]
        imag = formed[d * beams : (d + 1) * beams, gates:]
        top = jnp.concatenate([real, imag], axis=1)
        whole = jnp.concatenate([top, jnp.concatenate([-imag, real], axis=1)], axis=0)
        g_high, g_low = split(whole)
        both.append((g_high, g_low))
        cov = lax.dot_general(g_high[:beams], g_high, NT, preferred_element_type=jnp.float32)
        cov = cov + lax.dot_general(g_high[:beams], g_low, NT, preferred_element_type=jnp.float32)
        cov = cov + lax.dot_general(g_low[:beams], g_high, NT, preferred_element_type=jnp.float32)
        cov = cov * (1.0 / gates)
        on_diagonal = sub == lane
        trace = jnp.sum(jnp.where(on_diagonal, cov, 0.0), axis=(0, 1), keepdims=True)
        loading = load_ratio * trace / beams + epsilon
        cov = jnp.where(on_diagonal, cov + loading, cov)
        rows_ref[pl.ds(d, beams, stride=bins), :] = cov
    steer = steer_ref[...]
    rows = [rows_ref[8 * q : 8 * q + 8] for q in range(beams // 2)]
    rows.append(jnp.concatenate([steer, steer], axis=0))
    conj = -eliminate(rows, beams)[:bins]
    response = jnp.sum(conj * steer, axis=1, keepdims=True)
    weight = conj / response
    w_high, w_low = split(weight)
    first_side = side_ref[0] == 0
    half = gates // ranges
    row = lax.broadcasted_iota(jnp.int32, (bins, half), 0)
    outs = [jnp.zeros((bins, half), jnp.float32)] * (2 * ranges)
    for d in range(bins):
        g_high, g_low = both[d]
        out = jnp.dot(w_high, g_high, preferred_element_type=jnp.float32)
        out = out + jnp.dot(w_high, g_low, preferred_element_type=jnp.float32)
        out = out + jnp.dot(w_low, g_high, preferred_element_type=jnp.float32)
        outs = [
            jnp.where(row == d, out[:, n * half : (n + 1) * half], kept) for n, kept in enumerate(outs)
        ]
    nothing = jnp.zeros((bins, half), jnp.float32)
    for part in range(2):
        first, second = outs[2 * part : 2 * part + 2]
        own_ref[part] = jnp.concatenate(
            [jnp.where(first_side, first, nothing), jnp.where(first_side, nothing, second)], axis=0
        )
        send_ref[part] = jnp.concatenate(
            [jnp.where(first_side, second, nothing), jnp.where(first_side, nothing, first)], axis=0
        )


def on_device_owned(echoes, replica, beam_weights, steering):
    elems, ranges = lax.axis_size("elem"), lax.axis_size("range")
    devices = elems * ranges
    _, own_elements, pulses, gate_count = echoes.shape
    bins = pulses // devices
    elements = beam_weights.shape[2]
    gates = gate_count * ranges
    side = lax.axis_index("range")
    half = lax.axis_index("elem") // (elems // 2)
    group = devices // 2
    groups = [list(range(group)), list(range(group, devices))]

    def gathered(owner_half):
        sent = spectra(owner_half, echoes, devices)
        bound = lax.all_to_all(sent, ("elem", "range"), 0, 0, tiled=True, axis_index_groups=groups)
        return bound.reshape(elems // 2, ranges, own_elements // 2, 4 * bins, gate_count)

    here = lax.dynamic_slice_in_dim(beam_weights, half * (elements // 2), elements // 2, 2)
    spread_weights = spread(here, bins)
    crossing = partial_sums(gathered(1 - half), spread_weights, bins, jnp.bfloat16)
    far = lax.ppermute(crossing, "elem", [(n, (n + elems // 2) % elems) for n in range(elems)])
    near = partial_sums(gathered(half), spread_weights, bins, jnp.float32)
    pulse = pulse_kernel(replica, gates)[:, :, :gates]
    pulse = pulse.transpose(0, 2, 1, 3).reshape(2 * gates, 2 * gates)
    own_steering = lax.dynamic_slice_in_dim(steering, side * bins, bins, 1)
    steer_row = jnp.concatenate([own_steering[0], -own_steering[1]], axis=1)
    shape = jax.ShapeDtypeStruct((2, 2 * bins, gate_count), jnp.float32)
    own, send = pl.pallas_call(
        beams_body,
        in_specs=[pl.BlockSpec(memory_space=pltpu.SMEM)] + whole_vmem(4),
        out_specs=whole_vmem(2),
        out_shape=[shape, shape],
        scratch_shapes=[pltpu.VMEM((bins * beam_weights.shape[1], 2 * beam_weights.shape[1]), jnp.float32)],
        compiler_params=pltpu.CompilerParams(vmem_limit_bytes=BEAMS_VMEM),
        name="beams",
    )(side.reshape(1).astype(jnp.int32), near, far, pulse, steer_row)
    return own + lax.ppermute(send, "range", [(0, 1), (1, 0)])


def on_device(echoes, replica, beam_weights, steering):
    elems, ranges = lax.axis_size("elem"), lax.axis_size("range")
    pulses, gate_count = echoes.shape[2:]
    beams, elements = beam_weights.shape[1:]
    owned = (
        ranges == 2
        and pulses == 4 * elems * ranges
        and gate_count % 128 == 0
        and beams == 64
        and elems % 2 == 0
        and elements % 256 == 0
        and echoes.shape[1] % 8 == 0
        and replica.shape[1] <= gate_count
    )
    run = on_device_owned if owned else on_device_general
    return run(echoes, replica, beam_weights, steering)


def solution(mesh):
    return jax.shard_map(
        on_device,
        mesh=mesh,
        in_specs=(P(None, "elem", None, "range"), P(), P(), P(None, "elem", None)),
        out_specs=P(None, "elem", "range"),
        check_vma=False,
    )
```

```python
import functools

import jax
import jax.numpy as jnp
import numpy as np
from jax import lax
from jax.experimental import pallas as pl
from jax.experimental.pallas import tpu as pltpu
from jax.sharding import PartitionSpec as P

load_ratio = 0.1
epsilon = 1e-06
SPECTRA_VMEM = 56 << 20
STEPS = 2
BLOCK = 16
SMALL_VMEM = 14 << 20
BEAMS_VMEM = 24 << 20


def shifted(value, axis, steps):
    count = lax.axis_size(axis)
    first, last = (max(0, -steps), min(count, count - steps))
    return lax.ppermute(value, axis, [(source, source + steps) for source in range(first, last)])


def correlation_matrix(tap_values, gate_count):
    tap_count = tap_values.shape[0]
    span_width = gate_count + tap_count - 1
    padded_taps = jnp.concatenate(
        [tap_values, jnp.zeros((span_width + 1 - tap_count,), tap_values.dtype)]
    )
    tiled_rows = jnp.tile(padded_taps, gate_count)[: gate_count * span_width].reshape(
        gate_count, span_width
    )
    return tiled_rows.T


def pulse_kernel(replica, gate_count):
    real_part = correlation_matrix(replica[0], gate_count)
    imag_part = correlation_matrix(replica[1], gate_count)
    return jnp.stack([jnp.stack([real_part, imag_part]), jnp.stack([-imag_part, real_part])])


def doppler_table(pulses):
    index = np.arange(pulses, dtype=np.int64)
    phase_index = (index[:, None] * index[None, :]) % pulses
    phase_angle = np.float32(2.0 * np.pi) * phase_index.astype(np.float32) / np.float32(pulses)
    scale = np.float32(1.0) / np.sqrt(np.float32(pulses))
    cosine = np.cos(phase_angle) * scale
    sine = np.sin(phase_angle) * scale
    table = np.stack([np.stack([cosine, -sine]), np.stack([sine, cosine])])
    return table.astype(jnp.bfloat16)


def beam_kernel(beam_weights):
    weight_re = beam_weights[0]
    weight_im = beam_weights[1]
    return jnp.stack([jnp.stack([weight_re, weight_im]), jnp.stack([-weight_im, weight_re])])


def adapt(gram_sum, steering, formed):
    beams = formed.shape[2]
    cov_re = gram_sum[:, :beams, :beams] + gram_sum[:, beams:, beams:]
    cov_im = gram_sum[:, beams:, :beams] - gram_sum[:, :beams, beams:]
    loading = load_ratio * jnp.trace(cov_re, axis1=1, axis2=2) / beams + epsilon
    upper = jnp.concatenate([cov_re, -cov_im], axis=2)
    lower = jnp.concatenate([cov_im, cov_re], axis=2)
    system = jnp.concatenate([upper, lower], axis=1)
    system = system + loading[:, None, None] * jnp.eye(2 * beams, dtype=jnp.float32)[None]
    factor = jnp.linalg.cholesky(system)
    right_side = jnp.concatenate([steering[0], steering[1]], axis=-1)
    solved = jax.scipy.linalg.cho_solve((factor, True), right_side[..., None])[..., 0]
    response = jnp.sum(right_side * solved, axis=-1)
    weights = solved / response[:, None]
    weight_re = weights[:, :beams]
    weight_im = weights[:, beams:]
    beam_re = formed[:, 0].astype(jnp.float32)
    beam_im = formed[:, 1].astype(jnp.float32)
    high = lax.Precision.HIGHEST
    out_re = jnp.einsum("db,dbr->dr", weight_re, beam_re, precision=high) + jnp.einsum(
        "db,dbr->dr", weight_im, beam_im, precision=high
    )
    out_im = jnp.einsum("db,dbr->dr", weight_re, beam_im, precision=high) - jnp.einsum(
        "db,dbr->dr", weight_im, beam_re, precision=high
    )
    return jnp.stack([out_re, out_im])


def on_device_general(echoes, replica, beam_weights, steering):
    pulses = echoes.shape[2]
    gate_count = echoes.shape[3]
    tap_count = replica.shape[1]
    following = shifted(echoes[:, :, :, : tap_count - 1], "range", -1)
    padded = jnp.concatenate([echoes, following], axis=3)
    compressed = jnp.einsum(
        "cepj,cojr->oepr",
        padded,
        pulse_kernel(replica, gate_count),
        preferred_element_type=jnp.float32,
    ).astype(jnp.bfloat16)
    doppler = jnp.einsum(
        "cepr,codp->oedr",
        compressed,
        jnp.asarray(doppler_table(pulses)),
        preferred_element_type=jnp.float32,
    ).astype(jnp.bfloat16)
    kernel_full = beam_kernel(beam_weights)
    own_bins = pulses // lax.axis_size("elem")
    beam_sums = jnp.einsum(
        "cedr,cobe->dobr",
        lax.all_to_all(doppler, "elem", split_axis=2, concat_axis=1, tiled=True),
        kernel_full,
        preferred_element_type=jnp.float32,
    )
    formed = beam_sums.astype(jnp.bfloat16)
    beams = formed.shape[2]
    stacked = formed.reshape(own_bins, 2 * beams, gate_count)
    partial_gram = jnp.einsum("dbr,dcr->dbc", stacked, stacked, preferred_element_type=jnp.float32)
    gram_sum = lax.psum(partial_gram, "range") / (gate_count * lax.axis_size("range"))
    return adapt(gram_sum, steering, formed)


def whole_vmem(count):
    return [pl.BlockSpec(memory_space=pltpu.VMEM)] * count


def spectra_body(half_ref, table_hbm, echo_hbm, out_hbm, table_ref, echo_ref, out_ref, table_sem, in_sem, out_sem):
    members = out_ref.shape[0]
    gates = echo_ref.shape[3]
    steps = in_sem.shape[0]
    block = echo_ref.shape[1] // steps
    pairs = block // 2
    fetch_table = pltpu.make_async_copy(table_hbm.at[half_ref[0]], table_ref, table_sem)
    fetches = [
        pltpu.make_async_copy(
            echo_hbm.at[:, pl.ds(step * block, block)],
            echo_ref.at[:, pl.ds(step * block, block)],
            in_sem.at[step],
        )
        for step in range(steps)
    ]
    stores = [
        pltpu.make_async_copy(
            out_ref.at[:, pl.ds(step * pairs, pairs)],
            out_hbm.at[:, pl.ds(step * pairs, pairs)],
            out_sem.at[step],
        )
        for step in range(steps)
    ]
    fetch_table.start()
    for fetch in fetches:
        fetch.start()
    fetch_table.wait()
    table = table_ref[...]
    for step in range(steps):
        fetches[step].wait()
        for pair in range(step * pairs, (step + 1) * pairs):
            even, odd = 2 * pair, 2 * pair + 1
            samples = jnp.concatenate(
                [
                    jnp.concatenate([echo_ref[0, even], echo_ref[0, odd]], axis=1),
                    jnp.concatenate([echo_ref[1, even], echo_ref[1, odd]], axis=1),
                ],
                axis=0,
            )
            bins = jnp.dot(table, samples, preferred_element_type=jnp.float32)
            bins = bins.reshape(members, bins.shape[0] // members, 2 * gates)
            rows = jnp.concatenate([bins[:, :, :gates], bins[:, :, gates:]], axis=1)
            out_ref[:, pair] = rows.astype(jnp.bfloat16)
        stores[step].start()
    for store in stores:
        store.wait()


def spectra(half, echoes, devices, steps=STEPS):
    _, elements, pulses, gates = echoes.shape
    bins = pulses // devices
    members = devices // 2
    table = doppler_table(pulses)
    table = table.transpose(2, 1, 0, 3).reshape(devices, bins, 2, 2 * pulses)
    table = table.transpose(0, 2, 1, 3).reshape(2, pulses, 2 * pulses)
    shape = (members, elements // 2, 4 * bins, gates)
    return pl.pallas_call(
        spectra_body,
        in_specs=[pl.BlockSpec(memory_space=pltpu.SMEM)] + [pl.BlockSpec(memory_space=pl.ANY)] * 2,
        out_specs=pl.BlockSpec(memory_space=pl.ANY),
        out_shape=jax.ShapeDtypeStruct(shape, jnp.bfloat16),
        scratch_shapes=[
            pltpu.VMEM((pulses, 2 * pulses), jnp.bfloat16),
            pltpu.VMEM(echoes.shape, jnp.bfloat16),
            pltpu.VMEM(shape, jnp.bfloat16),
            pltpu.SemaphoreType.DMA(()),
            pltpu.SemaphoreType.DMA((steps,)),
            pltpu.SemaphoreType.DMA((steps,)),
        ],
        compiler_params=pltpu.CompilerParams(vmem_limit_bytes=SPECTRA_VMEM),
        name="spectra",
    )(half.reshape(1).astype(jnp.int32), jnp.asarray(table), echoes)


def spread_body(weight_ref, out_ref, *, bins):
    beams = weight_ref.shape[1]
    elements = weight_ref.shape[2]
    group = 128
    width = group * 2 * bins
    lane = lax.broadcasted_iota(jnp.int32, (group, width), 1)
    row = lax.broadcasted_iota(jnp.int32, (group, width), 0)
    repeat = jnp.where(lane // (2 * bins) == row, 1.0, 0.0).astype(jnp.bfloat16)
    col = lax.broadcasted_iota(jnp.int32, (beams, width), 1)
    is_real = (col // bins) % 2 == 0
    for at in range(elements // group):
        span = slice(at * group, (at + 1) * group)
        here = slice(at * width, (at + 1) * width)
        real = jnp.dot(weight_ref[0, :, span], repeat, preferred_element_type=jnp.float32)
        imag = jnp.dot(weight_ref[1, :, span], repeat, preferred_element_type=jnp.float32)
        out_ref[:beams, here] = jnp.where(is_real, real, -imag).astype(jnp.bfloat16)
        out_ref[beams:, here] = jnp.where(is_real, imag, real).astype(jnp.bfloat16)


def spread(beam_weights, bins):
    _, beams, elements = beam_weights.shape
    return pl.pallas_call(
        functools.partial(spread_body, bins=bins),
        in_specs=whole_vmem(1),
        out_specs=whole_vmem(1)[0],
        out_shape=jax.ShapeDtypeStruct((2 * beams, elements * 2 * bins), jnp.bfloat16),
        compiler_params=pltpu.CompilerParams(vmem_limit_bytes=SMALL_VMEM),
        name="spread",
    )(beam_weights)


def beam_sums(spectra_ref, spread_ref, bins):
    elems, ranges = spectra_ref.shape[:2]
    rows = spectra_ref.shape[2] * spectra_ref.shape[3]
    received = jnp.concatenate(
        [
            jnp.concatenate(
                [spectra_ref[n, j].reshape(rows, spectra_ref.shape[4]) for n in range(elems)], axis=0
            )
            for j in range(ranges)
        ],
        axis=1,
    )
    weights = spread_ref[...]
    own = lax.broadcasted_iota(jnp.int32, weights.shape, 1) % bins
    return [
        jnp.dot(
            jnp.where(own == d, weights, jnp.zeros_like(weights)),
            received,
            preferred_element_type=jnp.float32,
        )
        for d in range(bins)
    ]


def partial_body(spectra_ref, spread_ref, out_ref):
    for d, value in enumerate(beam_sums(spectra_ref, spread_ref, out_ref.shape[0])):
        out_ref[d] = value.astype(out_ref.dtype)


def partial_sums(bound, spread_weights, bins, dtype):
    shape = (bins, spread_weights.shape[0], bound.shape[1] * bound.shape[4])
    return pl.pallas_call(
        partial_body,
        in_specs=whole_vmem(2),
        out_specs=whole_vmem(1)[0],
        out_shape=jax.ShapeDtypeStruct(shape, dtype),
        compiler_params=pltpu.CompilerParams(vmem_limit_bytes=BEAMS_VMEM),
        name="partial_sums",
    )(bound, spread_weights)


def split(value):
    high = value.astype(jnp.bfloat16)
    return high, (value - high.astype(jnp.float32)).astype(jnp.bfloat16)


NT = (((1,), (1,)), ((), ()))


def c_mul(a, b):
    return a[0] * b[0] - a[1] * b[1], a[0] * b[1] + a[1] * b[0]
def c_mulc(a, b):
    return a[0] * b[0] + a[1] * b[1], a[1] * b[0] - a[0] * b[1]
def conj(a): return a[0], -a[1]
def c_add(a, b): return a[0] + b[0], a[1] + b[1]
def c_sub(a, b): return a[0] - b[0], a[1] - b[1]
def scale(a, r): return a[0] * r, a[1] * r

def inverse_pair(m):
    a, b, d = m
    r = 1.0 / (a * d - (b[0] * b[0] + b[1] * b[1]))
    return d * r, (-b[0] * r, -b[1] * r), a * r

def inverse_four(e):
    ea, eb, ed = inverse_pair((e[0][0][0], e[0][1], e[1][1][0]))
    f = [[e[0][2], e[0][3]], [e[1][2], e[1][3]]]
    t = [[None, None], [None, None]]
    for l in range(2):
        t[0][l] = c_add(scale(f[0][l], ea), c_mul(eb, f[1][l]))
        t[1][l] = c_add(c_mulc(f[0][l], eb), scale(f[1][l], ed))
    def herm(l, m):
        return c_add(c_mulc(t[0][m], f[0][l]), c_mulc(t[1][m], f[1][l]))
    def herm_re(l):
        return (t[0][l][0]*f[0][l][0] + t[0][l][1]*f[0][l][1]) + (t[1][l][0]*f[1][l][0] + t[1][l][1]*f[1][l][1])
    s = (e[2][2][0] - herm_re(0), c_sub(e[2][3], herm(0, 1)), e[3][3][0] - herm_re(1))
    sa, sb, sd = inverse_pair(s)
    u = [[None, None], [None, None]]
    for j in range(2):
        x = c_add(scale(t[j][0], sa), c_mulc(t[j][1], sb))
        y = c_add(c_mul(t[j][0], sb), scale(t[j][1], sd))
        u[j][0] = (-x[0], -x[1]); u[j][1] = (-y[0], -y[1])
    def corr(j, m):
        return c_add(c_mulc(u[j][0], t[m][0]), c_mulc(u[j][1], t[m][1]))
    zero = jnp.zeros_like(ea)
    p00 = ea - corr(0, 0)[0]; p11 = ed - corr(1, 1)[0]
    p01 = c_sub(eb, corr(0, 1))
    inv = [[None]*4 for _ in range(4)]
    inv[0][0] = (p00, None); inv[1][1] = (p11, None); inv[0][1] = p01
    inv[2][2] = (sa, None); inv[3][3] = (sd, None); inv[2][3] = sb
    for j in range(2):
        for l in range(2): inv[j][2+l] = u[j][l]
    for j in range(4):
        for l in range(j): inv[j][l] = conj(inv[l][j])
    return inv


def turn(x):
    half = x.shape[1] // 2
    lane = lax.broadcasted_iota(jnp.int32, x.shape, 1)
    y = pltpu.roll(x, half, 1)
    return jnp.where(lane < half, -y, y)


def sweep(rows, columns, updated):
    shape = rows[0].shape
    beams = shape[1] // 2
    lane = lax.broadcasted_iota(jnp.int32, shape, 1)
    upper = lax.broadcasted_iota(jnp.int32, shape, 0) < 4

    def col(x, k):
        return jnp.broadcast_to(x[:, k : k + 1], shape)

    for step, k in enumerate(columns):
        inside = ((lane >= k) & (lane < k + 4)) | ((lane >= beams + k) & (lane < beams + k + 4))
        pivot = []
        for q in (2 * step, 2 * step + 1):
            x = rows[q]
            y = pltpu.roll(x, 4, 0)
            pivot += [jnp.where(upper, x, y), jnp.where(upper, y, x)]
        entry = [[None] * 4 for _ in range(4)]
        for j in range(4):
            for l in range(j, 4):
                entry[j][l] = (col(pivot[j], k + l), col(pivot[j], beams + k + l) if l > j else None)
        inv = inverse_four(entry)
        unit = [jnp.where(lane == k + l, 1.0, jnp.where(inside, 0.0, pivot[l])) for l in range(4)]
        turned = [turn(x) for x in unit]
        b, bt = [], []
        for j in range(4):
            acc, tacc = unit[j] * inv[j][j][0], turned[j] * inv[j][j][0]
            for l in range(4):
                if l != j:
                    acc = acc + (unit[l] * inv[j][l][0] + turned[l] * inv[j][l][1])
                    tacc = tacc + (turned[l] * inv[j][l][0] - unit[l] * inv[j][l][1])
            b.append(acc)
            bt.append(tacc)
        for q in updated(step):
            x = rows[q]
            acc = jnp.where(inside, 0.0, x)
            for l in range(4):
                acc = acc - (col(x, k + l) * b[l] + col(x, beams + k + l) * bt[l])
            rows[q] = acc
        for q in (0, 1):
            rows[2 * step + q] = jnp.where(upper, b[2 * q], b[2 * q + 1])
    return rows


def eliminate(systems, sources, rows_ref, size=BLOCK):
    count = len(systems)
    beams = systems[0].shape[0]
    blocks = size // 2
    rest = [
        jnp.concatenate([systems[n], jnp.broadcast_to(sources[n], (8, 2 * beams))], axis=0) for n in range(count)
    ]
    for first in range(0, beams, size):
        base = count * first
        for n in range(count):
            rows_ref[pl.ds(base + n, size, stride=count), :] = rest[n][:size]
        rows = [rows_ref[base + 8 * q : base + 8 * q + 8] for q in range(blocks)]
        columns = range(first, first + size, 4)
        if first + size == beams:
            bottoms = [value[size : size + 1] for value in rest]
            rows.append(jnp.concatenate(bottoms + bottoms, axis=0))
            return sweep(rows, columns, lambda step: range(2 * step + 2, blocks + 1))[blocks]
        rows = sweep(rows, columns, lambda step: [q for q in range(blocks) if q // 2 != step])
        for q in range(blocks):
            rows_ref[base + 8 * q : base + 8 * q + 8] = rows[q]
        for n in range(count):
            top = rows_ref[pl.ds(base + n, size, stride=count), :]
            before = [jnp.zeros((first, 2 * beams), jnp.float32)] * (first > 0)
            after = [jnp.zeros((beams - first - size, 2 * beams), jnp.float32)]
            high, low = split(jnp.concatenate(before + [top] + after + before + [turn(top)] + after, axis=0))
            value = rest[n][size:]
            v_high, v_low = split(value)
            taken = jnp.dot(v_high, high, preferred_element_type=jnp.float32)
            taken = taken + jnp.dot(v_high, low, preferred_element_type=jnp.float32)
            taken = taken + jnp.dot(v_low, high, preferred_element_type=jnp.float32)
            at = lax.broadcasted_iota(jnp.int32, value.shape, 1) % beams
            rest[n] = jnp.where((at >= first) & (at < first + size), 0.0, value) - taken


def beams_body(
    side_ref, spectra_ref, spread_ref, far_ref, pulse_ref, steer_ref, own_ref, send_ref, rows_ref
):
    bins, total, gates = far_ref.shape
    beams = total // 2
    ranges = gates // own_ref.shape[2]
    near = beam_sums(spectra_ref, spread_ref, bins)
    sums = [near[d] + far_ref[d].astype(jnp.float32) for d in range(bins)]
    wide = jnp.concatenate(
        [jnp.concatenate([value[:beams], value[beams:]], axis=1) for value in sums], axis=0
    )
    high, low = split(wide)
    pulse = pulse_ref[...]
    formed = jnp.dot(high, pulse, preferred_element_type=jnp.float32) + jnp.dot(
        low, pulse, preferred_element_type=jnp.float32
    )
    sub = lax.broadcasted_iota(jnp.int32, (beams, 2 * beams), 0)
    lane = lax.broadcasted_iota(jnp.int32, (beams, 2 * beams), 1)
    both, systems = [], []
    for d in range(bins):
        real = formed[d * beams : (d + 1) * beams, :gates]
        imag = formed[d * beams : (d + 1) * beams, gates:]
        top = jnp.concatenate([real, imag], axis=1)
        whole = jnp.concatenate([top, jnp.concatenate([-imag, real], axis=1)], axis=0)
        g_high, g_low = split(whole)
        both.append((g_high, g_low))
        cov = lax.dot_general(g_high[:beams], g_high, NT, preferred_element_type=jnp.float32)
        cov = cov + lax.dot_general(g_high[:beams], g_low, NT, preferred_element_type=jnp.float32)
        cov = cov + lax.dot_general(g_low[:beams], g_high, NT, preferred_element_type=jnp.float32)
        cov = cov * (1.0 / gates)
        on_diagonal = sub == lane
        trace = jnp.sum(jnp.where(on_diagonal, cov, 0.0), axis=(0, 1), keepdims=True)
        loading = load_ratio * trace / beams + epsilon
        cov = jnp.where(on_diagonal, cov + loading, cov)
        systems.append(cov)
    steer = steer_ref[...]
    sources = [steer[d : d + 1] for d in range(bins)]
    conj = -eliminate(systems, sources, rows_ref)[:bins]
    response = jnp.sum(conj * steer, axis=1, keepdims=True)
    weight = conj / response
    w_high, w_low = split(weight)
    first_side = side_ref[0] == 0
    half = gates // ranges
    row = lax.broadcasted_iota(jnp.int32, (bins, half), 0)
    outs = [jnp.zeros((bins, half), jnp.float32)] * (2 * ranges)
    for d in range(bins):
        g_high, g_low = both[d]
        out = jnp.dot(w_high, g_high, preferred_element_type=jnp.float32)
        out = out + jnp.dot(w_high, g_low, preferred_element_type=jnp.float32)
        out = out + jnp.dot(w_low, g_high, preferred_element_type=jnp.float32)
        outs = [
            jnp.where(row == d, out[:, n * half : (n + 1) * half], kept) for n, kept in enumerate(outs)
        ]
    nothing = jnp.zeros((bins, half), jnp.float32)
    for part in range(2):
        first, second = outs[2 * part : 2 * part + 2]
        own_ref[part] = jnp.concatenate(
            [jnp.where(first_side, first, nothing), jnp.where(first_side, nothing, second)], axis=0
        )
        send_ref[part] = jnp.concatenate(
            [jnp.where(first_side, second, nothing), jnp.where(first_side, nothing, first)], axis=0
        )


def on_device_owned(echoes, replica, beam_weights, steering):
    elems, ranges = lax.axis_size("elem"), lax.axis_size("range")
    devices = elems * ranges
    _, own_elements, pulses, gate_count = echoes.shape
    bins = pulses // devices
    elements = beam_weights.shape[2]
    gates = gate_count * ranges
    side = lax.axis_index("range")
    half = lax.axis_index("elem") // (elems // 2)
    group = devices // 2
    groups = [list(range(group)), list(range(group, devices))]

    def gathered(owner_half):
        sent = spectra(owner_half, echoes, devices)
        bound = lax.all_to_all(sent, ("elem", "range"), 0, 0, tiled=True, axis_index_groups=groups)
        return bound.reshape(elems // 2, ranges, own_elements // 2, 4 * bins, gate_count)

    here = lax.dynamic_slice_in_dim(beam_weights, half * (elements // 2), elements // 2, 2)
    spread_weights = spread(here, bins)
    crossing = partial_sums(gathered(1 - half), spread_weights, bins, jnp.bfloat16)
    far = lax.ppermute(crossing, "elem", [(n, (n + elems // 2) % elems) for n in range(elems)])
    near = gathered(half)
    pulse = pulse_kernel(replica, gates)[:, :, :gates]
    pulse = pulse.transpose(0, 2, 1, 3).reshape(2 * gates, 2 * gates)
    own_steering = lax.dynamic_slice_in_dim(steering, side * bins, bins, 1)
    steer_row = jnp.concatenate([own_steering[0], -own_steering[1]], axis=1)
    shape = jax.ShapeDtypeStruct((2, 2 * bins, gate_count), jnp.float32)
    own, send = pl.pallas_call(
        beams_body,
        in_specs=[pl.BlockSpec(memory_space=pltpu.SMEM)] + whole_vmem(5),
        out_specs=whole_vmem(2),
        out_shape=[shape, shape],
        scratch_shapes=[pltpu.VMEM((bins * beam_weights.shape[1], 2 * beam_weights.shape[1]), jnp.float32)],
        compiler_params=pltpu.CompilerParams(vmem_limit_bytes=BEAMS_VMEM),
        name="beams",
    )(side.reshape(1).astype(jnp.int32), near, spread_weights, far, pulse, steer_row)
    return own + lax.ppermute(send, "range", [(0, 1), (1, 0)])


def on_device(echoes, replica, beam_weights, steering):
    elems, ranges = lax.axis_size("elem"), lax.axis_size("range")
    pulses, gate_count = echoes.shape[2:]
    beams, elements = beam_weights.shape[1:]
    owned = (
        ranges == 2
        and pulses == 4 * elems * ranges
        and gate_count % 128 == 0
        and beams == 64
        and elems % 2 == 0
        and elements % 256 == 0
        and echoes.shape[1] % 8 == 0
        and replica.shape[1] <= gate_count
    )
    run = on_device_owned if owned else on_device_general
    return run(echoes, replica, beam_weights, steering)


def solution(mesh):
    return jax.shard_map(
        on_device,
        mesh=mesh,
        in_specs=(P(None, "elem", None, "range"), P(), P(), P(None, "elem", None)),
        out_specs=P(None, "elem", "range"),
        check_vma=False,
    )
```

```python
import functools

import jax
import jax.numpy as jnp
import numpy as np
from jax import lax
from jax.experimental import pallas as pl
from jax.experimental.pallas import tpu as pltpu
from jax.sharding import PartitionSpec as P

load_ratio = 0.1
epsilon = 1e-06
SPECTRA_VMEM = 56 << 20
STEPS = 2
BLOCK = 16
SMALL_VMEM = 14 << 20
BEAMS_VMEM = 24 << 20


def shifted(value, axis, steps):
    count = lax.axis_size(axis)
    first, last = (max(0, -steps), min(count, count - steps))
    return lax.ppermute(value, axis, [(source, source + steps) for source in range(first, last)])


def correlation_matrix(tap_values, gate_count):
    tap_count = tap_values.shape[0]
    span_width = gate_count + tap_count - 1
    padded_taps = jnp.concatenate(
        [tap_values, jnp.zeros((span_width + 1 - tap_count,), tap_values.dtype)]
    )
    tiled_rows = jnp.tile(padded_taps, gate_count)[: gate_count * span_width].reshape(
        gate_count, span_width
    )
    return tiled_rows.T


def pulse_kernel(replica, gate_count):
    real_part = correlation_matrix(replica[0], gate_count)
    imag_part = correlation_matrix(replica[1], gate_count)
    return jnp.stack([jnp.stack([real_part, imag_part]), jnp.stack([-imag_part, real_part])])


def doppler_table(pulses):
    index = np.arange(pulses, dtype=np.int64)
    phase_index = (index[:, None] * index[None, :]) % pulses
    phase_angle = np.float32(2.0 * np.pi) * phase_index.astype(np.float32) / np.float32(pulses)
    scale = np.float32(1.0) / np.sqrt(np.float32(pulses))
    cosine = np.cos(phase_angle) * scale
    sine = np.sin(phase_angle) * scale
    table = np.stack([np.stack([cosine, -sine]), np.stack([sine, cosine])])
    return table.astype(jnp.bfloat16)


def beam_kernel(beam_weights):
    weight_re = beam_weights[0]
    weight_im = beam_weights[1]
    return jnp.stack([jnp.stack([weight_re, weight_im]), jnp.stack([-weight_im, weight_re])])


def adapt(gram_sum, steering, formed):
    beams = formed.shape[2]
    cov_re = gram_sum[:, :beams, :beams] + gram_sum[:, beams:, beams:]
    cov_im = gram_sum[:, beams:, :beams] - gram_sum[:, :beams, beams:]
    loading = load_ratio * jnp.trace(cov_re, axis1=1, axis2=2) / beams + epsilon
    upper = jnp.concatenate([cov_re, -cov_im], axis=2)
    lower = jnp.concatenate([cov_im, cov_re], axis=2)
    system = jnp.concatenate([upper, lower], axis=1)
    system = system + loading[:, None, None] * jnp.eye(2 * beams, dtype=jnp.float32)[None]
    factor = jnp.linalg.cholesky(system)
    right_side = jnp.concatenate([steering[0], steering[1]], axis=-1)
    solved = jax.scipy.linalg.cho_solve((factor, True), right_side[..., None])[..., 0]
    response = jnp.sum(right_side * solved, axis=-1)
    weights = solved / response[:, None]
    weight_re = weights[:, :beams]
    weight_im = weights[:, beams:]
    beam_re = formed[:, 0].astype(jnp.float32)
    beam_im = formed[:, 1].astype(jnp.float32)
    high = lax.Precision.HIGHEST
    out_re = jnp.einsum("db,dbr->dr", weight_re, beam_re, precision=high) + jnp.einsum(
        "db,dbr->dr", weight_im, beam_im, precision=high
    )
    out_im = jnp.einsum("db,dbr->dr", weight_re, beam_im, precision=high) - jnp.einsum(
        "db,dbr->dr", weight_im, beam_re, precision=high
    )
    return jnp.stack([out_re, out_im])


def on_device_general(echoes, replica, beam_weights, steering):
    pulses = echoes.shape[2]
    gate_count = echoes.shape[3]
    tap_count = replica.shape[1]
    following = shifted(echoes[:, :, :, : tap_count - 1], "range", -1)
    padded = jnp.concatenate([echoes, following], axis=3)
    compressed = jnp.einsum(
        "cepj,cojr->oepr",
        padded,
        pulse_kernel(replica, gate_count),
        preferred_element_type=jnp.float32,
    ).astype(jnp.bfloat16)
    doppler = jnp.einsum(
        "cepr,codp->oedr",
        compressed,
        jnp.asarray(doppler_table(pulses)),
        preferred_element_type=jnp.float32,
    ).astype(jnp.bfloat16)
    kernel_full = beam_kernel(beam_weights)
    own_bins = pulses // lax.axis_size("elem")
    beam_sums = jnp.einsum(
        "cedr,cobe->dobr",
        lax.all_to_all(doppler, "elem", split_axis=2, concat_axis=1, tiled=True),
        kernel_full,
        preferred_element_type=jnp.float32,
    )
    formed = beam_sums.astype(jnp.bfloat16)
    beams = formed.shape[2]
    stacked = formed.reshape(own_bins, 2 * beams, gate_count)
    partial_gram = jnp.einsum("dbr,dcr->dbc", stacked, stacked, preferred_element_type=jnp.float32)
    gram_sum = lax.psum(partial_gram, "range") / (gate_count * lax.axis_size("range"))
    return adapt(gram_sum, steering, formed)


def whole_vmem(count):
    return [pl.BlockSpec(memory_space=pltpu.VMEM)] * count


def spectra_body(half_ref, table_hbm, echo_hbm, out_hbm, table_ref, echo_ref, out_ref, table_sem, in_sem, out_sem):
    members = out_ref.shape[0]
    gates = echo_ref.shape[3]
    steps = in_sem.shape[0]
    block = echo_ref.shape[1] // steps
    pairs = block // 2
    fetch_table = pltpu.make_async_copy(table_hbm.at[half_ref[0]], table_ref, table_sem)
    fetches = [
        pltpu.make_async_copy(
            echo_hbm.at[:, pl.ds(step * block, block)],
            echo_ref.at[:, pl.ds(step * block, block)],
            in_sem.at[step],
        )
        for step in range(steps)
    ]
    stores = [
        pltpu.make_async_copy(
            out_ref.at[:, pl.ds(step * pairs, pairs)],
            out_hbm.at[:, pl.ds(step * pairs, pairs)],
            out_sem.at[step],
        )
        for step in range(steps)
    ]
    fetch_table.start()
    for fetch in fetches:
        fetch.start()
    fetch_table.wait()
    table = table_ref[...]
    for step in range(steps):
        fetches[step].wait()
        for pair in range(step * pairs, (step + 1) * pairs):
            even, odd = 2 * pair, 2 * pair + 1
            samples = jnp.concatenate(
                [
                    jnp.concatenate([echo_ref[0, even], echo_ref[0, odd]], axis=1),
                    jnp.concatenate([echo_ref[1, even], echo_ref[1, odd]], axis=1),
                ],
                axis=0,
            )
            bins = jnp.dot(table, samples, preferred_element_type=jnp.float32)
            bins = bins.reshape(members, bins.shape[0] // members, 2 * gates)
            rows = jnp.concatenate([bins[:, :, :gates], bins[:, :, gates:]], axis=1)
            out_ref[:, pair] = rows.astype(jnp.bfloat16)
        stores[step].start()
    for store in stores:
        store.wait()


def spectra(half, echoes, devices, steps=STEPS):
    _, elements, pulses, gates = echoes.shape
    bins = pulses // devices
    members = devices // 2
    table = doppler_table(pulses)
    table = table.transpose(2, 1, 0, 3).reshape(devices, bins, 2, 2 * pulses)
    table = table.transpose(0, 2, 1, 3).reshape(2, pulses, 2 * pulses)
    shape = (members, elements // 2, 4 * bins, gates)
    return pl.pallas_call(
        spectra_body,
        in_specs=[pl.BlockSpec(memory_space=pltpu.SMEM)] + [pl.BlockSpec(memory_space=pl.ANY)] * 2,
        out_specs=pl.BlockSpec(memory_space=pl.ANY),
        out_shape=jax.ShapeDtypeStruct(shape, jnp.bfloat16),
        scratch_shapes=[
            pltpu.VMEM((pulses, 2 * pulses), jnp.bfloat16),
            pltpu.VMEM(echoes.shape, jnp.bfloat16),
            pltpu.VMEM(shape, jnp.bfloat16),
            pltpu.SemaphoreType.DMA(()),
            pltpu.SemaphoreType.DMA((steps,)),
            pltpu.SemaphoreType.DMA((steps,)),
        ],
        compiler_params=pltpu.CompilerParams(vmem_limit_bytes=SPECTRA_VMEM),
        name="spectra",
    )(half.reshape(1).astype(jnp.int32), jnp.asarray(table), echoes)


def spread_body(weight_ref, out_ref, *, bins):
    beams = weight_ref.shape[1]
    elements = weight_ref.shape[2]
    group = 128
    width = group * 2 * bins
    lane = lax.broadcasted_iota(jnp.int32, (group, width), 1)
    row = lax.broadcasted_iota(jnp.int32, (group, width), 0)
    repeat = jnp.where(lane // (2 * bins) == row, 1.0, 0.0).astype(jnp.bfloat16)
    col = lax.broadcasted_iota(jnp.int32, (beams, width), 1)
    is_real = (col // bins) % 2 == 0
    for at in range(elements // group):
        span = slice(at * group, (at + 1) * group)
        here = slice(at * width, (at + 1) * width)
        real = jnp.dot(weight_ref[0, :, span], repeat, preferred_element_type=jnp.float32)
        imag = jnp.dot(weight_ref[1, :, span], repeat, preferred_element_type=jnp.float32)
        out_ref[:beams, here] = jnp.where(is_real, real, -imag).astype(jnp.bfloat16)
        out_ref[beams:, here] = jnp.where(is_real, imag, real).astype(jnp.bfloat16)


def spread(beam_weights, bins):
    _, beams, elements = beam_weights.shape
    return pl.pallas_call(
        functools.partial(spread_body, bins=bins),
        in_specs=whole_vmem(1),
        out_specs=whole_vmem(1)[0],
        out_shape=jax.ShapeDtypeStruct((2 * beams, elements * 2 * bins), jnp.bfloat16),
        compiler_params=pltpu.CompilerParams(vmem_limit_bytes=SMALL_VMEM),
        name="spread",
    )(beam_weights)


def beam_sums(spectra_ref, spread_ref, bins):
    elems, ranges = spectra_ref.shape[:2]
    rows = spectra_ref.shape[2] * spectra_ref.shape[3]
    received = jnp.concatenate(
        [
            jnp.concatenate(
                [spectra_ref[n, j].reshape(rows, spectra_ref.shape[4]) for n in range(elems)], axis=0
            )
            for j in range(ranges)
        ],
        axis=1,
    )
    weights = spread_ref[...]
    own = lax.broadcasted_iota(jnp.int32, weights.shape, 1) % bins
    return [
        jnp.dot(
            jnp.where(own == d, weights, jnp.zeros_like(weights)),
            received,
            preferred_element_type=jnp.float32,
        )
        for d in range(bins)
    ]


def partial_body(spectra_ref, spread_ref, out_ref):
    for d, value in enumerate(beam_sums(spectra_ref, spread_ref, out_ref.shape[0])):
        out_ref[d] = value.astype(out_ref.dtype)


def partial_sums(bound, spread_weights, bins, dtype):
    shape = (bins, spread_weights.shape[0], bound.shape[1] * bound.shape[4])
    return pl.pallas_call(
        partial_body,
        in_specs=whole_vmem(2),
        out_specs=whole_vmem(1)[0],
        out_shape=jax.ShapeDtypeStruct(shape, dtype),
        compiler_params=pltpu.CompilerParams(vmem_limit_bytes=BEAMS_VMEM),
        name="partial_sums",
    )(bound, spread_weights)


def split(value):
    high = value.astype(jnp.bfloat16)
    return high, (value - high.astype(jnp.float32)).astype(jnp.bfloat16)


NT = (((1,), (1,)), ((), ()))


def c_mul(a, b):
    return a[0] * b[0] - a[1] * b[1], a[0] * b[1] + a[1] * b[0]
def c_mulc(a, b):
    return a[0] * b[0] + a[1] * b[1], a[1] * b[0] - a[0] * b[1]
def conj(a): return a[0], -a[1]
def c_add(a, b): return a[0] + b[0], a[1] + b[1]
def c_sub(a, b): return a[0] - b[0], a[1] - b[1]
def scale(a, r): return a[0] * r, a[1] * r

def inverse_pair(m):
    a, b, d = m
    r = 1.0 / (a * d - (b[0] * b[0] + b[1] * b[1]))
    return d * r, (-b[0] * r, -b[1] * r), a * r

def inverse_four(e):
    ea, eb, ed = inverse_pair((e[0][0][0], e[0][1], e[1][1][0]))
    f = [[e[0][2], e[0][3]], [e[1][2], e[1][3]]]
    t = [[None, None], [None, None]]
    for l in range(2):
        t[0][l] = c_add(scale(f[0][l], ea), c_mul(eb, f[1][l]))
        t[1][l] = c_add(c_mulc(f[0][l], eb), scale(f[1][l], ed))
    def herm(l, m):
        return c_add(c_mulc(t[0][m], f[0][l]), c_mulc(t[1][m], f[1][l]))
    def herm_re(l):
        return (t[0][l][0]*f[0][l][0] + t[0][l][1]*f[0][l][1]) + (t[1][l][0]*f[1][l][0] + t[1][l][1]*f[1][l][1])
    s = (e[2][2][0] - herm_re(0), c_sub(e[2][3], herm(0, 1)), e[3][3][0] - herm_re(1))
    sa, sb, sd = inverse_pair(s)
    u = [[None, None], [None, None]]
    for j in range(2):
        x = c_add(scale(t[j][0], sa), c_mulc(t[j][1], sb))
        y = c_add(c_mul(t[j][0], sb), scale(t[j][1], sd))
        u[j][0] = (-x[0], -x[1]); u[j][1] = (-y[0], -y[1])
    def corr(j, m):
        return c_add(c_mulc(u[j][0], t[m][0]), c_mulc(u[j][1], t[m][1]))
    zero = jnp.zeros_like(ea)
    p00 = ea - corr(0, 0)[0]; p11 = ed - corr(1, 1)[0]
    p01 = c_sub(eb, corr(0, 1))
    inv = [[None]*4 for _ in range(4)]
    inv[0][0] = (p00, None); inv[1][1] = (p11, None); inv[0][1] = p01
    inv[2][2] = (sa, None); inv[3][3] = (sd, None); inv[2][3] = sb
    for j in range(2):
        for l in range(2): inv[j][2+l] = u[j][l]
    for j in range(4):
        for l in range(j): inv[j][l] = conj(inv[l][j])
    return inv


def turn(x):
    half = x.shape[1] // 2
    lane = lax.broadcasted_iota(jnp.int32, x.shape, 1)
    y = pltpu.roll(x, half, 1)
    return jnp.where(lane < half, -y, y)


def sweep(rows, columns, updated):
    shape = rows[0].shape
    beams = shape[1] // 2
    lane = lax.broadcasted_iota(jnp.int32, shape, 1)
    upper = lax.broadcasted_iota(jnp.int32, shape, 0) < 4

    def col(x, k):
        return jnp.broadcast_to(x[:, k : k + 1], shape)

    for step, k in enumerate(columns):
        inside = ((lane >= k) & (lane < k + 4)) | ((lane >= beams + k) & (lane < beams + k + 4))
        pivot = []
        for q in (2 * step, 2 * step + 1):
            x = rows[q]
            y = pltpu.roll(x, 4, 0)
            pivot += [jnp.where(upper, x, y), jnp.where(upper, y, x)]
        entry = [[None] * 4 for _ in range(4)]
        for j in range(4):
            for l in range(j, 4):
                entry[j][l] = (col(pivot[j], k + l), col(pivot[j], beams + k + l) if l > j else None)
        inv = inverse_four(entry)
        unit = [jnp.where(lane == k + l, 1.0, jnp.where(inside, 0.0, pivot[l])) for l in range(4)]
        turned = [turn(x) for x in unit]
        b, bt = [], []
        for j in range(4):
            acc, tacc = unit[j] * inv[j][j][0], turned[j] * inv[j][j][0]
            for l in range(4):
                if l != j:
                    acc = acc + (unit[l] * inv[j][l][0] + turned[l] * inv[j][l][1])
                    tacc = tacc + (turned[l] * inv[j][l][0] - unit[l] * inv[j][l][1])
            b.append(acc)
            bt.append(tacc)
        for q in updated(step):
            x = rows[q]
            acc = jnp.where(inside, 0.0, x)
            for l in range(4):
                acc = acc - (col(x, k + l) * b[l] + col(x, beams + k + l) * bt[l])
            rows[q] = acc
        for q in (0, 1):
            rows[2 * step + q] = jnp.where(upper, b[2 * q], b[2 * q + 1])
    return rows


def eliminate(systems, sources, rows_ref, size=BLOCK):
    count = len(systems)
    beams = systems[0].shape[0]
    blocks = size // 2
    rest = [
        jnp.concatenate([systems[n], jnp.broadcast_to(sources[n], (8, 2 * beams))], axis=0) for n in range(count)
    ]
    for first in range(0, beams, size):
        base = count * first
        for n in range(count):
            rows_ref[pl.ds(base + n, size, stride=count), :] = rest[n][:size]
        rows = [rows_ref[base + 8 * q : base + 8 * q + 8] for q in range(blocks)]
        columns = range(first, first + size, 4)
        if first + size == beams:
            bottoms = [value[size : size + 1] for value in rest]
            rows.append(jnp.concatenate(bottoms + bottoms, axis=0))
            return sweep(rows, columns, lambda step: range(2 * step + 2, blocks + 1))[blocks]
        rows = sweep(rows, columns, lambda step: [q for q in range(blocks) if q // 2 != step])
        for q in range(blocks):
            rows_ref[base + 8 * q : base + 8 * q + 8] = rows[q]
        at = (lax.broadcasted_iota(jnp.int32, rest[0][size:].shape, 1) - first) % beams
        for n in range(count):
            top = rows_ref[pl.ds(base + n, size, stride=count), :]
            value = rest[n][size:]
            taken = jnp.dot(
                packed_left(value, at, size), packed_right(top, first), preferred_element_type=jnp.float32
            )
            rest[n] = jnp.where(at < size, 0.0, value) - taken


def packed_left(value, at, size):
    high, low = (part.astype(jnp.float32) for part in split(value))
    again = jnp.where(at < 2 * size, pltpu.roll(low, size, 1), pltpu.roll(high, 2 * size, 1))
    return jnp.where(at < size, high, again).astype(jnp.bfloat16)


def packed_right(top, first):
    size, width = top.shape
    count = width // size
    pieces = [jnp.zeros(top.shape, jnp.bfloat16)] * count
    for start, rows in ((first, top), (first + width // 2, turn(top))):
        high, low = split(rows)
        for step, piece in enumerate((high, high, low)):
            pieces[(start // size + step) % count] = piece
    return jnp.concatenate(pieces, axis=0)


def beams_body(
    side_ref, spectra_ref, spread_ref, far_ref, pulse_ref, steer_ref, own_ref, send_ref, rows_ref
):
    bins, total, gates = far_ref.shape
    beams = total // 2
    ranges = gates // own_ref.shape[2]
    near = beam_sums(spectra_ref, spread_ref, bins)
    sums = [near[d] + far_ref[d].astype(jnp.float32) for d in range(bins)]
    half = gates // ranges
    high, low = split(
        jnp.concatenate(
            [
                jnp.concatenate(
                    [
                        value[part * beams : (part + 1) * beams, block * half : (block + 1) * half]
                        for block in range(ranges)
                        for part in range(2)
                    ],
                    axis=1,
                )
                for value in sums
            ],
            axis=0,
        )
    )
    formed = [0.0] * ranges
    for block in range(ranges):
        into = slice(block * 2 * half, (block + 1) * 2 * half)
        pulse = pulse_ref[block * 2 * half :, into]
        for piece in (high, low):
            formed[block] = formed[block] + jnp.dot(
                piece[:, block * 2 * half :], pulse, preferred_element_type=jnp.float32
            )
    sub = lax.broadcasted_iota(jnp.int32, (beams, 2 * beams), 0)
    lane = lax.broadcasted_iota(jnp.int32, (beams, 2 * beams), 1)
    both, systems = [], []
    for d in range(bins):
        mine = slice(d * beams, (d + 1) * beams)
        real = jnp.concatenate([value[mine, :half] for value in formed], axis=1)
        imag = jnp.concatenate([value[mine, half:] for value in formed], axis=1)
        top = jnp.concatenate([real, imag], axis=1)
        t_high, t_low = split(top)
        u_high, u_low = split(jnp.concatenate([-imag, real], axis=1))
        left = jnp.concatenate([t_high, t_low], axis=0)
        both.append(left)
        products = lax.dot_general(
            left, jnp.concatenate([t_high, u_high, t_low, u_low], axis=0), NT, preferred_element_type=jnp.float32
        )
        cov = (
            products[:beams, : 2 * beams] + products[:beams, 2 * beams :] + products[beams:, : 2 * beams]
        )
        cov = cov * (1.0 / gates)
        on_diagonal = sub == lane
        trace = jnp.sum(jnp.where(on_diagonal, cov, 0.0), axis=(0, 1), keepdims=True)
        loading = load_ratio * trace / beams + epsilon
        cov = jnp.where(on_diagonal, cov + loading, cov) * (1.0 / loading)
        systems.append(cov)
    steer = steer_ref[...]
    sources = [steer[d : d + 1] for d in range(bins)]
    conj = -eliminate(systems, sources, rows_ref)[:bins]
    response = jnp.sum(conj * steer, axis=1, keepdims=True)
    weight = conj / response
    part_of = lax.broadcasted_iota(jnp.int32, weight.shape, 1) < beams
    other = pltpu.roll(weight, beams, 1)
    pieces = []
    for twice in (jnp.where(part_of, weight, other), jnp.where(part_of, other, weight)):
        w_high, w_low = split(twice)
        pieces += [w_high, jnp.where(part_of, w_low, jnp.zeros_like(w_low))]
    left = jnp.concatenate(pieces, axis=0)
    first_side = side_ref[0] == 0
    row = lax.broadcasted_iota(jnp.int32, (bins, 2 * gates), 0)
    by_real = by_imag = jnp.zeros((bins, 2 * gates), jnp.float32)
    for d in range(bins):
        out = jnp.dot(left, both[d], preferred_element_type=jnp.float32)
        by_real = jnp.where(row == d, out[:bins] + out[bins : 2 * bins], by_real)
        by_imag = jnp.where(row == d, out[2 * bins : 3 * bins] + out[3 * bins :], by_imag)
    joined = (
        by_real[:, :gates] - by_imag[:, gates:],
        by_real[:, gates:] + by_imag[:, :gates],
    )
    nothing = jnp.zeros((bins, half), jnp.float32)
    for part in range(2):
        first, second = joined[part][:, :half], joined[part][:, half:]
        own_ref[part] = jnp.concatenate(
            [jnp.where(first_side, first, nothing), jnp.where(first_side, nothing, second)], axis=0
        )
        send_ref[part] = jnp.concatenate(
            [jnp.where(first_side, second, nothing), jnp.where(first_side, nothing, first)], axis=0
        )


def on_device_owned(echoes, replica, beam_weights, steering):
    elems, ranges = lax.axis_size("elem"), lax.axis_size("range")
    devices = elems * ranges
    _, own_elements, pulses, gate_count = echoes.shape
    bins = pulses // devices
    elements = beam_weights.shape[2]
    gates = gate_count * ranges
    side = lax.axis_index("range")
    half = lax.axis_index("elem") // (elems // 2)
    group = devices // 2
    groups = [list(range(group)), list(range(group, devices))]

    def gathered(owner_half):
        sent = spectra(owner_half, echoes, devices)
        bound = lax.all_to_all(sent, ("elem", "range"), 0, 0, tiled=True, axis_index_groups=groups)
        return bound.reshape(elems // 2, ranges, own_elements // 2, 4 * bins, gate_count)

    here = lax.dynamic_slice_in_dim(beam_weights, half * (elements // 2), elements // 2, 2)
    spread_weights = spread(here, bins)
    crossing = partial_sums(gathered(1 - half), spread_weights, bins, jnp.bfloat16)
    far = lax.ppermute(crossing, "elem", [(n, (n + elems // 2) % elems) for n in range(elems)])
    near = gathered(half)
    pulse = pulse_kernel(replica, gates)[:, :, :gates]
    pulse = pulse.reshape(2, 2, ranges, gate_count, ranges, gate_count)
    pulse = pulse.transpose(2, 0, 3, 4, 1, 5).reshape(2 * gates, 2 * gates)
    own_steering = lax.dynamic_slice_in_dim(steering, side * bins, bins, 1)
    steer_row = jnp.concatenate([own_steering[0], -own_steering[1]], axis=1)
    shape = jax.ShapeDtypeStruct((2, 2 * bins, gate_count), jnp.float32)
    own, send = pl.pallas_call(
        beams_body,
        in_specs=[pl.BlockSpec(memory_space=pltpu.SMEM)] + whole_vmem(5),
        out_specs=whole_vmem(2),
        out_shape=[shape, shape],
        scratch_shapes=[pltpu.VMEM((bins * beam_weights.shape[1], 2 * beam_weights.shape[1]), jnp.float32)],
        compiler_params=pltpu.CompilerParams(vmem_limit_bytes=BEAMS_VMEM),
        name="beams",
    )(side.reshape(1).astype(jnp.int32), near, spread_weights, far, pulse, steer_row)
    return own + lax.ppermute(send, "range", [(0, 1), (1, 0)])


def on_device(echoes, replica, beam_weights, steering):
    elems, ranges = lax.axis_size("elem"), lax.axis_size("range")
    pulses, gate_count = echoes.shape[2:]
    beams, elements = beam_weights.shape[1:]
    owned = (
        ranges == 2
        and pulses == 4 * elems * ranges
        and gate_count % 128 == 0
        and beams == 64
        and elems % 2 == 0
        and elements % 256 == 0
        and echoes.shape[1] % 8 == 0
        and replica.shape[1] <= gate_count
    )
    run = on_device_owned if owned else on_device_general
    return run(echoes, replica, beam_weights, steering)


def solution(mesh):
    return jax.shard_map(
        on_device,
        mesh=mesh,
        in_specs=(P(None, "elem", None, "range"), P(), P(), P(None, "elem", None)),
        out_specs=P(None, "elem", "range"),
        check_vma=False,
    )
```

```python
import functools

import jax
import jax.numpy as jnp
import numpy as np
from jax import lax
from jax.experimental import pallas as pl
from jax.experimental.pallas import tpu as pltpu
from jax.sharding import PartitionSpec as P

load_ratio = 0.1
epsilon = 1e-06
SPECTRA_VMEM = 56 << 20
STEPS = 2
BLOCK = 16
SMALL_VMEM = 14 << 20
BEAMS_VMEM = 24 << 20


def shifted(value, axis, steps):
    count = lax.axis_size(axis)
    first, last = (max(0, -steps), min(count, count - steps))
    return lax.ppermute(value, axis, [(source, source + steps) for source in range(first, last)])


def correlation_matrix(tap_values, gate_count):
    tap_count = tap_values.shape[0]
    span_width = gate_count + tap_count - 1
    padded_taps = jnp.concatenate(
        [tap_values, jnp.zeros((span_width + 1 - tap_count,), tap_values.dtype)]
    )
    tiled_rows = jnp.tile(padded_taps, gate_count)[: gate_count * span_width].reshape(
        gate_count, span_width
    )
    return tiled_rows.T


def pulse_kernel(replica, gate_count):
    real_part = correlation_matrix(replica[0], gate_count)
    imag_part = correlation_matrix(replica[1], gate_count)
    return jnp.stack([jnp.stack([real_part, imag_part]), jnp.stack([-imag_part, real_part])])


def doppler_table(pulses):
    index = np.arange(pulses, dtype=np.int64)
    phase_index = (index[:, None] * index[None, :]) % pulses
    phase_angle = np.float32(2.0 * np.pi) * phase_index.astype(np.float32) / np.float32(pulses)
    scale = np.float32(1.0) / np.sqrt(np.float32(pulses))
    cosine = np.cos(phase_angle) * scale
    sine = np.sin(phase_angle) * scale
    table = np.stack([np.stack([cosine, -sine]), np.stack([sine, cosine])])
    return table.astype(jnp.bfloat16)


def beam_kernel(beam_weights):
    weight_re = beam_weights[0]
    weight_im = beam_weights[1]
    return jnp.stack([jnp.stack([weight_re, weight_im]), jnp.stack([-weight_im, weight_re])])


def adapt(gram_sum, steering, formed):
    beams = formed.shape[2]
    cov_re = gram_sum[:, :beams, :beams] + gram_sum[:, beams:, beams:]
    cov_im = gram_sum[:, beams:, :beams] - gram_sum[:, :beams, beams:]
    loading = load_ratio * jnp.trace(cov_re, axis1=1, axis2=2) / beams + epsilon
    upper = jnp.concatenate([cov_re, -cov_im], axis=2)
    lower = jnp.concatenate([cov_im, cov_re], axis=2)
    system = jnp.concatenate([upper, lower], axis=1)
    system = system + loading[:, None, None] * jnp.eye(2 * beams, dtype=jnp.float32)[None]
    factor = jnp.linalg.cholesky(system)
    right_side = jnp.concatenate([steering[0], steering[1]], axis=-1)
    solved = jax.scipy.linalg.cho_solve((factor, True), right_side[..., None])[..., 0]
    response = jnp.sum(right_side * solved, axis=-1)
    weights = solved / response[:, None]
    weight_re = weights[:, :beams]
    weight_im = weights[:, beams:]
    beam_re = formed[:, 0].astype(jnp.float32)
    beam_im = formed[:, 1].astype(jnp.float32)
    high = lax.Precision.HIGHEST
    out_re = jnp.einsum("db,dbr->dr", weight_re, beam_re, precision=high) + jnp.einsum(
        "db,dbr->dr", weight_im, beam_im, precision=high
    )
    out_im = jnp.einsum("db,dbr->dr", weight_re, beam_im, precision=high) - jnp.einsum(
        "db,dbr->dr", weight_im, beam_re, precision=high
    )
    return jnp.stack([out_re, out_im])


def on_device_general(echoes, replica, beam_weights, steering):
    pulses = echoes.shape[2]
    gate_count = echoes.shape[3]
    tap_count = replica.shape[1]
    following = shifted(echoes[:, :, :, : tap_count - 1], "range", -1)
    padded = jnp.concatenate([echoes, following], axis=3)
    compressed = jnp.einsum(
        "cepj,cojr->oepr",
        padded,
        pulse_kernel(replica, gate_count),
        preferred_element_type=jnp.float32,
    ).astype(jnp.bfloat16)
    doppler = jnp.einsum(
        "cepr,codp->oedr",
        compressed,
        jnp.asarray(doppler_table(pulses)),
        preferred_element_type=jnp.float32,
    ).astype(jnp.bfloat16)
    kernel_full = beam_kernel(beam_weights)
    own_bins = pulses // lax.axis_size("elem")
    beam_sums = jnp.einsum(
        "cedr,cobe->dobr",
        lax.all_to_all(doppler, "elem", split_axis=2, concat_axis=1, tiled=True),
        kernel_full,
        preferred_element_type=jnp.float32,
    )
    formed = beam_sums.astype(jnp.bfloat16)
    beams = formed.shape[2]
    stacked = formed.reshape(own_bins, 2 * beams, gate_count)
    partial_gram = jnp.einsum("dbr,dcr->dbc", stacked, stacked, preferred_element_type=jnp.float32)
    gram_sum = lax.psum(partial_gram, "range") / (gate_count * lax.axis_size("range"))
    return adapt(gram_sum, steering, formed)


def whole_vmem(count):
    return [pl.BlockSpec(memory_space=pltpu.VMEM)] * count


def spectra_body(half_ref, table_hbm, echo_hbm, out_hbm, table_ref, echo_ref, out_ref, table_sem, in_sem, out_sem):
    members = out_ref.shape[0]
    gates = echo_ref.shape[3]
    steps = in_sem.shape[0]
    block = echo_ref.shape[1] // steps
    pairs = block // 2
    fetch_table = pltpu.make_async_copy(table_hbm.at[half_ref[0]], table_ref, table_sem)
    fetches = [
        pltpu.make_async_copy(
            echo_hbm.at[:, pl.ds(step * block, block)],
            echo_ref.at[:, pl.ds(step * block, block)],
            in_sem.at[step],
        )
        for step in range(steps)
    ]
    stores = [
        pltpu.make_async_copy(
            out_ref.at[:, pl.ds(step * pairs, pairs)],
            out_hbm.at[:, pl.ds(step * pairs, pairs)],
            out_sem.at[step],
        )
        for step in range(steps)
    ]
    fetch_table.start()
    for fetch in fetches:
        fetch.start()
    fetch_table.wait()
    table = table_ref[...]
    for step in range(steps):
        fetches[step].wait()
        for pair in range(step * pairs, (step + 1) * pairs):
            even, odd = 2 * pair, 2 * pair + 1
            samples = jnp.concatenate(
                [
                    jnp.concatenate([echo_ref[0, even], echo_ref[0, odd]], axis=1),
                    jnp.concatenate([echo_ref[1, even], echo_ref[1, odd]], axis=1),
                ],
                axis=0,
            )
            bins = jnp.dot(table, samples, preferred_element_type=jnp.float32)
            bins = bins.reshape(members, bins.shape[0] // members, 2 * gates)
            rows = jnp.concatenate([bins[:, :, :gates], bins[:, :, gates:]], axis=1)
            out_ref[:, pair] = rows.astype(jnp.bfloat16)
        stores[step].start()
    for store in stores:
        store.wait()


def spectra(half, echoes, devices, steps=STEPS):
    _, elements, pulses, gates = echoes.shape
    bins = pulses // devices
    members = devices // 2
    table = doppler_table(pulses)
    table = table.transpose(2, 1, 0, 3).reshape(devices, bins, 2, 2 * pulses)
    table = table.transpose(0, 2, 1, 3).reshape(2, pulses, 2 * pulses)
    shape = (members, elements // 2, 4 * bins, gates)
    return pl.pallas_call(
        spectra_body,
        in_specs=[pl.BlockSpec(memory_space=pltpu.SMEM)] + [pl.BlockSpec(memory_space=pl.ANY)] * 2,
        out_specs=pl.BlockSpec(memory_space=pl.ANY),
        out_shape=jax.ShapeDtypeStruct(shape, jnp.bfloat16),
        scratch_shapes=[
            pltpu.VMEM((pulses, 2 * pulses), jnp.bfloat16),
            pltpu.VMEM(echoes.shape, jnp.bfloat16),
            pltpu.VMEM(shape, jnp.bfloat16),
            pltpu.SemaphoreType.DMA(()),
            pltpu.SemaphoreType.DMA((steps,)),
            pltpu.SemaphoreType.DMA((steps,)),
        ],
        compiler_params=pltpu.CompilerParams(vmem_limit_bytes=SPECTRA_VMEM),
        name="spectra",
    )(half.reshape(1).astype(jnp.int32), jnp.asarray(table), echoes)


def spread_body(weight_ref, out_ref, *, bins):
    beams = weight_ref.shape[1]
    elements = weight_ref.shape[2]
    group = 128
    width = group * 2 * bins
    lane = lax.broadcasted_iota(jnp.int32, (group, width), 1)
    row = lax.broadcasted_iota(jnp.int32, (group, width), 0)
    repeat = jnp.where(lane // (2 * bins) == row, 1.0, 0.0).astype(jnp.bfloat16)
    col = lax.broadcasted_iota(jnp.int32, (beams, width), 1)
    is_real = (col // bins) % 2 == 0
    for at in range(elements // group):
        span = slice(at * group, (at + 1) * group)
        here = slice(at * width, (at + 1) * width)
        real = jnp.dot(weight_ref[0, :, span], repeat, preferred_element_type=jnp.float32)
        imag = jnp.dot(weight_ref[1, :, span], repeat, preferred_element_type=jnp.float32)
        out_ref[:beams, here] = jnp.where(is_real, real, -imag).astype(jnp.bfloat16)
        out_ref[beams:, here] = jnp.where(is_real, imag, real).astype(jnp.bfloat16)


def spread(beam_weights, bins):
    _, beams, elements = beam_weights.shape
    return pl.pallas_call(
        functools.partial(spread_body, bins=bins),
        in_specs=whole_vmem(1),
        out_specs=whole_vmem(1)[0],
        out_shape=jax.ShapeDtypeStruct((2 * beams, elements * 2 * bins), jnp.bfloat16),
        compiler_params=pltpu.CompilerParams(vmem_limit_bytes=SMALL_VMEM),
        name="spread",
    )(beam_weights)


def beam_sums(spectra_ref, spread_ref, bins):
    elems, ranges = spectra_ref.shape[:2]
    rows = spectra_ref.shape[2] * spectra_ref.shape[3]
    received = jnp.concatenate(
        [
            jnp.concatenate(
                [spectra_ref[n, j].reshape(rows, spectra_ref.shape[4]) for n in range(elems)], axis=0
            )
            for j in range(ranges)
        ],
        axis=1,
    )
    weights = spread_ref[...]
    own = lax.broadcasted_iota(jnp.int32, weights.shape, 1) % bins
    return [
        jnp.dot(
            jnp.where(own == d, weights, jnp.zeros_like(weights)),
            received,
            preferred_element_type=jnp.float32,
        )
        for d in range(bins)
    ]


def crossing_body(side_ref, spectra_ref, spread_ref, same_ref, other_ref):
    bins, _, gates = same_ref.shape
    first_side = side_ref[0] == 0
    for d, value in enumerate(beam_sums(spectra_ref, spread_ref, bins)):
        first, second = value[:, :gates], value[:, gates:]
        same_ref[d] = jnp.where(first_side, first, second).astype(same_ref.dtype)
        other_ref[d] = jnp.where(first_side, second, first).astype(other_ref.dtype)


def crossing_sums(side, bound, spread_weights, bins):
    shape = jax.ShapeDtypeStruct((bins, spread_weights.shape[0], bound.shape[4]), jnp.bfloat16)
    return pl.pallas_call(
        crossing_body,
        in_specs=[pl.BlockSpec(memory_space=pltpu.SMEM)] + whole_vmem(2),
        out_specs=whole_vmem(2),
        out_shape=[shape, shape],
        compiler_params=pltpu.CompilerParams(vmem_limit_bytes=BEAMS_VMEM),
        name="crossing_sums",
    )(side, bound, spread_weights)


def split(value):
    high = value.astype(jnp.bfloat16)
    return high, (value - high.astype(jnp.float32)).astype(jnp.bfloat16)


NT = (((1,), (1,)), ((), ()))


def c_mul(a, b):
    return a[0] * b[0] - a[1] * b[1], a[0] * b[1] + a[1] * b[0]
def c_mulc(a, b):
    return a[0] * b[0] + a[1] * b[1], a[1] * b[0] - a[0] * b[1]
def conj(a): return a[0], -a[1]
def c_add(a, b): return a[0] + b[0], a[1] + b[1]
def c_sub(a, b): return a[0] - b[0], a[1] - b[1]
def scale(a, r): return a[0] * r, a[1] * r

def inverse_pair(m):
    a, b, d = m
    r = 1.0 / (a * d - (b[0] * b[0] + b[1] * b[1]))
    return d * r, (-b[0] * r, -b[1] * r), a * r

def inverse_four(e):
    ea, eb, ed = inverse_pair((e[0][0][0], e[0][1], e[1][1][0]))
    f = [[e[0][2], e[0][3]], [e[1][2], e[1][3]]]
    t = [[None, None], [None, None]]
    for l in range(2):
        t[0][l] = c_add(scale(f[0][l], ea), c_mul(eb, f[1][l]))
        t[1][l] = c_add(c_mulc(f[0][l], eb), scale(f[1][l], ed))
    def herm(l, m):
        return c_add(c_mulc(t[0][m], f[0][l]), c_mulc(t[1][m], f[1][l]))
    def herm_re(l):
        return (t[0][l][0]*f[0][l][0] + t[0][l][1]*f[0][l][1]) + (t[1][l][0]*f[1][l][0] + t[1][l][1]*f[1][l][1])
    s = (e[2][2][0] - herm_re(0), c_sub(e[2][3], herm(0, 1)), e[3][3][0] - herm_re(1))
    sa, sb, sd = inverse_pair(s)
    u = [[None, None], [None, None]]
    for j in range(2):
        x = c_add(scale(t[j][0], sa), c_mulc(t[j][1], sb))
        y = c_add(c_mul(t[j][0], sb), scale(t[j][1], sd))
        u[j][0] = (-x[0], -x[1]); u[j][1] = (-y[0], -y[1])
    def corr(j, m):
        return c_add(c_mulc(u[j][0], t[m][0]), c_mulc(u[j][1], t[m][1]))
    zero = jnp.zeros_like(ea)
    p00 = ea - corr(0, 0)[0]; p11 = ed - corr(1, 1)[0]
    p01 = c_sub(eb, corr(0, 1))
    inv = [[None]*4 for _ in range(4)]
    inv[0][0] = (p00, None); inv[1][1] = (p11, None); inv[0][1] = p01
    inv[2][2] = (sa, None); inv[3][3] = (sd, None); inv[2][3] = sb
    for j in range(2):
        for l in range(2): inv[j][2+l] = u[j][l]
    for j in range(4):
        for l in range(j): inv[j][l] = conj(inv[l][j])
    return inv


def turn(x):
    half = x.shape[1] // 2
    lane = lax.broadcasted_iota(jnp.int32, x.shape, 1)
    y = pltpu.roll(x, half, 1)
    return jnp.where(lane < half, -y, y)


def sweep(rows, columns, updated):
    shape = rows[0].shape
    beams = shape[1] // 2
    lane = lax.broadcasted_iota(jnp.int32, shape, 1)
    upper = lax.broadcasted_iota(jnp.int32, shape, 0) < 4

    def col(x, k):
        return jnp.broadcast_to(x[:, k : k + 1], shape)

    for step, k in enumerate(columns):
        inside = ((lane >= k) & (lane < k + 4)) | ((lane >= beams + k) & (lane < beams + k + 4))
        pivot = []
        for q in (2 * step, 2 * step + 1):
            x = rows[q]
            y = pltpu.roll(x, 4, 0)
            pivot += [jnp.where(upper, x, y), jnp.where(upper, y, x)]
        entry = [[None] * 4 for _ in range(4)]
        for j in range(4):
            for l in range(j, 4):
                entry[j][l] = (col(pivot[j], k + l), col(pivot[j], beams + k + l) if l > j else None)
        inv = inverse_four(entry)
        unit = [jnp.where(lane == k + l, 1.0, jnp.where(inside, 0.0, pivot[l])) for l in range(4)]
        turned = [turn(x) for x in unit]
        b, bt = [], []
        for j in range(4):
            acc, tacc = unit[j] * inv[j][j][0], turned[j] * inv[j][j][0]
            for l in range(4):
                if l != j:
                    acc = acc + (unit[l] * inv[j][l][0] + turned[l] * inv[j][l][1])
                    tacc = tacc + (turned[l] * inv[j][l][0] - unit[l] * inv[j][l][1])
            b.append(acc)
            bt.append(tacc)
        for q in updated(step):
            x = rows[q]
            acc = jnp.where(inside, 0.0, x)
            for l in range(4):
                acc = acc - (col(x, k + l) * b[l] + col(x, beams + k + l) * bt[l])
            rows[q] = acc
        for q in (0, 1):
            rows[2 * step + q] = jnp.where(upper, b[2 * q], b[2 * q + 1])
    return rows


def eliminate(systems, sources, rows_ref, size=BLOCK):
    count = len(systems)
    beams = systems[0].shape[0]
    blocks = size // 2
    rest = [
        jnp.concatenate([systems[n], jnp.broadcast_to(sources[n], (8, 2 * beams))], axis=0) for n in range(count)
    ]
    for first in range(0, beams, size):
        base = count * first
        for n in range(count):
            rows_ref[pl.ds(base + n, size, stride=count), :] = rest[n][:size]
        rows = [rows_ref[base + 8 * q : base + 8 * q + 8] for q in range(blocks)]
        columns = range(first, first + size, 4)
        if first + size == beams:
            bottoms = [value[size : size + 1] for value in rest]
            rows.append(jnp.concatenate(bottoms + bottoms, axis=0))
            return sweep(rows, columns, lambda step: range(2 * step + 2, blocks + 1))[blocks]
        rows = sweep(rows, columns, lambda step: [q for q in range(blocks) if q // 2 != step])
        for q in range(blocks):
            rows_ref[base + 8 * q : base + 8 * q + 8] = rows[q]
        at = (lax.broadcasted_iota(jnp.int32, rest[0][size:].shape, 1) - first) % beams
        for n in range(count):
            top = rows_ref[pl.ds(base + n, size, stride=count), :]
            value = rest[n][size:]
            taken = jnp.dot(
                packed_left(value, at, size), packed_right(top, first), preferred_element_type=jnp.float32
            )
            rest[n] = jnp.where(at < size, 0.0, value) - taken


def packed_left(value, at, size):
    high, low = (part.astype(jnp.float32) for part in split(value))
    again = jnp.where(at < 2 * size, pltpu.roll(low, size, 1), pltpu.roll(high, 2 * size, 1))
    return jnp.where(at < size, high, again).astype(jnp.bfloat16)


def packed_right(top, first):
    size, width = top.shape
    count = width // size
    pieces = [jnp.zeros(top.shape, jnp.bfloat16)] * count
    for start, rows in ((first, top), (first + width // 2, turn(top))):
        high, low = split(rows)
        for step, piece in enumerate((high, high, low)):
            pieces[(start // size + step) % count] = piece
    return jnp.concatenate(pieces, axis=0)


def beams_body(
    side_ref, spectra_ref, spread_ref, same_ref, other_ref, pulse_ref, steer_ref, own_ref, send_ref, rows_ref
):
    bins, total, half = same_ref.shape
    beams = total // 2
    ranges = spectra_ref.shape[1]
    gates = ranges * half
    first_side = side_ref[0] == 0
    near = beam_sums(spectra_ref, spread_ref, bins)
    sums = []
    for d in range(bins):
        same, other = same_ref[d].astype(jnp.float32), other_ref[d].astype(jnp.float32)
        far = [jnp.where(first_side, same, other), jnp.where(first_side, other, same)]
        sums.append(near[d] + jnp.concatenate(far, axis=1))
    high, low = split(
        jnp.concatenate(
            [
                jnp.concatenate(
                    [
                        value[part * beams : (part + 1) * beams, block * half : (block + 1) * half]
                        for block in range(ranges)
                        for part in range(2)
                    ],
                    axis=1,
                )
                for value in sums
            ],
            axis=0,
        )
    )
    formed = [0.0] * ranges
    for block in range(ranges):
        into = slice(block * 2 * half, (block + 1) * 2 * half)
        pulse = pulse_ref[block * 2 * half :, into]
        for piece in (high, low):
            formed[block] = formed[block] + jnp.dot(
                piece[:, block * 2 * half :], pulse, preferred_element_type=jnp.float32
            )
    sub = lax.broadcasted_iota(jnp.int32, (beams, 2 * beams), 0)
    lane = lax.broadcasted_iota(jnp.int32, (beams, 2 * beams), 1)
    both, systems = [], []
    for d in range(bins):
        mine = slice(d * beams, (d + 1) * beams)
        real = jnp.concatenate([value[mine, :half] for value in formed], axis=1)
        imag = jnp.concatenate([value[mine, half:] for value in formed], axis=1)
        top = jnp.concatenate([real, imag], axis=1)
        t_high, t_low = split(top)
        u_high, u_low = split(jnp.concatenate([-imag, real], axis=1))
        left = jnp.concatenate([t_high, t_low], axis=0)
        both.append(left)
        products = lax.dot_general(
            left, jnp.concatenate([t_high, u_high, t_low, u_low], axis=0), NT, preferred_element_type=jnp.float32
        )
        cov = (
            products[:beams, : 2 * beams] + products[:beams, 2 * beams :] + products[beams:, : 2 * beams]
        )
        cov = cov * (1.0 / gates)
        on_diagonal = sub == lane
        trace = jnp.sum(jnp.where(on_diagonal, cov, 0.0), axis=(0, 1), keepdims=True)
        loading = load_ratio * trace / beams + epsilon
        cov = jnp.where(on_diagonal, cov + loading, cov) * (1.0 / loading)
        systems.append(cov)
    steer = steer_ref[...]
    sources = [steer[d : d + 1] for d in range(bins)]
    conj = -eliminate(systems, sources, rows_ref)[:bins]
    response = jnp.sum(conj * steer, axis=1, keepdims=True)
    weight = conj / response
    part_of = lax.broadcasted_iota(jnp.int32, weight.shape, 1) < beams
    other = pltpu.roll(weight, beams, 1)
    pieces = []
    for twice in (jnp.where(part_of, weight, other), jnp.where(part_of, other, weight)):
        w_high, w_low = split(twice)
        pieces += [w_high, jnp.where(part_of, w_low, jnp.zeros_like(w_low))]
    left = jnp.concatenate(pieces, axis=0)
    row = lax.broadcasted_iota(jnp.int32, (bins, 2 * gates), 0)
    by_real = by_imag = jnp.zeros((bins, 2 * gates), jnp.float32)
    for d in range(bins):
        out = jnp.dot(left, both[d], preferred_element_type=jnp.float32)
        by_real = jnp.where(row == d, out[:bins] + out[bins : 2 * bins], by_real)
        by_imag = jnp.where(row == d, out[2 * bins : 3 * bins] + out[3 * bins :], by_imag)
    joined = (
        by_real[:, :gates] - by_imag[:, gates:],
        by_real[:, gates:] + by_imag[:, :gates],
    )
    nothing = jnp.zeros((bins, half), jnp.float32)
    for part in range(2):
        first, second = joined[part][:, :half], joined[part][:, half:]
        own_ref[part] = jnp.concatenate(
            [jnp.where(first_side, first, nothing), jnp.where(first_side, nothing, second)], axis=0
        )
        send_ref[part] = jnp.concatenate(
            [jnp.where(first_side, second, nothing), jnp.where(first_side, nothing, first)], axis=0
        )


def on_device_owned(echoes, replica, beam_weights, steering):
    elems, ranges = lax.axis_size("elem"), lax.axis_size("range")
    devices = elems * ranges
    _, own_elements, pulses, gate_count = echoes.shape
    bins = pulses // devices
    elements = beam_weights.shape[2]
    gates = gate_count * ranges
    side = lax.axis_index("range")
    half = lax.axis_index("elem") // (elems // 2)
    group = devices // 2
    seat = side.reshape(1).astype(jnp.int32)
    here = lax.dynamic_slice_in_dim(beam_weights, half * (elements // 2), elements // 2, 2)
    spread_weights = spread(here, bins)

    def exchanged(owner_half, axes, size):
        groups = [list(range(size)), list(range(size, 2 * size))]
        sent = spectra(owner_half, echoes, devices)
        bound = lax.all_to_all(sent, axes, 0, 0, tiled=True, axis_index_groups=groups)
        return bound.reshape(elems // 2, ranges, own_elements // 2, 4 * bins, gate_count)

    same, other = crossing_sums(seat, exchanged(1 - half, "elem", elems // 2), spread_weights, bins)
    across = [(n + group) % devices for n in range(devices)]
    same = lax.ppermute(same, ("elem", "range"), list(enumerate(across)))
    other = lax.ppermute(other, ("elem", "range"), [(n, to ^ 1) for n, to in enumerate(across)])
    near = exchanged(half, ("elem", "range"), group)
    pulse = pulse_kernel(replica, gates)[:, :, :gates]
    pulse = pulse.reshape(2, 2, ranges, gate_count, ranges, gate_count)
    pulse = pulse.transpose(2, 0, 3, 4, 1, 5).reshape(2 * gates, 2 * gates)
    own_steering = lax.dynamic_slice_in_dim(steering, side * bins, bins, 1)
    steer_row = jnp.concatenate([own_steering[0], -own_steering[1]], axis=1)
    shape = jax.ShapeDtypeStruct((2, 2 * bins, gate_count), jnp.float32)
    own, send = pl.pallas_call(
        beams_body,
        in_specs=[pl.BlockSpec(memory_space=pltpu.SMEM)] + whole_vmem(6),
        out_specs=whole_vmem(2),
        out_shape=[shape, shape],
        scratch_shapes=[pltpu.VMEM((bins * beam_weights.shape[1], 2 * beam_weights.shape[1]), jnp.float32)],
        compiler_params=pltpu.CompilerParams(vmem_limit_bytes=BEAMS_VMEM),
        name="beams",
    )(seat, near, spread_weights, same, other, pulse, steer_row)
    return own + lax.ppermute(send, "range", [(0, 1), (1, 0)])


def on_device(echoes, replica, beam_weights, steering):
    elems, ranges = lax.axis_size("elem"), lax.axis_size("range")
    pulses, gate_count = echoes.shape[2:]
    beams, elements = beam_weights.shape[1:]
    owned = (
        ranges == 2
        and pulses == 4 * elems * ranges
        and gate_count % 128 == 0
        and beams == 64
        and elems % 2 == 0
        and elements % 256 == 0
        and echoes.shape[1] % 8 == 0
        and replica.shape[1] <= gate_count
    )
    run = on_device_owned if owned else on_device_general
    return run(echoes, replica, beam_weights, steering)


def solution(mesh):
    return jax.shard_map(
        on_device,
        mesh=mesh,
        in_specs=(P(None, "elem", None, "range"), P(), P(), P(None, "elem", None)),
        out_specs=P(None, "elem", "range"),
        check_vma=False,
    )
```

```python
import functools

import jax
import jax.numpy as jnp
import numpy as np
from jax import lax
from jax.experimental import pallas as pl
from jax.experimental.pallas import tpu as pltpu
from jax.sharding import PartitionSpec as P

load_ratio = 0.1
epsilon = 1e-06
SPECTRA_VMEM = 56 << 20
STEPS = 2
BLOCK = 16
SMALL_VMEM = 14 << 20
BEAMS_VMEM = 24 << 20


def shifted(value, axis, steps):
    count = lax.axis_size(axis)
    first, last = (max(0, -steps), min(count, count - steps))
    return lax.ppermute(value, axis, [(source, source + steps) for source in range(first, last)])


def correlation_matrix(tap_values, gate_count):
    tap_count = tap_values.shape[0]
    span_width = gate_count + tap_count - 1
    padded_taps = jnp.concatenate(
        [tap_values, jnp.zeros((span_width + 1 - tap_count,), tap_values.dtype)]
    )
    tiled_rows = jnp.tile(padded_taps, gate_count)[: gate_count * span_width].reshape(
        gate_count, span_width
    )
    return tiled_rows.T


def pulse_kernel(replica, gate_count):
    real_part = correlation_matrix(replica[0], gate_count)
    imag_part = correlation_matrix(replica[1], gate_count)
    return jnp.stack([jnp.stack([real_part, imag_part]), jnp.stack([-imag_part, real_part])])


def doppler_table(pulses):
    index = np.arange(pulses, dtype=np.int64)
    phase_index = (index[:, None] * index[None, :]) % pulses
    phase_angle = np.float32(2.0 * np.pi) * phase_index.astype(np.float32) / np.float32(pulses)
    scale = np.float32(1.0) / np.sqrt(np.float32(pulses))
    cosine = np.cos(phase_angle) * scale
    sine = np.sin(phase_angle) * scale
    table = np.stack([np.stack([cosine, -sine]), np.stack([sine, cosine])])
    return table.astype(jnp.bfloat16)


def beam_kernel(beam_weights):
    weight_re = beam_weights[0]
    weight_im = beam_weights[1]
    return jnp.stack([jnp.stack([weight_re, weight_im]), jnp.stack([-weight_im, weight_re])])


def adapt(gram_sum, steering, formed):
    beams = formed.shape[2]
    cov_re = gram_sum[:, :beams, :beams] + gram_sum[:, beams:, beams:]
    cov_im = gram_sum[:, beams:, :beams] - gram_sum[:, :beams, beams:]
    loading = load_ratio * jnp.trace(cov_re, axis1=1, axis2=2) / beams + epsilon
    upper = jnp.concatenate([cov_re, -cov_im], axis=2)
    lower = jnp.concatenate([cov_im, cov_re], axis=2)
    system = jnp.concatenate([upper, lower], axis=1)
    system = system + loading[:, None, None] * jnp.eye(2 * beams, dtype=jnp.float32)[None]
    factor = jnp.linalg.cholesky(system)
    right_side = jnp.concatenate([steering[0], steering[1]], axis=-1)
    solved = jax.scipy.linalg.cho_solve((factor, True), right_side[..., None])[..., 0]
    response = jnp.sum(right_side * solved, axis=-1)
    weights = solved / response[:, None]
    weight_re = weights[:, :beams]
    weight_im = weights[:, beams:]
    beam_re = formed[:, 0].astype(jnp.float32)
    beam_im = formed[:, 1].astype(jnp.float32)
    high = lax.Precision.HIGHEST
    out_re = jnp.einsum("db,dbr->dr", weight_re, beam_re, precision=high) + jnp.einsum(
        "db,dbr->dr", weight_im, beam_im, precision=high
    )
    out_im = jnp.einsum("db,dbr->dr", weight_re, beam_im, precision=high) - jnp.einsum(
        "db,dbr->dr", weight_im, beam_re, precision=high
    )
    return jnp.stack([out_re, out_im])


def on_device_general(echoes, replica, beam_weights, steering):
    pulses = echoes.shape[2]
    gate_count = echoes.shape[3]
    tap_count = replica.shape[1]
    following = shifted(echoes[:, :, :, : tap_count - 1], "range", -1)
    padded = jnp.concatenate([echoes, following], axis=3)
    compressed = jnp.einsum(
        "cepj,cojr->oepr",
        padded,
        pulse_kernel(replica, gate_count),
        preferred_element_type=jnp.float32,
    ).astype(jnp.bfloat16)
    doppler = jnp.einsum(
        "cepr,codp->oedr",
        compressed,
        jnp.asarray(doppler_table(pulses)),
        preferred_element_type=jnp.float32,
    ).astype(jnp.bfloat16)
    kernel_full = beam_kernel(beam_weights)
    own_bins = pulses // lax.axis_size("elem")
    beam_sums = jnp.einsum(
        "cedr,cobe->dobr",
        lax.all_to_all(doppler, "elem", split_axis=2, concat_axis=1, tiled=True),
        kernel_full,
        preferred_element_type=jnp.float32,
    )
    formed = beam_sums.astype(jnp.bfloat16)
    beams = formed.shape[2]
    stacked = formed.reshape(own_bins, 2 * beams, gate_count)
    partial_gram = jnp.einsum("dbr,dcr->dbc", stacked, stacked, preferred_element_type=jnp.float32)
    gram_sum = lax.psum(partial_gram, "range") / (gate_count * lax.axis_size("range"))
    return adapt(gram_sum, steering, formed)


def whole_vmem(count):
    return [pl.BlockSpec(memory_space=pltpu.VMEM)] * count


def spectra_body(half_ref, place_ref, table_hbm, echo_hbm, *refs, apart):
    *out_hbm, table_ref, echo_ref, out_ref, table_sem, in_sem, out_sem = refs
    members = table_ref.shape[0]
    gates = echo_ref.shape[3]
    steps = in_sem.shape[0]
    block = echo_ref.shape[1] // steps
    pairs = block // 2
    fetch_table = pltpu.make_async_copy(table_hbm.at[half_ref[0]], table_ref, table_sem)
    fetches = [
        pltpu.make_async_copy(
            echo_hbm.at[:, pl.ds(step * block, block)],
            echo_ref.at[:, pl.ds(step * block, block)],
            in_sem.at[step],
        )
        for step in range(steps)
    ]
    if apart:
        stores = [
            pltpu.make_async_copy(out_ref.at[n], out_hbm[n], out_sem.at[n]) for n in range(members)
        ]
    else:
        stores = [
            pltpu.make_async_copy(
                out_ref.at[:, :, pl.ds(step * pairs, pairs)],
                out_hbm[0].at[:, :, pl.ds(step * pairs, pairs)],
                out_sem.at[step],
            )
            for step in range(steps)
        ]
    fetch_table.start()
    for fetch in fetches:
        fetch.start()
    fetch_table.wait()
    place = place_ref[0]
    table = jnp.concatenate([table_ref[place ^ n if apart else n] for n in range(members)], axis=0)
    sides = out_ref.shape[1]
    for step in range(steps):
        fetches[step].wait()
        for pair in range(step * pairs, (step + 1) * pairs):
            even, odd = 2 * pair, 2 * pair + 1
            samples = jnp.concatenate(
                [
                    jnp.concatenate([echo_ref[0, even], echo_ref[0, odd]], axis=1),
                    jnp.concatenate([echo_ref[1, even], echo_ref[1, odd]], axis=1),
                ],
                axis=0,
            )
            bins = jnp.dot(table, samples, preferred_element_type=jnp.float32)
            bins = bins.reshape(members, sides, bins.shape[0] // (members * sides), 2 * gates)
            rows = jnp.concatenate([bins[..., :gates], bins[..., gates:]], axis=2)
            out_ref[:, :, pair] = rows.astype(jnp.bfloat16)
        if not apart:
            stores[step].start()
    if apart:
        for store in stores:
            store.start()
    for store in stores:
        store.wait()


def spectra(half, place, echoes, members, sides, apart, steps=STEPS):
    _, elements, pulses, gates = echoes.shape
    devices = 2 * members * sides
    bins = pulses // devices
    table = doppler_table(pulses)
    table = table.transpose(2, 1, 0, 3).reshape(devices, bins, 2, 2 * pulses)
    table = table.transpose(0, 2, 1, 3).reshape(2, members, sides * 2 * bins, 2 * pulses)
    block = (sides, elements // 2, 4 * bins, gates)
    anywhere = pl.BlockSpec(memory_space=pl.ANY)
    count = members if apart else 1
    shape = jax.ShapeDtypeStruct(block if apart else (members, *block), jnp.bfloat16)
    return pl.pallas_call(
        functools.partial(spectra_body, apart=apart),
        in_specs=[pl.BlockSpec(memory_space=pltpu.SMEM)] * 2 + [anywhere, anywhere],
        out_specs=[anywhere] * count,
        out_shape=[shape] * count,
        scratch_shapes=[
            pltpu.VMEM(table.shape[1:], jnp.bfloat16),
            pltpu.VMEM(echoes.shape, jnp.bfloat16),
            pltpu.VMEM((members, *block), jnp.bfloat16),
            pltpu.SemaphoreType.DMA(()),
            pltpu.SemaphoreType.DMA((steps,)),
            pltpu.SemaphoreType.DMA((members if apart else steps,)),
        ],
        compiler_params=pltpu.CompilerParams(vmem_limit_bytes=SPECTRA_VMEM),
        name="spectra",
    )(half, place, jnp.asarray(table), echoes)


def spread_body(weight_ref, out_ref, *, bins):
    beams = weight_ref.shape[1]
    elements = weight_ref.shape[2]
    own = out_ref.shape[2]
    group = 128
    width = group * 2 * bins
    lane = lax.broadcasted_iota(jnp.int32, (group, width), 1)
    row = lax.broadcasted_iota(jnp.int32, (group, width), 0)
    repeat = jnp.where(lane // (2 * bins) == row, 1.0, 0.0).astype(jnp.bfloat16)
    col = lax.broadcasted_iota(jnp.int32, (beams, width), 1)
    is_real = (col // bins) % 2 == 0
    for at in range(elements // group):
        span = slice(at * group, (at + 1) * group)
        real = jnp.dot(weight_ref[0, :, span], repeat, preferred_element_type=jnp.float32)
        imag = jnp.dot(weight_ref[1, :, span], repeat, preferred_element_type=jnp.float32)
        to_real = jnp.where(is_real, real, -imag).astype(jnp.bfloat16)
        to_imag = jnp.where(is_real, imag, real).astype(jnp.bfloat16)
        for n in range(width // own):
            out_ref[at * (width // own) + n, :beams] = to_real[:, n * own : (n + 1) * own]
            out_ref[at * (width // own) + n, beams:] = to_imag[:, n * own : (n + 1) * own]


def spread(beam_weights, bins, members):
    _, beams, elements = beam_weights.shape
    return pl.pallas_call(
        functools.partial(spread_body, bins=bins),
        in_specs=whole_vmem(1),
        out_specs=whole_vmem(1)[0],
        out_shape=jax.ShapeDtypeStruct((members, 2 * beams, elements // members * 2 * bins), jnp.bfloat16),
        compiler_params=pltpu.CompilerParams(vmem_limit_bytes=SMALL_VMEM),
        name="spread",
    )(beam_weights)


def beam_sums(blocks, weights, bins):
    received = jnp.concatenate(
        [
            jnp.concatenate([block[j].reshape(-1, block.shape[3]) for block in blocks], axis=0)
            for j in range(blocks[0].shape[0])
        ],
        axis=1,
    )
    weights = jnp.concatenate(weights, axis=1)
    own = lax.broadcasted_iota(jnp.int32, weights.shape, 1) % bins
    return [
        jnp.dot(
            jnp.where(own == d, weights, jnp.zeros_like(weights)),
            received,
            preferred_element_type=jnp.float32,
        )
        for d in range(bins)
    ]


def crossing_body(place_ref, side_ref, spread_ref, *refs):
    *block_refs, same_ref, other_ref = refs
    bins, _, gates = same_ref.shape
    place, first_side = place_ref[0], side_ref[0] == 0
    weights = [spread_ref[place ^ n] for n in range(len(block_refs))]
    for d, value in enumerate(beam_sums([ref[...] for ref in block_refs], weights, bins)):
        first, second = value[:, :gates], value[:, gates:]
        same_ref[d] = jnp.where(first_side, first, second).astype(same_ref.dtype)
        other_ref[d] = jnp.where(first_side, second, first).astype(other_ref.dtype)


def crossing_sums(place, side, blocks, spread_weights, bins):
    shape = jax.ShapeDtypeStruct((bins, spread_weights.shape[1], blocks[0].shape[3]), jnp.bfloat16)
    return pl.pallas_call(
        crossing_body,
        in_specs=[pl.BlockSpec(memory_space=pltpu.SMEM)] * 2 + whole_vmem(1 + len(blocks)),
        out_specs=whole_vmem(2),
        out_shape=[shape, shape],
        compiler_params=pltpu.CompilerParams(vmem_limit_bytes=BEAMS_VMEM),
        name="crossing_sums",
    )(place, side, spread_weights, *blocks)


def split(value):
    high = value.astype(jnp.bfloat16)
    return high, (value - high.astype(jnp.float32)).astype(jnp.bfloat16)


NT = (((1,), (1,)), ((), ()))


def c_mul(a, b):
    return a[0] * b[0] - a[1] * b[1], a[0] * b[1] + a[1] * b[0]
def c_mulc(a, b):
    return a[0] * b[0] + a[1] * b[1], a[1] * b[0] - a[0] * b[1]
def conj(a): return a[0], -a[1]
def c_add(a, b): return a[0] + b[0], a[1] + b[1]
def c_sub(a, b): return a[0] - b[0], a[1] - b[1]
def scale(a, r): return a[0] * r, a[1] * r

def inverse_pair(m):
    a, b, d = m
    r = 1.0 / (a * d - (b[0] * b[0] + b[1] * b[1]))
    return d * r, (-b[0] * r, -b[1] * r), a * r

def inverse_four(e):
    ea, eb, ed = inverse_pair((e[0][0][0], e[0][1], e[1][1][0]))
    f = [[e[0][2], e[0][3]], [e[1][2], e[1][3]]]
    t = [[None, None], [None, None]]
    for l in range(2):
        t[0][l] = c_add(scale(f[0][l], ea), c_mul(eb, f[1][l]))
        t[1][l] = c_add(c_mulc(f[0][l], eb), scale(f[1][l], ed))
    def herm(l, m):
        return c_add(c_mulc(t[0][m], f[0][l]), c_mulc(t[1][m], f[1][l]))
    def herm_re(l):
        return (t[0][l][0]*f[0][l][0] + t[0][l][1]*f[0][l][1]) + (t[1][l][0]*f[1][l][0] + t[1][l][1]*f[1][l][1])
    s = (e[2][2][0] - herm_re(0), c_sub(e[2][3], herm(0, 1)), e[3][3][0] - herm_re(1))
    sa, sb, sd = inverse_pair(s)
    u = [[None, None], [None, None]]
    for j in range(2):
        x = c_add(scale(t[j][0], sa), c_mulc(t[j][1], sb))
        y = c_add(c_mul(t[j][0], sb), scale(t[j][1], sd))
        u[j][0] = (-x[0], -x[1]); u[j][1] = (-y[0], -y[1])
    def corr(j, m):
        return c_add(c_mulc(u[j][0], t[m][0]), c_mulc(u[j][1], t[m][1]))
    zero = jnp.zeros_like(ea)
    p00 = ea - corr(0, 0)[0]; p11 = ed - corr(1, 1)[0]
    p01 = c_sub(eb, corr(0, 1))
    inv = [[None]*4 for _ in range(4)]
    inv[0][0] = (p00, None); inv[1][1] = (p11, None); inv[0][1] = p01
    inv[2][2] = (sa, None); inv[3][3] = (sd, None); inv[2][3] = sb
    for j in range(2):
        for l in range(2): inv[j][2+l] = u[j][l]
    for j in range(4):
        for l in range(j): inv[j][l] = conj(inv[l][j])
    return inv


def turn(x):
    half = x.shape[1] // 2
    lane = lax.broadcasted_iota(jnp.int32, x.shape, 1)
    y = pltpu.roll(x, half, 1)
    return jnp.where(lane < half, -y, y)


def sweep(rows, columns, updated):
    shape = rows[0].shape
    beams = shape[1] // 2
    lane = lax.broadcasted_iota(jnp.int32, shape, 1)
    upper = lax.broadcasted_iota(jnp.int32, shape, 0) < 4

    def col(x, k):
        return jnp.broadcast_to(x[:, k : k + 1], shape)

    for step, k in enumerate(columns):
        inside = ((lane >= k) & (lane < k + 4)) | ((lane >= beams + k) & (lane < beams + k + 4))
        pivot = []
        for q in (2 * step, 2 * step + 1):
            x = rows[q]
            y = pltpu.roll(x, 4, 0)
            pivot += [jnp.where(upper, x, y), jnp.where(upper, y, x)]
        entry = [[None] * 4 for _ in range(4)]
        for j in range(4):
            for l in range(j, 4):
                entry[j][l] = (col(pivot[j], k + l), col(pivot[j], beams + k + l) if l > j else None)
        inv = inverse_four(entry)
        unit = [jnp.where(lane == k + l, 1.0, jnp.where(inside, 0.0, pivot[l])) for l in range(4)]
        turned = [turn(x) for x in unit]
        b, bt = [], []
        for j in range(4):
            acc, tacc = unit[j] * inv[j][j][0], turned[j] * inv[j][j][0]
            for l in range(4):
                if l != j:
                    acc = acc + (unit[l] * inv[j][l][0] + turned[l] * inv[j][l][1])
                    tacc = tacc + (turned[l] * inv[j][l][0] - unit[l] * inv[j][l][1])
            b.append(acc)
            bt.append(tacc)
        for q in updated(step):
            x = rows[q]
            acc = jnp.where(inside, 0.0, x)
            for l in range(4):
                acc = acc - (col(x, k + l) * b[l] + col(x, beams + k + l) * bt[l])
            rows[q] = acc
        for q in (0, 1):
            rows[2 * step + q] = jnp.where(upper, b[2 * q], b[2 * q + 1])
    return rows


def eliminate(systems, sources, rows_ref, size=BLOCK):
    count = len(systems)
    beams = systems[0].shape[0]
    blocks = size // 2
    rest = [
        jnp.concatenate([systems[n], jnp.broadcast_to(sources[n], (8, 2 * beams))], axis=0) for n in range(count)
    ]
    for first in range(0, beams, size):
        base = count * first
        for n in range(count):
            rows_ref[pl.ds(base + n, size, stride=count), :] = rest[n][:size]
        rows = [rows_ref[base + 8 * q : base + 8 * q + 8] for q in range(blocks)]
        columns = range(first, first + size, 4)
        if first + size == beams:
            bottoms = [value[size : size + 1] for value in rest]
            rows.append(jnp.concatenate(bottoms + bottoms, axis=0))
            return sweep(rows, columns, lambda step: range(2 * step + 2, blocks + 1))[blocks]
        rows = sweep(rows, columns, lambda step: [q for q in range(blocks) if q // 2 != step])
        for q in range(blocks):
            rows_ref[base + 8 * q : base + 8 * q + 8] = rows[q]
        at = (lax.broadcasted_iota(jnp.int32, rest[0][size:].shape, 1) - first) % beams
        for n in range(count):
            top = rows_ref[pl.ds(base + n, size, stride=count), :]
            value = rest[n][size:]
            taken = jnp.dot(
                packed_left(value, at, size), packed_right(top, first), preferred_element_type=jnp.float32
            )
            rest[n] = jnp.where(at < size, 0.0, value) - taken


def packed_left(value, at, size):
    high, low = (part.astype(jnp.float32) for part in split(value))
    again = jnp.where(at < 2 * size, pltpu.roll(low, size, 1), pltpu.roll(high, 2 * size, 1))
    return jnp.where(at < size, high, again).astype(jnp.bfloat16)


def packed_right(top, first):
    size, width = top.shape
    count = width // size
    pieces = [jnp.zeros(top.shape, jnp.bfloat16)] * count
    for start, rows in ((first, top), (first + width // 2, turn(top))):
        high, low = split(rows)
        for step, piece in enumerate((high, high, low)):
            pieces[(start // size + step) % count] = piece
    return jnp.concatenate(pieces, axis=0)


def beams_body(
    side_ref, spectra_ref, spread_ref, same_ref, other_ref, pulse_ref, steer_ref, own_ref, send_ref, rows_ref
):
    bins, total, half = same_ref.shape
    beams = total // 2
    ranges = spectra_ref.shape[1]
    gates = ranges * half
    first_side = side_ref[0] == 0
    members = range(spectra_ref.shape[0])
    near = beam_sums([spectra_ref[n] for n in members], [spread_ref[n] for n in members], bins)
    sums = []
    for d in range(bins):
        same, other = same_ref[d].astype(jnp.float32), other_ref[d].astype(jnp.float32)
        far = [jnp.where(first_side, same, other), jnp.where(first_side, other, same)]
        sums.append(near[d] + jnp.concatenate(far, axis=1))
    high, low = split(
        jnp.concatenate(
            [
                jnp.concatenate(
                    [
                        value[part * beams : (part + 1) * beams, block * half : (block + 1) * half]
                        for block in range(ranges)
                        for part in range(2)
                    ],
                    axis=1,
                )
                for value in sums
            ],
            axis=0,
        )
    )
    formed = [0.0] * ranges
    for block in range(ranges):
        into = slice(block * 2 * half, (block + 1) * 2 * half)
        pulse = pulse_ref[block * 2 * half :, into]
        for piece in (high, low):
            formed[block] = formed[block] + jnp.dot(
                piece[:, block * 2 * half :], pulse, preferred_element_type=jnp.float32
            )
    sub = lax.broadcasted_iota(jnp.int32, (beams, 2 * beams), 0)
    lane = lax.broadcasted_iota(jnp.int32, (beams, 2 * beams), 1)
    both, systems = [], []
    for d in range(bins):
        mine = slice(d * beams, (d + 1) * beams)
        real = jnp.concatenate([value[mine, :half] for value in formed], axis=1)
        imag = jnp.concatenate([value[mine, half:] for value in formed], axis=1)
        top = jnp.concatenate([real, imag], axis=1)
        t_high, t_low = split(top)
        u_high, u_low = split(jnp.concatenate([-imag, real], axis=1))
        left = jnp.concatenate([t_high, t_low], axis=0)
        both.append(left)
        products = lax.dot_general(
            left, jnp.concatenate([t_high, u_high, t_low, u_low], axis=0), NT, preferred_element_type=jnp.float32
        )
        cov = (
            products[:beams, : 2 * beams] + products[:beams, 2 * beams :] + products[beams:, : 2 * beams]
        )
        cov = cov * (1.0 / gates)
        on_diagonal = sub == lane
        trace = jnp.sum(jnp.where(on_diagonal, cov, 0.0), axis=(0, 1), keepdims=True)
        loading = load_ratio * trace / beams + epsilon
        cov = jnp.where(on_diagonal, cov + loading, cov) * (1.0 / loading)
        systems.append(cov)
    steer = steer_ref[...]
    sources = [steer[d : d + 1] for d in range(bins)]
    conj = -eliminate(systems, sources, rows_ref)[:bins]
    response = jnp.sum(conj * steer, axis=1, keepdims=True)
    weight = conj / response
    part_of = lax.broadcasted_iota(jnp.int32, weight.shape, 1) < beams
    other = pltpu.roll(weight, beams, 1)
    pieces = []
    for twice in (jnp.where(part_of, weight, other), jnp.where(part_of, other, weight)):
        w_high, w_low = split(twice)
        pieces += [w_high, jnp.where(part_of, w_low, jnp.zeros_like(w_low))]
    left = jnp.concatenate(pieces, axis=0)
    row = lax.broadcasted_iota(jnp.int32, (bins, 2 * gates), 0)
    by_real = by_imag = jnp.zeros((bins, 2 * gates), jnp.float32)
    for d in range(bins):
        out = jnp.dot(left, both[d], preferred_element_type=jnp.float32)
        by_real = jnp.where(row == d, out[:bins] + out[bins : 2 * bins], by_real)
        by_imag = jnp.where(row == d, out[2 * bins : 3 * bins] + out[3 * bins :], by_imag)
    joined = (
        by_real[:, :gates] - by_imag[:, gates:],
        by_real[:, gates:] + by_imag[:, :gates],
    )
    nothing = jnp.zeros((bins, half), jnp.float32)
    for part in range(2):
        first, second = joined[part][:, :half], joined[part][:, half:]
        own_ref[part] = jnp.concatenate(
            [jnp.where(first_side, first, nothing), jnp.where(first_side, nothing, second)], axis=0
        )
        send_ref[part] = jnp.concatenate(
            [jnp.where(first_side, second, nothing), jnp.where(first_side, nothing, first)], axis=0
        )


def on_device_owned(echoes, replica, beam_weights, steering):
    elems, ranges = lax.axis_size("elem"), lax.axis_size("range")
    devices = elems * ranges
    _, own_elements, pulses, gate_count = echoes.shape
    bins = pulses // devices
    elements = beam_weights.shape[2]
    gates = gate_count * ranges
    side = lax.axis_index("range")
    half = lax.axis_index("elem") // (elems // 2)
    group = devices // 2
    members = elems // 2
    place, far_half, near_half, seat = (
        value.reshape(1).astype(jnp.int32)
        for value in (lax.axis_index("elem") % members, 1 - half, half, side)
    )
    here = lax.dynamic_slice_in_dim(beam_weights, half * (elements // 2), elements // 2, 2)
    spread_weights = spread(here, bins, members)
    blocks = spectra(far_half, place, echoes, members, ranges, True)
    blocks = [blocks[0]] + [
        lax.ppermute(blocks[n], "elem", [(m, m ^ n) for m in range(elems)]) for n in range(1, members)
    ]
    (sent,) = spectra(near_half, place, echoes, members, ranges, False)
    sent, *blocks[1:] = lax.optimization_barrier((sent, *blocks[1:]))
    same, other = crossing_sums(place, seat, blocks, spread_weights, bins)
    across = [(n + group) % devices for n in range(devices)]
    same = lax.ppermute(same, ("elem", "range"), list(enumerate(across)))
    other = lax.ppermute(other, ("elem", "range"), [(n, to ^ 1) for n, to in enumerate(across)])
    near = lax.all_to_all(
        sent.reshape(group, *sent.shape[2:]),
        ("elem", "range"),
        0,
        0,
        tiled=True,
        axis_index_groups=[list(range(group)), list(range(group, devices))],
    )
    near = near.reshape(members, ranges, own_elements // 2, 4 * bins, gate_count)
    pulse = pulse_kernel(replica, gates)[:, :, :gates]
    pulse = pulse.reshape(2, 2, ranges, gate_count, ranges, gate_count)
    pulse = pulse.transpose(2, 0, 3, 4, 1, 5).reshape(2 * gates, 2 * gates)
    own_steering = lax.dynamic_slice_in_dim(steering, side * bins, bins, 1)
    steer_row = jnp.concatenate([own_steering[0], -own_steering[1]], axis=1)
    shape = jax.ShapeDtypeStruct((2, 2 * bins, gate_count), jnp.float32)
    own, send = pl.pallas_call(
        beams_body,
        in_specs=[pl.BlockSpec(memory_space=pltpu.SMEM)] + whole_vmem(6),
        out_specs=whole_vmem(2),
        out_shape=[shape, shape],
        scratch_shapes=[pltpu.VMEM((bins * beam_weights.shape[1], 2 * beam_weights.shape[1]), jnp.float32)],
        compiler_params=pltpu.CompilerParams(vmem_limit_bytes=BEAMS_VMEM),
        name="beams",
    )(seat, near, spread_weights, same, other, pulse, steer_row)
    return own + lax.ppermute(send, "range", [(0, 1), (1, 0)])


def on_device(echoes, replica, beam_weights, steering):
    elems, ranges = lax.axis_size("elem"), lax.axis_size("range")
    pulses, gate_count = echoes.shape[2:]
    beams, elements = beam_weights.shape[1:]
    owned = (
        ranges == 2
        and pulses == 4 * elems * ranges
        and gate_count % 128 == 0
        and beams == 64
        and elems % 2 == 0
        and elems & (elems - 1) == 0
        and 128 % echoes.shape[1] == 0
        and elements % 256 == 0
        and echoes.shape[1] % 8 == 0
        and replica.shape[1] <= gate_count
    )
    run = on_device_owned if owned else on_device_general
    return run(echoes, replica, beam_weights, steering)


def solution(mesh):
    return jax.shard_map(
        on_device,
        mesh=mesh,
        in_specs=(P(None, "elem", None, "range"), P(), P(), P(None, "elem", None)),
        out_specs=P(None, "elem", "range"),
        check_vma=False,
    )
```

```python
import functools

import jax
import jax.numpy as jnp
import numpy as np
from jax import lax
from jax.experimental import pallas as pl
from jax.experimental.pallas import tpu as pltpu
from jax.sharding import PartitionSpec as P

load_ratio = 0.1
epsilon = 1e-06
SPECTRA_VMEM = 56 << 20
STEPS = 2
BLOCK = 16
SMALL_VMEM = 14 << 20
BEAMS_VMEM = 24 << 20


def shifted(value, axis, steps):
    count = lax.axis_size(axis)
    first, last = (max(0, -steps), min(count, count - steps))
    return lax.ppermute(value, axis, [(source, source + steps) for source in range(first, last)])


def correlation_matrix(tap_values, gate_count):
    tap_count = tap_values.shape[0]
    span_width = gate_count + tap_count - 1
    padded_taps = jnp.concatenate(
        [tap_values, jnp.zeros((span_width + 1 - tap_count,), tap_values.dtype)]
    )
    tiled_rows = jnp.tile(padded_taps, gate_count)[: gate_count * span_width].reshape(
        gate_count, span_width
    )
    return tiled_rows.T


def pulse_kernel(replica, gate_count):
    real_part = correlation_matrix(replica[0], gate_count)
    imag_part = correlation_matrix(replica[1], gate_count)
    return jnp.stack([jnp.stack([real_part, imag_part]), jnp.stack([-imag_part, real_part])])


def doppler_table(pulses):
    index = np.arange(pulses, dtype=np.int64)
    phase_index = (index[:, None] * index[None, :]) % pulses
    phase_angle = np.float32(2.0 * np.pi) * phase_index.astype(np.float32) / np.float32(pulses)
    scale = np.float32(1.0) / np.sqrt(np.float32(pulses))
    cosine = np.cos(phase_angle) * scale
    sine = np.sin(phase_angle) * scale
    table = np.stack([np.stack([cosine, -sine]), np.stack([sine, cosine])])
    return table.astype(jnp.bfloat16)


def beam_kernel(beam_weights):
    weight_re = beam_weights[0]
    weight_im = beam_weights[1]
    return jnp.stack([jnp.stack([weight_re, weight_im]), jnp.stack([-weight_im, weight_re])])


def adapt(gram_sum, steering, formed):
    beams = formed.shape[2]
    cov_re = gram_sum[:, :beams, :beams] + gram_sum[:, beams:, beams:]
    cov_im = gram_sum[:, beams:, :beams] - gram_sum[:, :beams, beams:]
    loading = load_ratio * jnp.trace(cov_re, axis1=1, axis2=2) / beams + epsilon
    upper = jnp.concatenate([cov_re, -cov_im], axis=2)
    lower = jnp.concatenate([cov_im, cov_re], axis=2)
    system = jnp.concatenate([upper, lower], axis=1)
    system = system + loading[:, None, None] * jnp.eye(2 * beams, dtype=jnp.float32)[None]
    factor = jnp.linalg.cholesky(system)
    right_side = jnp.concatenate([steering[0], steering[1]], axis=-1)
    solved = jax.scipy.linalg.cho_solve((factor, True), right_side[..., None])[..., 0]
    response = jnp.sum(right_side * solved, axis=-1)
    weights = solved / response[:, None]
    weight_re = weights[:, :beams]
    weight_im = weights[:, beams:]
    beam_re = formed[:, 0].astype(jnp.float32)
    beam_im = formed[:, 1].astype(jnp.float32)
    high = lax.Precision.HIGHEST
    out_re = jnp.einsum("db,dbr->dr", weight_re, beam_re, precision=high) + jnp.einsum(
        "db,dbr->dr", weight_im, beam_im, precision=high
    )
    out_im = jnp.einsum("db,dbr->dr", weight_re, beam_im, precision=high) - jnp.einsum(
        "db,dbr->dr", weight_im, beam_re, precision=high
    )
    return jnp.stack([out_re, out_im])


def on_device_general(echoes, replica, beam_weights, steering):
    pulses = echoes.shape[2]
    gate_count = echoes.shape[3]
    tap_count = replica.shape[1]
    following = shifted(echoes[:, :, :, : tap_count - 1], "range", -1)
    padded = jnp.concatenate([echoes, following], axis=3)
    compressed = jnp.einsum(
        "cepj,cojr->oepr",
        padded,
        pulse_kernel(replica, gate_count),
        preferred_element_type=jnp.float32,
    ).astype(jnp.bfloat16)
    doppler = jnp.einsum(
        "cepr,codp->oedr",
        compressed,
        jnp.asarray(doppler_table(pulses)),
        preferred_element_type=jnp.float32,
    ).astype(jnp.bfloat16)
    kernel_full = beam_kernel(beam_weights)
    own_bins = pulses // lax.axis_size("elem")
    beam_sums = jnp.einsum(
        "cedr,cobe->dobr",
        lax.all_to_all(doppler, "elem", split_axis=2, concat_axis=1, tiled=True),
        kernel_full,
        preferred_element_type=jnp.float32,
    )
    formed = beam_sums.astype(jnp.bfloat16)
    beams = formed.shape[2]
    stacked = formed.reshape(own_bins, 2 * beams, gate_count)
    partial_gram = jnp.einsum("dbr,dcr->dbc", stacked, stacked, preferred_element_type=jnp.float32)
    gram_sum = lax.psum(partial_gram, "range") / (gate_count * lax.axis_size("range"))
    return adapt(gram_sum, steering, formed)


def whole_vmem(count):
    return [pl.BlockSpec(memory_space=pltpu.VMEM)] * count


def far_first(members):
    return [0] + sorted(range(1, members), key=lambda n: (-(n >> 1).bit_count(), n))


def spectra_body(half_ref, place_ref, table_hbm, echo_hbm, *refs, apart):
    *out_hbm, table_ref, echo_ref, out_ref, table_sem, in_sem, out_sem = refs
    members = table_ref.shape[0]
    gates = echo_ref.shape[3]
    steps = in_sem.shape[0]
    block = echo_ref.shape[1] // steps
    pairs = block // 2
    fetch_table = pltpu.make_async_copy(table_hbm.at[half_ref[0]], table_ref, table_sem)
    fetches = [
        pltpu.make_async_copy(
            echo_hbm.at[:, pl.ds(step * block, block)],
            echo_ref.at[:, pl.ds(step * block, block)],
            in_sem.at[step],
        )
        for step in range(steps)
    ]
    if apart:
        stores = [
            pltpu.make_async_copy(out_ref.at[n], out_hbm[n], out_sem.at[n]) for n in range(members)
        ]
    else:
        stores = [
            pltpu.make_async_copy(
                out_ref.at[:, :, pl.ds(step * pairs, pairs)],
                out_hbm[0].at[:, :, pl.ds(step * pairs, pairs)],
                out_sem.at[step],
            )
            for step in range(steps)
        ]
    fetch_table.start()
    for fetch in fetches:
        fetch.start()
    fetch_table.wait()
    place = place_ref[0]
    table = jnp.concatenate([table_ref[place ^ n if apart else n] for n in (far_first(members) if apart else range(members))], axis=0)
    sides = out_ref.shape[1]
    for step in range(steps):
        fetches[step].wait()
        for pair in range(step * pairs, (step + 1) * pairs):
            even, odd = 2 * pair, 2 * pair + 1
            samples = jnp.concatenate(
                [
                    jnp.concatenate([echo_ref[0, even], echo_ref[0, odd]], axis=1),
                    jnp.concatenate([echo_ref[1, even], echo_ref[1, odd]], axis=1),
                ],
                axis=0,
            )
            bins = jnp.dot(table, samples, preferred_element_type=jnp.float32)
            bins = bins.reshape(members, sides, bins.shape[0] // (members * sides), 2 * gates)
            rows = jnp.concatenate([bins[..., :gates], bins[..., gates:]], axis=2)
            out_ref[:, :, pair] = rows.astype(jnp.bfloat16)
        if not apart:
            stores[step].start()
    if apart:
        for store in stores:
            store.start()
    for store in stores:
        store.wait()


def spectra(half, place, echoes, members, sides, apart, steps=STEPS):
    _, elements, pulses, gates = echoes.shape
    devices = 2 * members * sides
    bins = pulses // devices
    table = doppler_table(pulses)
    table = table.transpose(2, 1, 0, 3).reshape(devices, bins, 2, 2 * pulses)
    table = table.transpose(0, 2, 1, 3).reshape(2, members, sides * 2 * bins, 2 * pulses)
    block = (sides, elements // 2, 4 * bins, gates)
    anywhere = pl.BlockSpec(memory_space=pl.ANY)
    count = members if apart else 1
    shape = jax.ShapeDtypeStruct(block if apart else (members, *block), jnp.bfloat16)
    return pl.pallas_call(
        functools.partial(spectra_body, apart=apart),
        in_specs=[pl.BlockSpec(memory_space=pltpu.SMEM)] * 2 + [anywhere, anywhere],
        out_specs=[anywhere] * count,
        out_shape=[shape] * count,
        scratch_shapes=[
            pltpu.VMEM(table.shape[1:], jnp.bfloat16),
            pltpu.VMEM(echoes.shape, jnp.bfloat16),
            pltpu.VMEM((members, *block), jnp.bfloat16),
            pltpu.SemaphoreType.DMA(()),
            pltpu.SemaphoreType.DMA((steps,)),
            pltpu.SemaphoreType.DMA((members if apart else steps,)),
        ],
        compiler_params=pltpu.CompilerParams(vmem_limit_bytes=SPECTRA_VMEM),
        name="spectra",
    )(half, place, jnp.asarray(table), echoes)


def spread_body(weight_ref, out_ref, *, bins):
    beams = weight_ref.shape[1]
    elements = weight_ref.shape[2]
    own = out_ref.shape[2]
    group = 128
    width = group * 2 * bins
    lane = lax.broadcasted_iota(jnp.int32, (group, width), 1)
    row = lax.broadcasted_iota(jnp.int32, (group, width), 0)
    repeat = jnp.where(lane // (2 * bins) == row, 1.0, 0.0).astype(jnp.bfloat16)
    col = lax.broadcasted_iota(jnp.int32, (beams, width), 1)
    is_real = (col // bins) % 2 == 0
    for at in range(elements // group):
        span = slice(at * group, (at + 1) * group)
        real = jnp.dot(weight_ref[0, :, span], repeat, preferred_element_type=jnp.float32)
        imag = jnp.dot(weight_ref[1, :, span], repeat, preferred_element_type=jnp.float32)
        to_real = jnp.where(is_real, real, -imag).astype(jnp.bfloat16)
        to_imag = jnp.where(is_real, imag, real).astype(jnp.bfloat16)
        for n in range(width // own):
            out_ref[at * (width // own) + n, :beams] = to_real[:, n * own : (n + 1) * own]
            out_ref[at * (width // own) + n, beams:] = to_imag[:, n * own : (n + 1) * own]


def spread(beam_weights, bins, members):
    _, beams, elements = beam_weights.shape
    return pl.pallas_call(
        functools.partial(spread_body, bins=bins),
        in_specs=whole_vmem(1),
        out_specs=whole_vmem(1)[0],
        out_shape=jax.ShapeDtypeStruct((members, 2 * beams, elements // members * 2 * bins), jnp.bfloat16),
        compiler_params=pltpu.CompilerParams(vmem_limit_bytes=SMALL_VMEM),
        name="spread",
    )(beam_weights)


def beam_sums(blocks, weights, bins):
    received = jnp.concatenate(
        [
            jnp.concatenate([block[j].reshape(-1, block.shape[3]) for block in blocks], axis=0)
            for j in range(blocks[0].shape[0])
        ],
        axis=1,
    )
    weights = jnp.concatenate(weights, axis=1)
    own = lax.broadcasted_iota(jnp.int32, weights.shape, 1) % bins
    return [
        jnp.dot(
            jnp.where(own == d, weights, jnp.zeros_like(weights)),
            received,
            preferred_element_type=jnp.float32,
        )
        for d in range(bins)
    ]


def crossing_body(place_ref, side_ref, spread_ref, *refs):
    *block_refs, same_ref, other_ref = refs
    bins, _, gates = same_ref.shape
    place, first_side = place_ref[0], side_ref[0] == 0
    weights = [spread_ref[place ^ n] for n in far_first(len(block_refs))]
    for d, value in enumerate(beam_sums([ref[...] for ref in block_refs], weights, bins)):
        first, second = value[:, :gates], value[:, gates:]
        same_ref[d] = jnp.where(first_side, first, second).astype(same_ref.dtype)
        other_ref[d] = jnp.where(first_side, second, first).astype(other_ref.dtype)


def crossing_sums(place, side, blocks, spread_weights, bins):
    shape = jax.ShapeDtypeStruct((bins, spread_weights.shape[1], blocks[0].shape[3]), jnp.bfloat16)
    return pl.pallas_call(
        crossing_body,
        in_specs=[pl.BlockSpec(memory_space=pltpu.SMEM)] * 2 + whole_vmem(1 + len(blocks)),
        out_specs=whole_vmem(2),
        out_shape=[shape, shape],
        compiler_params=pltpu.CompilerParams(vmem_limit_bytes=BEAMS_VMEM),
        name="crossing_sums",
    )(place, side, spread_weights, *blocks)


def split(value):
    high = value.astype(jnp.bfloat16)
    return high, (value - high.astype(jnp.float32)).astype(jnp.bfloat16)


NT = (((1,), (1,)), ((), ()))


def c_mul(a, b):
    return a[0] * b[0] - a[1] * b[1], a[0] * b[1] + a[1] * b[0]
def c_mulc(a, b):
    return a[0] * b[0] + a[1] * b[1], a[1] * b[0] - a[0] * b[1]
def conj(a): return a[0], -a[1]
def c_add(a, b): return a[0] + b[0], a[1] + b[1]
def c_sub(a, b): return a[0] - b[0], a[1] - b[1]
def scale(a, r): return a[0] * r, a[1] * r

def inverse_pair(m):
    a, b, d = m
    r = 1.0 / (a * d - (b[0] * b[0] + b[1] * b[1]))
    return d * r, (-b[0] * r, -b[1] * r), a * r

def inverse_four(e):
    ea, eb, ed = inverse_pair((e[0][0][0], e[0][1], e[1][1][0]))
    f = [[e[0][2], e[0][3]], [e[1][2], e[1][3]]]
    t = [[None, None], [None, None]]
    for l in range(2):
        t[0][l] = c_add(scale(f[0][l], ea), c_mul(eb, f[1][l]))
        t[1][l] = c_add(c_mulc(f[0][l], eb), scale(f[1][l], ed))
    def herm(l, m):
        return c_add(c_mulc(t[0][m], f[0][l]), c_mulc(t[1][m], f[1][l]))
    def herm_re(l):
        return (t[0][l][0]*f[0][l][0] + t[0][l][1]*f[0][l][1]) + (t[1][l][0]*f[1][l][0] + t[1][l][1]*f[1][l][1])
    s = (e[2][2][0] - herm_re(0), c_sub(e[2][3], herm(0, 1)), e[3][3][0] - herm_re(1))
    sa, sb, sd = inverse_pair(s)
    u = [[None, None], [None, None]]
    for j in range(2):
        x = c_add(scale(t[j][0], sa), c_mulc(t[j][1], sb))
        y = c_add(c_mul(t[j][0], sb), scale(t[j][1], sd))
        u[j][0] = (-x[0], -x[1]); u[j][1] = (-y[0], -y[1])
    def corr(j, m):
        return c_add(c_mulc(u[j][0], t[m][0]), c_mulc(u[j][1], t[m][1]))
    zero = jnp.zeros_like(ea)
    p00 = ea - corr(0, 0)[0]; p11 = ed - corr(1, 1)[0]
    p01 = c_sub(eb, corr(0, 1))
    inv = [[None]*4 for _ in range(4)]
    inv[0][0] = (p00, None); inv[1][1] = (p11, None); inv[0][1] = p01
    inv[2][2] = (sa, None); inv[3][3] = (sd, None); inv[2][3] = sb
    for j in range(2):
        for l in range(2): inv[j][2+l] = u[j][l]
    for j in range(4):
        for l in range(j): inv[j][l] = conj(inv[l][j])
    return inv


def turn(x):
    half = x.shape[1] // 2
    lane = lax.broadcasted_iota(jnp.int32, x.shape, 1)
    y = pltpu.roll(x, half, 1)
    return jnp.where(lane < half, -y, y)


def sweep(rows, columns, updated):
    shape = rows[0].shape
    beams = shape[1] // 2
    lane = lax.broadcasted_iota(jnp.int32, shape, 1)
    upper = lax.broadcasted_iota(jnp.int32, shape, 0) < 4

    def col(x, k):
        return jnp.broadcast_to(x[:, k : k + 1], shape)

    for step, k in enumerate(columns):
        inside = ((lane >= k) & (lane < k + 4)) | ((lane >= beams + k) & (lane < beams + k + 4))
        pivot = []
        for q in (2 * step, 2 * step + 1):
            x = rows[q]
            y = pltpu.roll(x, 4, 0)
            pivot += [jnp.where(upper, x, y), jnp.where(upper, y, x)]
        entry = [[None] * 4 for _ in range(4)]
        for j in range(4):
            for l in range(j, 4):
                entry[j][l] = (col(pivot[j], k + l), col(pivot[j], beams + k + l) if l > j else None)
        inv = inverse_four(entry)
        unit = [jnp.where(lane == k + l, 1.0, jnp.where(inside, 0.0, pivot[l])) for l in range(4)]
        turned = [turn(x) for x in unit]
        b, bt = [], []
        for j in range(4):
            acc, tacc = unit[j] * inv[j][j][0], turned[j] * inv[j][j][0]
            for l in range(4):
                if l != j:
                    acc = acc + (unit[l] * inv[j][l][0] + turned[l] * inv[j][l][1])
                    tacc = tacc + (turned[l] * inv[j][l][0] - unit[l] * inv[j][l][1])
            b.append(acc)
            bt.append(tacc)
        for q in updated(step):
            x = rows[q]
            acc = jnp.where(inside, 0.0, x)
            for l in range(4):
                acc = acc - (col(x, k + l) * b[l] + col(x, beams + k + l) * bt[l])
            rows[q] = acc
        for q in (0, 1):
            rows[2 * step + q] = jnp.where(upper, b[2 * q], b[2 * q + 1])
    return rows


def eliminate(systems, sources, rows_ref, size=BLOCK):
    count = len(systems)
    beams = systems[0].shape[0]
    blocks = size // 2
    rest = [
        jnp.concatenate([systems[n], jnp.broadcast_to(sources[n], (8, 2 * beams))], axis=0) for n in range(count)
    ]
    for first in range(0, beams, size):
        base = count * first
        for n in range(count):
            rows_ref[pl.ds(base + n, size, stride=count), :] = rest[n][:size]
        rows = [rows_ref[base + 8 * q : base + 8 * q + 8] for q in range(blocks)]
        columns = range(first, first + size, 4)
        if first + size == beams:
            bottoms = [value[size : size + 1] for value in rest]
            rows.append(jnp.concatenate(bottoms + bottoms, axis=0))
            return sweep(rows, columns, lambda step: range(2 * step + 2, blocks + 1))[blocks]
        rows = sweep(rows, columns, lambda step: [q for q in range(blocks) if q // 2 != step])
        for q in range(blocks):
            rows_ref[base + 8 * q : base + 8 * q + 8] = rows[q]
        at = (lax.broadcasted_iota(jnp.int32, rest[0][size:].shape, 1) - first) % beams
        for n in range(count):
            top = rows_ref[pl.ds(base + n, size, stride=count), :]
            value = rest[n][size:]
            taken = jnp.dot(
                packed_left(value, at, size), packed_right(top, first), preferred_element_type=jnp.float32
            )
            rest[n] = jnp.where(at < size, 0.0, value) - taken


def packed_left(value, at, size):
    high, low = (part.astype(jnp.float32) for part in split(value))
    again = jnp.where(at < 2 * size, pltpu.roll(low, size, 1), pltpu.roll(high, 2 * size, 1))
    return jnp.where(at < size, high, again).astype(jnp.bfloat16)


def packed_right(top, first):
    size, width = top.shape
    count = width // size
    pieces = [jnp.zeros(top.shape, jnp.bfloat16)] * count
    for start, rows in ((first, top), (first + width // 2, turn(top))):
        high, low = split(rows)
        for step, piece in enumerate((high, high, low)):
            pieces[(start // size + step) % count] = piece
    return jnp.concatenate(pieces, axis=0)


def beams_body(
    side_ref, spectra_ref, spread_ref, same_ref, other_ref, pulse_ref, steer_ref, own_ref, send_ref, rows_ref
):
    bins, total, half = same_ref.shape
    beams = total // 2
    ranges = spectra_ref.shape[1]
    gates = ranges * half
    first_side = side_ref[0] == 0
    members = range(spectra_ref.shape[0])
    near = beam_sums([spectra_ref[n] for n in members], [spread_ref[n] for n in members], bins)
    sums = []
    for d in range(bins):
        same, other = same_ref[d].astype(jnp.float32), other_ref[d].astype(jnp.float32)
        far = [jnp.where(first_side, same, other), jnp.where(first_side, other, same)]
        sums.append(near[d] + jnp.concatenate(far, axis=1))
    high, low = split(
        jnp.concatenate(
            [
                jnp.concatenate(
                    [
                        value[part * beams : (part + 1) * beams, block * half : (block + 1) * half]
                        for block in range(ranges)
                        for part in range(2)
                    ],
                    axis=1,
                )
                for value in sums
            ],
            axis=0,
        )
    )
    formed = [0.0] * ranges
    for block in range(ranges):
        into = slice(block * 2 * half, (block + 1) * 2 * half)
        pulse = pulse_ref[block * 2 * half :, into]
        for piece in (high, low):
            formed[block] = formed[block] + jnp.dot(
                piece[:, block * 2 * half :], pulse, preferred_element_type=jnp.float32
            )
    sub = lax.broadcasted_iota(jnp.int32, (beams, 2 * beams), 0)
    lane = lax.broadcasted_iota(jnp.int32, (beams, 2 * beams), 1)
    both, systems = [], []
    for d in range(bins):
        mine = slice(d * beams, (d + 1) * beams)
        real = jnp.concatenate([value[mine, :half] for value in formed], axis=1)
        imag = jnp.concatenate([value[mine, half:] for value in formed], axis=1)
        top = jnp.concatenate([real, imag], axis=1)
        t_high, t_low = split(top)
        u_high, u_low = split(jnp.concatenate([-imag, real], axis=1))
        left = jnp.concatenate([t_high, t_low], axis=0)
        both.append(left)
        products = lax.dot_general(
            left, jnp.concatenate([t_high, u_high, t_low, u_low], axis=0), NT, preferred_element_type=jnp.float32
        )
        cov = (
            products[:beams, : 2 * beams] + products[:beams, 2 * beams :] + products[beams:, : 2 * beams]
        )
        cov = cov * (1.0 / gates)
        on_diagonal = sub == lane
        trace = jnp.sum(jnp.where(on_diagonal, cov, 0.0), axis=(0, 1), keepdims=True)
        loading = load_ratio * trace / beams + epsilon
        cov = jnp.where(on_diagonal, cov + loading, cov) * (1.0 / loading)
        systems.append(cov)
    steer = steer_ref[...]
    sources = [steer[d : d + 1] for d in range(bins)]
    conj = -eliminate(systems, sources, rows_ref)[:bins]
    response = jnp.sum(conj * steer, axis=1, keepdims=True)
    weight = conj / response
    part_of = lax.broadcasted_iota(jnp.int32, weight.shape, 1) < beams
    other = pltpu.roll(weight, beams, 1)
    pieces = []
    for twice in (jnp.where(part_of, weight, other), jnp.where(part_of, other, weight)):
        w_high, w_low = split(twice)
        pieces += [w_high, jnp.where(part_of, w_low, jnp.zeros_like(w_low))]
    left = jnp.concatenate(pieces, axis=0)
    row = lax.broadcasted_iota(jnp.int32, (bins, 2 * gates), 0)
    by_real = by_imag = jnp.zeros((bins, 2 * gates), jnp.float32)
    for d in range(bins):
        out = jnp.dot(left, both[d], preferred_element_type=jnp.float32)
        by_real = jnp.where(row == d, out[:bins] + out[bins : 2 * bins], by_real)
        by_imag = jnp.where(row == d, out[2 * bins : 3 * bins] + out[3 * bins :], by_imag)
    joined = (
        by_real[:, :gates] - by_imag[:, gates:],
        by_real[:, gates:] + by_imag[:, :gates],
    )
    nothing = jnp.zeros((bins, half), jnp.float32)
    for part in range(2):
        first, second = joined[part][:, :half], joined[part][:, half:]
        own_ref[part] = jnp.concatenate(
            [jnp.where(first_side, first, nothing), jnp.where(first_side, nothing, second)], axis=0
        )
        send_ref[part] = jnp.concatenate(
            [jnp.where(first_side, second, nothing), jnp.where(first_side, nothing, first)], axis=0
        )


def on_device_owned(echoes, replica, beam_weights, steering):
    elems, ranges = lax.axis_size("elem"), lax.axis_size("range")
    devices = elems * ranges
    _, own_elements, pulses, gate_count = echoes.shape
    bins = pulses // devices
    elements = beam_weights.shape[2]
    gates = gate_count * ranges
    side = lax.axis_index("range")
    half = lax.axis_index("elem") // (elems // 2)
    group = devices // 2
    members = elems // 2
    place, far_half, near_half, seat = (
        value.reshape(1).astype(jnp.int32)
        for value in (lax.axis_index("elem") % members, 1 - half, half, side)
    )
    here = lax.dynamic_slice_in_dim(beam_weights, half * (elements // 2), elements // 2, 2)
    spread_weights = spread(here, bins, members)
    blocks = spectra(far_half, place, echoes, members, ranges, True)
    blocks = [
        block if n == 0 else lax.ppermute(block, "elem", [(m, m ^ n) for m in range(elems)])
        for n, block in zip(far_first(members), blocks)
    ]
    (sent,) = spectra(near_half, place, echoes, members, ranges, False)
    sent, *blocks[1:] = lax.optimization_barrier((sent, *blocks[1:]))
    same, other = crossing_sums(place, seat, blocks, spread_weights, bins)
    across = [(n + group) % devices for n in range(devices)]
    same = lax.ppermute(same, ("elem", "range"), list(enumerate(across)))
    other = lax.ppermute(other, ("elem", "range"), [(n, to ^ 1) for n, to in enumerate(across)])
    near = lax.all_to_all(
        sent.reshape(group, *sent.shape[2:]),
        ("elem", "range"),
        0,
        0,
        tiled=True,
        axis_index_groups=[list(range(group)), list(range(group, devices))],
    )
    near = near.reshape(members, ranges, own_elements // 2, 4 * bins, gate_count)
    pulse = pulse_kernel(replica, gates)[:, :, :gates]
    pulse = pulse.reshape(2, 2, ranges, gate_count, ranges, gate_count)
    pulse = pulse.transpose(2, 0, 3, 4, 1, 5).reshape(2 * gates, 2 * gates)
    own_steering = lax.dynamic_slice_in_dim(steering, side * bins, bins, 1)
    steer_row = jnp.concatenate([own_steering[0], -own_steering[1]], axis=1)
    shape = jax.ShapeDtypeStruct((2, 2 * bins, gate_count), jnp.float32)
    own, send = pl.pallas_call(
        beams_body,
        in_specs=[pl.BlockSpec(memory_space=pltpu.SMEM)] + whole_vmem(6),
        out_specs=whole_vmem(2),
        out_shape=[shape, shape],
        scratch_shapes=[pltpu.VMEM((bins * beam_weights.shape[1], 2 * beam_weights.shape[1]), jnp.float32)],
        compiler_params=pltpu.CompilerParams(vmem_limit_bytes=BEAMS_VMEM),
        name="beams",
    )(seat, near, spread_weights, same, other, pulse, steer_row)
    return own + lax.ppermute(send, "range", [(0, 1), (1, 0)])


def on_device(echoes, replica, beam_weights, steering):
    elems, ranges = lax.axis_size("elem"), lax.axis_size("range")
    pulses, gate_count = echoes.shape[2:]
    beams, elements = beam_weights.shape[1:]
    owned = (
        ranges == 2
        and pulses == 4 * elems * ranges
        and gate_count % 128 == 0
        and beams == 64
        and elems % 2 == 0
        and elems & (elems - 1) == 0
        and 128 % echoes.shape[1] == 0
        and elements % 256 == 0
        and echoes.shape[1] % 8 == 0
        and replica.shape[1] <= gate_count
    )
    run = on_device_owned if owned else on_device_general
    return run(echoes, replica, beam_weights, steering)


def solution(mesh):
    return jax.shard_map(
        on_device,
        mesh=mesh,
        in_specs=(P(None, "elem", None, "range"), P(), P(), P(None, "elem", None)),
        out_specs=P(None, "elem", "range"),
        check_vma=False,
    )
```

```python
import functools

import jax
import jax.numpy as jnp
import numpy as np
from jax import lax
from jax.experimental import pallas as pl
from jax.experimental.pallas import tpu as pltpu
from jax.sharding import PartitionSpec as P

load_ratio = 0.1
epsilon = 1e-06
SPECTRA_VMEM = 56 << 20
STEPS = 2
BLOCK = 16
SMALL_VMEM = 14 << 20
BEAMS_VMEM = 24 << 20


def shifted(value, axis, steps):
    count = lax.axis_size(axis)
    first, last = (max(0, -steps), min(count, count - steps))
    return lax.ppermute(value, axis, [(source, source + steps) for source in range(first, last)])


def correlation_matrix(tap_values, gate_count):
    tap_count = tap_values.shape[0]
    span_width = gate_count + tap_count - 1
    padded_taps = jnp.concatenate(
        [tap_values, jnp.zeros((span_width + 1 - tap_count,), tap_values.dtype)]
    )
    tiled_rows = jnp.tile(padded_taps, gate_count)[: gate_count * span_width].reshape(
        gate_count, span_width
    )
    return tiled_rows.T


def pulse_kernel(replica, gate_count):
    real_part = correlation_matrix(replica[0], gate_count)
    imag_part = correlation_matrix(replica[1], gate_count)
    return jnp.stack([jnp.stack([real_part, imag_part]), jnp.stack([-imag_part, real_part])])


def doppler_table(pulses):
    index = np.arange(pulses, dtype=np.int64)
    phase_index = (index[:, None] * index[None, :]) % pulses
    phase_angle = np.float32(2.0 * np.pi) * phase_index.astype(np.float32) / np.float32(pulses)
    scale = np.float32(1.0) / np.sqrt(np.float32(pulses))
    cosine = np.cos(phase_angle) * scale
    sine = np.sin(phase_angle) * scale
    table = np.stack([np.stack([cosine, -sine]), np.stack([sine, cosine])])
    return table.astype(jnp.bfloat16)


def beam_kernel(beam_weights):
    weight_re = beam_weights[0]
    weight_im = beam_weights[1]
    return jnp.stack([jnp.stack([weight_re, weight_im]), jnp.stack([-weight_im, weight_re])])


def adapt(gram_sum, steering, formed):
    beams = formed.shape[2]
    cov_re = gram_sum[:, :beams, :beams] + gram_sum[:, beams:, beams:]
    cov_im = gram_sum[:, beams:, :beams] - gram_sum[:, :beams, beams:]
    loading = load_ratio * jnp.trace(cov_re, axis1=1, axis2=2) / beams + epsilon
    upper = jnp.concatenate([cov_re, -cov_im], axis=2)
    lower = jnp.concatenate([cov_im, cov_re], axis=2)
    system = jnp.concatenate([upper, lower], axis=1)
    system = system + loading[:, None, None] * jnp.eye(2 * beams, dtype=jnp.float32)[None]
    factor = jnp.linalg.cholesky(system)
    right_side = jnp.concatenate([steering[0], steering[1]], axis=-1)
    solved = jax.scipy.linalg.cho_solve((factor, True), right_side[..., None])[..., 0]
    response = jnp.sum(right_side * solved, axis=-1)
    weights = solved / response[:, None]
    weight_re = weights[:, :beams]
    weight_im = weights[:, beams:]
    beam_re = formed[:, 0].astype(jnp.float32)
    beam_im = formed[:, 1].astype(jnp.float32)
    high = lax.Precision.HIGHEST
    out_re = jnp.einsum("db,dbr->dr", weight_re, beam_re, precision=high) + jnp.einsum(
        "db,dbr->dr", weight_im, beam_im, precision=high
    )
    out_im = jnp.einsum("db,dbr->dr", weight_re, beam_im, precision=high) - jnp.einsum(
        "db,dbr->dr", weight_im, beam_re, precision=high
    )
    return jnp.stack([out_re, out_im])


def on_device_general(echoes, replica, beam_weights, steering):
    pulses = echoes.shape[2]
    gate_count = echoes.shape[3]
    tap_count = replica.shape[1]
    following = shifted(echoes[:, :, :, : tap_count - 1], "range", -1)
    padded = jnp.concatenate([echoes, following], axis=3)
    compressed = jnp.einsum(
        "cepj,cojr->oepr",
        padded,
        pulse_kernel(replica, gate_count),
        preferred_element_type=jnp.float32,
    ).astype(jnp.bfloat16)
    doppler = jnp.einsum(
        "cepr,codp->oedr",
        compressed,
        jnp.asarray(doppler_table(pulses)),
        preferred_element_type=jnp.float32,
    ).astype(jnp.bfloat16)
    kernel_full = beam_kernel(beam_weights)
    own_bins = pulses // lax.axis_size("elem")
    beam_sums = jnp.einsum(
        "cedr,cobe->dobr",
        lax.all_to_all(doppler, "elem", split_axis=2, concat_axis=1, tiled=True),
        kernel_full,
        preferred_element_type=jnp.float32,
    )
    formed = beam_sums.astype(jnp.bfloat16)
    beams = formed.shape[2]
    stacked = formed.reshape(own_bins, 2 * beams, gate_count)
    partial_gram = jnp.einsum("dbr,dcr->dbc", stacked, stacked, preferred_element_type=jnp.float32)
    gram_sum = lax.psum(partial_gram, "range") / (gate_count * lax.axis_size("range"))
    return adapt(gram_sum, steering, formed)


def whole_vmem(count):
    return [pl.BlockSpec(memory_space=pltpu.VMEM)] * count


def far_first(members):
    return [0] + sorted(range(1, members), key=lambda n: (-(n >> 1).bit_count(), n & 1, -n))


def spectra_body(half_ref, place_ref, table_hbm, echo_hbm, *refs, apart):
    *out_hbm, table_ref, echo_ref, out_ref, table_sem, in_sem, out_sem = refs
    members = table_ref.shape[0]
    gates = echo_ref.shape[3]
    steps = in_sem.shape[0]
    block = echo_ref.shape[1] // steps
    pairs = block // 2
    fetch_table = pltpu.make_async_copy(table_hbm.at[half_ref[0]], table_ref, table_sem)
    fetches = [
        pltpu.make_async_copy(
            echo_hbm.at[:, pl.ds(step * block, block)],
            echo_ref.at[:, pl.ds(step * block, block)],
            in_sem.at[step],
        )
        for step in range(steps)
    ]
    if apart:
        stores = [
            pltpu.make_async_copy(out_ref.at[n], out_hbm[n], out_sem.at[n]) for n in range(members)
        ]
    else:
        stores = [
            pltpu.make_async_copy(
                out_ref.at[:, :, pl.ds(step * pairs, pairs)],
                out_hbm[0].at[:, :, pl.ds(step * pairs, pairs)],
                out_sem.at[step],
            )
            for step in range(steps)
        ]
    fetch_table.start()
    for fetch in fetches:
        fetch.start()
    fetch_table.wait()
    place = place_ref[0]
    table = jnp.concatenate([table_ref[place ^ n if apart else n] for n in (far_first(members) if apart else range(members))], axis=0)
    sides = out_ref.shape[1]
    for step in range(steps):
        fetches[step].wait()
        for pair in range(step * pairs, (step + 1) * pairs):
            even, odd = 2 * pair, 2 * pair + 1
            samples = jnp.concatenate(
                [
                    jnp.concatenate([echo_ref[0, even], echo_ref[0, odd]], axis=1),
                    jnp.concatenate([echo_ref[1, even], echo_ref[1, odd]], axis=1),
                ],
                axis=0,
            )
            bins = jnp.dot(table, samples, preferred_element_type=jnp.float32)
            bins = bins.reshape(members, sides, bins.shape[0] // (members * sides), 2 * gates)
            rows = jnp.concatenate([bins[..., :gates], bins[..., gates:]], axis=2)
            out_ref[:, :, pair] = rows.astype(jnp.bfloat16)
        if not apart:
            stores[step].start()
    if apart:
        for store in stores:
            store.start()
    for store in stores:
        store.wait()


def spectra(half, place, echoes, members, sides, apart, steps=STEPS):
    _, elements, pulses, gates = echoes.shape
    devices = 2 * members * sides
    bins = pulses // devices
    table = doppler_table(pulses)
    table = table.transpose(2, 1, 0, 3).reshape(devices, bins, 2, 2 * pulses)
    table = table.transpose(0, 2, 1, 3).reshape(2, members, sides * 2 * bins, 2 * pulses)
    block = (sides, elements // 2, 4 * bins, gates)
    anywhere = pl.BlockSpec(memory_space=pl.ANY)
    count = members if apart else 1
    shape = jax.ShapeDtypeStruct(block if apart else (members, *block), jnp.bfloat16)
    return pl.pallas_call(
        functools.partial(spectra_body, apart=apart),
        in_specs=[pl.BlockSpec(memory_space=pltpu.SMEM)] * 2 + [anywhere, anywhere],
        out_specs=[anywhere] * count,
        out_shape=[shape] * count,
        scratch_shapes=[
            pltpu.VMEM(table.shape[1:], jnp.bfloat16),
            pltpu.VMEM(echoes.shape, jnp.bfloat16),
            pltpu.VMEM((members, *block), jnp.bfloat16),
            pltpu.SemaphoreType.DMA(()),
            pltpu.SemaphoreType.DMA((steps,)),
            pltpu.SemaphoreType.DMA((members if apart else steps,)),
        ],
        compiler_params=pltpu.CompilerParams(vmem_limit_bytes=SPECTRA_VMEM),
        name="spectra",
    )(half, place, jnp.asarray(table), echoes)


def spread_body(weight_ref, out_ref, *, bins):
    beams = weight_ref.shape[1]
    elements = weight_ref.shape[2]
    own = out_ref.shape[2]
    group = 128
    width = group * 2 * bins
    lane = lax.broadcasted_iota(jnp.int32, (group, width), 1)
    row = lax.broadcasted_iota(jnp.int32, (group, width), 0)
    repeat = jnp.where(lane // (2 * bins) == row, 1.0, 0.0).astype(jnp.bfloat16)
    col = lax.broadcasted_iota(jnp.int32, (beams, width), 1)
    is_real = (col // bins) % 2 == 0
    for at in range(elements // group):
        span = slice(at * group, (at + 1) * group)
        real = jnp.dot(weight_ref[0, :, span], repeat, preferred_element_type=jnp.float32)
        imag = jnp.dot(weight_ref[1, :, span], repeat, preferred_element_type=jnp.float32)
        to_real = jnp.where(is_real, real, -imag).astype(jnp.bfloat16)
        to_imag = jnp.where(is_real, imag, real).astype(jnp.bfloat16)
        for n in range(width // own):
            out_ref[at * (width // own) + n, :beams] = to_real[:, n * own : (n + 1) * own]
            out_ref[at * (width // own) + n, beams:] = to_imag[:, n * own : (n + 1) * own]


def spread(beam_weights, bins, members):
    _, beams, elements = beam_weights.shape
    return pl.pallas_call(
        functools.partial(spread_body, bins=bins),
        in_specs=whole_vmem(1),
        out_specs=whole_vmem(1)[0],
        out_shape=jax.ShapeDtypeStruct((members, 2 * beams, elements // members * 2 * bins), jnp.bfloat16),
        compiler_params=pltpu.CompilerParams(vmem_limit_bytes=SMALL_VMEM),
        name="spread",
    )(beam_weights)


def beam_sums(blocks, weights, bins):
    received = jnp.concatenate(
        [
            jnp.concatenate([block[j].reshape(-1, block.shape[3]) for block in blocks], axis=0)
            for j in range(blocks[0].shape[0])
        ],
        axis=1,
    )
    weights = jnp.concatenate(weights, axis=1)
    own = lax.broadcasted_iota(jnp.int32, weights.shape, 1) % bins
    return [
        jnp.dot(
            jnp.where(own == d, weights, jnp.zeros_like(weights)),
            received,
            preferred_element_type=jnp.float32,
        )
        for d in range(bins)
    ]


def crossing_body(place_ref, side_ref, spread_ref, *refs):
    *block_refs, same_ref, other_ref = refs
    bins, _, gates = same_ref.shape
    place, first_side = place_ref[0], side_ref[0] == 0
    weights = [spread_ref[place ^ n] for n in far_first(len(block_refs))]
    for d, value in enumerate(beam_sums([ref[...] for ref in block_refs], weights, bins)):
        first, second = value[:, :gates], value[:, gates:]
        same_ref[d] = jnp.where(first_side, first, second).astype(same_ref.dtype)
        other_ref[d] = jnp.where(first_side, second, first).astype(other_ref.dtype)


def crossing_sums(place, side, blocks, spread_weights, bins):
    shape = jax.ShapeDtypeStruct((bins, spread_weights.shape[1], blocks[0].shape[3]), jnp.bfloat16)
    return pl.pallas_call(
        crossing_body,
        in_specs=[pl.BlockSpec(memory_space=pltpu.SMEM)] * 2 + whole_vmem(1 + len(blocks)),
        out_specs=whole_vmem(2),
        out_shape=[shape, shape],
        compiler_params=pltpu.CompilerParams(vmem_limit_bytes=BEAMS_VMEM),
        name="crossing_sums",
    )(place, side, spread_weights, *blocks)


def split(value):
    high = value.astype(jnp.bfloat16)
    return high, (value - high.astype(jnp.float32)).astype(jnp.bfloat16)


NT = (((1,), (1,)), ((), ()))


def c_mul(a, b):
    return a[0] * b[0] - a[1] * b[1], a[0] * b[1] + a[1] * b[0]
def c_mulc(a, b):
    return a[0] * b[0] + a[1] * b[1], a[1] * b[0] - a[0] * b[1]
def conj(a): return a[0], -a[1]
def c_add(a, b): return a[0] + b[0], a[1] + b[1]
def c_sub(a, b): return a[0] - b[0], a[1] - b[1]
def scale(a, r): return a[0] * r, a[1] * r

def inverse_pair(m):
    a, b, d = m
    r = 1.0 / (a * d - (b[0] * b[0] + b[1] * b[1]))
    return d * r, (-b[0] * r, -b[1] * r), a * r

def inverse_four(e):
    ea, eb, ed = inverse_pair((e[0][0][0], e[0][1], e[1][1][0]))
    f = [[e[0][2], e[0][3]], [e[1][2], e[1][3]]]
    t = [[None, None], [None, None]]
    for l in range(2):
        t[0][l] = c_add(scale(f[0][l], ea), c_mul(eb, f[1][l]))
        t[1][l] = c_add(c_mulc(f[0][l], eb), scale(f[1][l], ed))
    def herm(l, m):
        return c_add(c_mulc(t[0][m], f[0][l]), c_mulc(t[1][m], f[1][l]))
    def herm_re(l):
        return (t[0][l][0]*f[0][l][0] + t[0][l][1]*f[0][l][1]) + (t[1][l][0]*f[1][l][0] + t[1][l][1]*f[1][l][1])
    s = (e[2][2][0] - herm_re(0), c_sub(e[2][3], herm(0, 1)), e[3][3][0] - herm_re(1))
    sa, sb, sd = inverse_pair(s)
    u = [[None, None], [None, None]]
    for j in range(2):
        x = c_add(scale(t[j][0], sa), c_mulc(t[j][1], sb))
        y = c_add(c_mul(t[j][0], sb), scale(t[j][1], sd))
        u[j][0] = (-x[0], -x[1]); u[j][1] = (-y[0], -y[1])
    def corr(j, m):
        return c_add(c_mulc(u[j][0], t[m][0]), c_mulc(u[j][1], t[m][1]))
    zero = jnp.zeros_like(ea)
    p00 = ea - corr(0, 0)[0]; p11 = ed - corr(1, 1)[0]
    p01 = c_sub(eb, corr(0, 1))
    inv = [[None]*4 for _ in range(4)]
    inv[0][0] = (p00, None); inv[1][1] = (p11, None); inv[0][1] = p01
    inv[2][2] = (sa, None); inv[3][3] = (sd, None); inv[2][3] = sb
    for j in range(2):
        for l in range(2): inv[j][2+l] = u[j][l]
    for j in range(4):
        for l in range(j): inv[j][l] = conj(inv[l][j])
    return inv


def turn(x):
    half = x.shape[1] // 2
    lane = lax.broadcasted_iota(jnp.int32, x.shape, 1)
    y = pltpu.roll(x, half, 1)
    return jnp.where(lane < half, -y, y)


def sweep(rows, columns, updated):
    shape = rows[0].shape
    beams = shape[1] // 2
    lane = lax.broadcasted_iota(jnp.int32, shape, 1)
    upper = lax.broadcasted_iota(jnp.int32, shape, 0) < 4

    def col(x, k):
        return jnp.broadcast_to(x[:, k : k + 1], shape)

    first = lane < beams
    base = jnp.where(first, 0, beams)

    def pick(x, k):
        return jnp.take_along_axis(x, base + k, axis=1, mode="promise_in_bounds")

    for step, k in enumerate(columns):
        inside = ((lane >= k) & (lane < k + 4)) | ((lane >= beams + k) & (lane < beams + k + 4))
        pivot = []
        for q in (2 * step, 2 * step + 1):
            x = rows[q]
            y = pltpu.roll(x, 4, 0)
            pivot += [jnp.where(upper, x, y), jnp.where(upper, y, x)]
        entry = [[None] * 4 for _ in range(4)]
        for j in range(4):
            for l in range(j, 4):
                entry[j][l] = (col(pivot[j], k + l), col(pivot[j], beams + k + l) if l > j else None)
        inv = inverse_four(entry)
        unit = [jnp.where(lane == k + l, 1.0, jnp.where(inside, 0.0, pivot[l])) for l in range(4)]
        turned = [turn(x) for x in unit]
        b, bt = [], []
        for j in range(4):
            acc, tacc = unit[j] * inv[j][j][0], turned[j] * inv[j][j][0]
            for l in range(4):
                if l != j:
                    acc = acc + (unit[l] * inv[j][l][0] + turned[l] * inv[j][l][1])
                    tacc = tacc + (turned[l] * inv[j][l][0] - unit[l] * inv[j][l][1])
            b.append(acc)
            bt.append(tacc)
        same = [jnp.where(first, b[l], bt[l]) for l in range(4)]
        cross = [-jnp.where(first, bt[l], b[l]) for l in range(4)]
        for q in sorted(updated(step), key=lambda q: q // 2 != step + 1):
            x = rows[q]
            kept = jnp.where(inside, 0.0, x)
            if q // 2 == step + 1:
                for l in range(4):
                    kept = kept - (col(x, k + l) * b[l] + col(x, beams + k + l) * bt[l])
                rows[q] = kept
            else:
                both = [pick(x, k + l) for l in range(4)]
                straight = (both[0] * same[0] + both[1] * same[1]) + (both[2] * same[2] + both[3] * same[3])
                swapped = (both[0] * cross[0] + both[1] * cross[1]) + (both[2] * cross[2] + both[3] * cross[3])
                rows[q] = (kept - straight) - pltpu.roll(swapped, beams, 1)
        for q in (0, 1):
            rows[2 * step + q] = jnp.where(upper, b[2 * q], b[2 * q + 1])
    return rows


def eliminate(systems, sources, rows_ref, size=BLOCK):
    count = len(systems)
    beams = systems[0].shape[0]
    blocks = size // 2
    rest = [
        jnp.concatenate([systems[n], jnp.broadcast_to(sources[n], (8, 2 * beams))], axis=0) for n in range(count)
    ]
    for first in range(0, beams, size):
        base = count * first
        for n in range(count):
            rows_ref[pl.ds(base + n, size, stride=count), :] = rest[n][:size]
        rows = [rows_ref[base + 8 * q : base + 8 * q + 8] for q in range(blocks)]
        columns = range(first, first + size, 4)
        if first + size == beams:
            bottoms = [value[size : size + 1] for value in rest]
            rows.append(jnp.concatenate(bottoms + bottoms, axis=0))
            return sweep(rows, columns, lambda step: range(2 * step + 2, blocks + 1))[blocks]
        rows = sweep(rows, columns, lambda step: [q for q in range(blocks) if q // 2 != step])
        for q in range(blocks):
            rows_ref[base + 8 * q : base + 8 * q + 8] = rows[q]
        at = (lax.broadcasted_iota(jnp.int32, rest[0][size:].shape, 1) - first) % beams
        for n in range(count):
            top = rows_ref[pl.ds(base + n, size, stride=count), :]
            value = rest[n][size:]
            taken = jnp.dot(
                packed_left(value, at, size), packed_right(top, first), preferred_element_type=jnp.float32
            )
            rest[n] = jnp.where(at < size, 0.0, value) - taken


def packed_left(value, at, size):
    high, low = (part.astype(jnp.float32) for part in split(value))
    again = jnp.where(at < 2 * size, pltpu.roll(low, size, 1), pltpu.roll(high, 2 * size, 1))
    return jnp.where(at < size, high, again).astype(jnp.bfloat16)


def packed_right(top, first):
    size, width = top.shape
    count = width // size
    pieces = [jnp.zeros(top.shape, jnp.bfloat16)] * count
    for start, rows in ((first, top), (first + width // 2, turn(top))):
        high, low = split(rows)
        for step, piece in enumerate((high, high, low)):
            pieces[(start // size + step) % count] = piece
    return jnp.concatenate(pieces, axis=0)


def beams_body(
    side_ref, spectra_ref, spread_ref, same_ref, other_ref, pulse_ref, steer_ref, own_ref, send_ref, rows_ref
):
    bins, total, half = same_ref.shape
    beams = total // 2
    ranges = spectra_ref.shape[1]
    gates = ranges * half
    first_side = side_ref[0] == 0
    members = range(spectra_ref.shape[0])
    near = beam_sums([spectra_ref[n] for n in members], [spread_ref[n] for n in members], bins)
    sums = []
    for d in range(bins):
        same, other = same_ref[d].astype(jnp.float32), other_ref[d].astype(jnp.float32)
        far = [jnp.where(first_side, same, other), jnp.where(first_side, other, same)]
        sums.append(near[d] + jnp.concatenate(far, axis=1))
    high, low = split(
        jnp.concatenate(
            [
                jnp.concatenate(
                    [
                        value[part * beams : (part + 1) * beams, block * half : (block + 1) * half]
                        for block in range(ranges)
                        for part in range(2)
                    ],
                    axis=1,
                )
                for value in sums
            ],
            axis=0,
        )
    )
    formed = [0.0] * ranges
    for block in range(ranges):
        into = slice(block * 2 * half, (block + 1) * 2 * half)
        pulse = pulse_ref[block * 2 * half :, into]
        for piece in (high, low):
            formed[block] = formed[block] + jnp.dot(
                piece[:, block * 2 * half :], pulse, preferred_element_type=jnp.float32
            )
    sub = lax.broadcasted_iota(jnp.int32, (beams, 2 * beams), 0)
    lane = lax.broadcasted_iota(jnp.int32, (beams, 2 * beams), 1)
    both, systems = [], []
    for d in range(bins):
        mine = slice(d * beams, (d + 1) * beams)
        real = jnp.concatenate([value[mine, :half] for value in formed], axis=1)
        imag = jnp.concatenate([value[mine, half:] for value in formed], axis=1)
        top = jnp.concatenate([real, imag], axis=1)
        t_high, t_low = split(top)
        u_high, u_low = split(jnp.concatenate([-imag, real], axis=1))
        left = jnp.concatenate([t_high, t_low], axis=0)
        both.append(left)
        products = lax.dot_general(
            left, jnp.concatenate([t_high, u_high, t_low, u_low], axis=0), NT, preferred_element_type=jnp.float32
        )
        cov = (
            products[:beams, : 2 * beams] + products[:beams, 2 * beams :] + products[beams:, : 2 * beams]
        )
        cov = cov * (1.0 / gates)
        on_diagonal = sub == lane
        trace = jnp.sum(jnp.where(on_diagonal, cov, 0.0), axis=(0, 1), keepdims=True)
        loading = load_ratio * trace / beams + epsilon
        cov = jnp.where(on_diagonal, cov + loading, cov) * (1.0 / loading)
        systems.append(cov)
    steer = steer_ref[...]
    sources = [steer[d : d + 1] for d in range(bins)]
    conj = -eliminate(systems, sources, rows_ref)[:bins]
    response = jnp.sum(conj * steer, axis=1, keepdims=True)
    weight = conj / response
    part_of = lax.broadcasted_iota(jnp.int32, weight.shape, 1) < beams
    other = pltpu.roll(weight, beams, 1)
    pieces = []
    for twice in (jnp.where(part_of, weight, other), jnp.where(part_of, other, weight)):
        w_high, w_low = split(twice)
        pieces += [w_high, jnp.where(part_of, w_low, jnp.zeros_like(w_low))]
    left = jnp.concatenate(pieces, axis=0)
    row = lax.broadcasted_iota(jnp.int32, (bins, 2 * gates), 0)
    by_real = by_imag = jnp.zeros((bins, 2 * gates), jnp.float32)
    for d in range(bins):
        out = jnp.dot(left, both[d], preferred_element_type=jnp.float32)
        by_real = jnp.where(row == d, out[:bins] + out[bins : 2 * bins], by_real)
        by_imag = jnp.where(row == d, out[2 * bins : 3 * bins] + out[3 * bins :], by_imag)
    joined = (
        by_real[:, :gates] - by_imag[:, gates:],
        by_real[:, gates:] + by_imag[:, :gates],
    )
    nothing = jnp.zeros((bins, half), jnp.float32)
    for part in range(2):
        first, second = joined[part][:, :half], joined[part][:, half:]
        own_ref[part] = jnp.concatenate(
            [jnp.where(first_side, first, nothing), jnp.where(first_side, nothing, second)], axis=0
        )
        send_ref[part] = jnp.concatenate(
            [jnp.where(first_side, second, nothing), jnp.where(first_side, nothing, first)], axis=0
        )


def on_device_owned(echoes, replica, beam_weights, steering):
    elems, ranges = lax.axis_size("elem"), lax.axis_size("range")
    devices = elems * ranges
    _, own_elements, pulses, gate_count = echoes.shape
    bins = pulses // devices
    elements = beam_weights.shape[2]
    gates = gate_count * ranges
    side = lax.axis_index("range")
    half = lax.axis_index("elem") // (elems // 2)
    group = devices // 2
    members = elems // 2
    place, far_half, near_half, seat = (
        value.reshape(1).astype(jnp.int32)
        for value in (lax.axis_index("elem") % members, 1 - half, half, side)
    )
    here = lax.dynamic_slice_in_dim(beam_weights, half * (elements // 2), elements // 2, 2)
    spread_weights = spread(here, bins, members)
    blocks = spectra(far_half, place, echoes, members, ranges, True)
    blocks = [
        block if n == 0 else lax.ppermute(block, "elem", [(m, m ^ n) for m in range(elems)])
        for n, block in zip(far_first(members), blocks)
    ]
    (sent,) = spectra(near_half, place, echoes, members, ranges, False)
    sent, *blocks[1:] = lax.optimization_barrier((sent, *blocks[1:]))
    same, other = crossing_sums(place, seat, blocks, spread_weights, bins)
    across = [(n + group) % devices for n in range(devices)]
    same = lax.ppermute(same, ("elem", "range"), list(enumerate(across)))
    other = lax.ppermute(other, ("elem", "range"), [(n, to ^ 1) for n, to in enumerate(across)])
    near = lax.all_to_all(
        sent.reshape(group, *sent.shape[2:]),
        ("elem", "range"),
        0,
        0,
        tiled=True,
        axis_index_groups=[list(range(group)), list(range(group, devices))],
    )
    near = near.reshape(members, ranges, own_elements // 2, 4 * bins, gate_count)
    pulse = pulse_kernel(replica, gates)[:, :, :gates]
    pulse = pulse.reshape(2, 2, ranges, gate_count, ranges, gate_count)
    pulse = pulse.transpose(2, 0, 3, 4, 1, 5).reshape(2 * gates, 2 * gates)
    own_steering = lax.dynamic_slice_in_dim(steering, side * bins, bins, 1)
    steer_row = jnp.concatenate([own_steering[0], -own_steering[1]], axis=1)
    shape = jax.ShapeDtypeStruct((2, 2 * bins, gate_count), jnp.float32)
    own, send = pl.pallas_call(
        beams_body,
        in_specs=[pl.BlockSpec(memory_space=pltpu.SMEM)] + whole_vmem(6),
        out_specs=whole_vmem(2),
        out_shape=[shape, shape],
        scratch_shapes=[pltpu.VMEM((bins * beam_weights.shape[1], 2 * beam_weights.shape[1]), jnp.float32)],
        compiler_params=pltpu.CompilerParams(vmem_limit_bytes=BEAMS_VMEM),
        name="beams",
    )(seat, near, spread_weights, same, other, pulse, steer_row)
    return own + lax.ppermute(send, "range", [(0, 1), (1, 0)])


def on_device(echoes, replica, beam_weights, steering):
    elems, ranges = lax.axis_size("elem"), lax.axis_size("range")
    pulses, gate_count = echoes.shape[2:]
    beams, elements = beam_weights.shape[1:]
    owned = (
        ranges == 2
        and pulses == 4 * elems * ranges
        and gate_count % 128 == 0
        and beams == 64
        and elems % 2 == 0
        and elems & (elems - 1) == 0
        and 128 % echoes.shape[1] == 0
        and elements % 256 == 0
        and echoes.shape[1] % 8 == 0
        and replica.shape[1] <= gate_count
    )
    run = on_device_owned if owned else on_device_general
    return run(echoes, replica, beam_weights, steering)


def solution(mesh):
    return jax.shard_map(
        on_device,
        mesh=mesh,
        in_specs=(P(None, "elem", None, "range"), P(), P(), P(None, "elem", None)),
        out_specs=P(None, "elem", "range"),
        check_vma=False,
    )
```

```python
import functools

import jax
import jax.numpy as jnp
import numpy as np
from jax import lax
from jax.experimental import pallas as pl
from jax.experimental.pallas import tpu as pltpu
from jax.sharding import PartitionSpec as P

load_ratio = 0.1
epsilon = 1e-06
SPECTRA_VMEM = 56 << 20
STEPS = 2
BLOCK = 16
SMALL_VMEM = 14 << 20
BEAMS_VMEM = 24 << 20


def shifted(value, axis, steps):
    count = lax.axis_size(axis)
    first, last = (max(0, -steps), min(count, count - steps))
    return lax.ppermute(value, axis, [(source, source + steps) for source in range(first, last)])


def correlation_matrix(tap_values, gate_count):
    tap_count = tap_values.shape[0]
    span_width = gate_count + tap_count - 1
    padded_taps = jnp.concatenate(
        [tap_values, jnp.zeros((span_width + 1 - tap_count,), tap_values.dtype)]
    )
    tiled_rows = jnp.tile(padded_taps, gate_count)[: gate_count * span_width].reshape(
        gate_count, span_width
    )
    return tiled_rows.T


def pulse_kernel(replica, gate_count):
    real_part = correlation_matrix(replica[0], gate_count)
    imag_part = correlation_matrix(replica[1], gate_count)
    return jnp.stack([jnp.stack([real_part, imag_part]), jnp.stack([-imag_part, real_part])])


def doppler_table(pulses):
    index = np.arange(pulses, dtype=np.int64)
    phase_index = (index[:, None] * index[None, :]) % pulses
    phase_angle = np.float32(2.0 * np.pi) * phase_index.astype(np.float32) / np.float32(pulses)
    scale = np.float32(1.0) / np.sqrt(np.float32(pulses))
    cosine = np.cos(phase_angle) * scale
    sine = np.sin(phase_angle) * scale
    table = np.stack([np.stack([cosine, -sine]), np.stack([sine, cosine])])
    return table.astype(jnp.bfloat16)


def beam_kernel(beam_weights):
    weight_re = beam_weights[0]
    weight_im = beam_weights[1]
    return jnp.stack([jnp.stack([weight_re, weight_im]), jnp.stack([-weight_im, weight_re])])


def adapt(gram_sum, steering, formed):
    beams = formed.shape[2]
    cov_re = gram_sum[:, :beams, :beams] + gram_sum[:, beams:, beams:]
    cov_im = gram_sum[:, beams:, :beams] - gram_sum[:, :beams, beams:]
    loading = load_ratio * jnp.trace(cov_re, axis1=1, axis2=2) / beams + epsilon
    upper = jnp.concatenate([cov_re, -cov_im], axis=2)
    lower = jnp.concatenate([cov_im, cov_re], axis=2)
    system = jnp.concatenate([upper, lower], axis=1)
    system = system + loading[:, None, None] * jnp.eye(2 * beams, dtype=jnp.float32)[None]
    factor = jnp.linalg.cholesky(system)
    right_side = jnp.concatenate([steering[0], steering[1]], axis=-1)
    solved = jax.scipy.linalg.cho_solve((factor, True), right_side[..., None])[..., 0]
    response = jnp.sum(right_side * solved, axis=-1)
    weights = solved / response[:, None]
    weight_re = weights[:, :beams]
    weight_im = weights[:, beams:]
    beam_re = formed[:, 0].astype(jnp.float32)
    beam_im = formed[:, 1].astype(jnp.float32)
    high = lax.Precision.HIGHEST
    out_re = jnp.einsum("db,dbr->dr", weight_re, beam_re, precision=high) + jnp.einsum(
        "db,dbr->dr", weight_im, beam_im, precision=high
    )
    out_im = jnp.einsum("db,dbr->dr", weight_re, beam_im, precision=high) - jnp.einsum(
        "db,dbr->dr", weight_im, beam_re, precision=high
    )
    return jnp.stack([out_re, out_im])


def on_device_general(echoes, replica, beam_weights, steering):
    pulses = echoes.shape[2]
    gate_count = echoes.shape[3]
    tap_count = replica.shape[1]
    following = shifted(echoes[:, :, :, : tap_count - 1], "range", -1)
    padded = jnp.concatenate([echoes, following], axis=3)
    compressed = jnp.einsum(
        "cepj,cojr->oepr",
        padded,
        pulse_kernel(replica, gate_count),
        preferred_element_type=jnp.float32,
    ).astype(jnp.bfloat16)
    doppler = jnp.einsum(
        "cepr,codp->oedr",
        compressed,
        jnp.asarray(doppler_table(pulses)),
        preferred_element_type=jnp.float32,
    ).astype(jnp.bfloat16)
    kernel_full = beam_kernel(beam_weights)
    own_bins = pulses // lax.axis_size("elem")
    beam_sums = jnp.einsum(
        "cedr,cobe->dobr",
        lax.all_to_all(doppler, "elem", split_axis=2, concat_axis=1, tiled=True),
        kernel_full,
        preferred_element_type=jnp.float32,
    )
    formed = beam_sums.astype(jnp.bfloat16)
    beams = formed.shape[2]
    stacked = formed.reshape(own_bins, 2 * beams, gate_count)
    partial_gram = jnp.einsum("dbr,dcr->dbc", stacked, stacked, preferred_element_type=jnp.float32)
    gram_sum = lax.psum(partial_gram, "range") / (gate_count * lax.axis_size("range"))
    return adapt(gram_sum, steering, formed)


def whole_vmem(count):
    return [pl.BlockSpec(memory_space=pltpu.VMEM)] * count


def far_first(members):
    return [0] + sorted(range(1, members), key=lambda n: (-(n >> 1).bit_count(), n & 1, -n))


def spectra_body(half_ref, place_ref, table_hbm, echo_hbm, *refs, apart):
    *out_hbm, table_ref, echo_ref, out_ref, table_sem, in_sem, out_sem = refs
    members = table_ref.shape[0]
    gates = echo_ref.shape[3]
    steps = in_sem.shape[0]
    block = echo_ref.shape[1] // steps
    pairs = block // 2
    fetch_table = pltpu.make_async_copy(table_hbm.at[half_ref[0]], table_ref, table_sem)
    fetches = [
        pltpu.make_async_copy(
            echo_hbm.at[:, pl.ds(step * block, block)],
            echo_ref.at[:, pl.ds(step * block, block)],
            in_sem.at[step],
        )
        for step in range(steps)
    ]
    if apart:
        stores = [
            pltpu.make_async_copy(out_ref.at[n], out_hbm[n], out_sem.at[n]) for n in range(members)
        ]
    else:
        stores = [
            pltpu.make_async_copy(
                out_ref.at[:, :, pl.ds(step * pairs, pairs)],
                out_hbm[0].at[:, :, pl.ds(step * pairs, pairs)],
                out_sem.at[step],
            )
            for step in range(steps)
        ]
    fetch_table.start()
    for fetch in fetches:
        fetch.start()
    fetch_table.wait()
    place = place_ref[0]
    table = jnp.concatenate([table_ref[place ^ n if apart else n] for n in (far_first(members) if apart else range(members))], axis=0)
    sides = out_ref.shape[1]
    for step in range(steps):
        fetches[step].wait()
        for pair in range(step * pairs, (step + 1) * pairs):
            even, odd = 2 * pair, 2 * pair + 1
            samples = jnp.concatenate(
                [
                    jnp.concatenate([echo_ref[0, even], echo_ref[0, odd]], axis=1),
                    jnp.concatenate([echo_ref[1, even], echo_ref[1, odd]], axis=1),
                ],
                axis=0,
            )
            bins = jnp.dot(table, samples, preferred_element_type=jnp.float32)
            bins = bins.reshape(members, sides, bins.shape[0] // (members * sides), 2 * gates)
            rows = jnp.concatenate([bins[..., :gates], bins[..., gates:]], axis=2)
            out_ref[:, :, pair] = rows.astype(jnp.bfloat16)
        if not apart:
            stores[step].start()
    if apart:
        for store in stores:
            store.start()
    for store in stores:
        store.wait()


def spectra(half, place, echoes, members, sides, apart, steps=STEPS):
    _, elements, pulses, gates = echoes.shape
    devices = 2 * members * sides
    bins = pulses // devices
    table = doppler_table(pulses)
    table = table.transpose(2, 1, 0, 3).reshape(devices, bins, 2, 2 * pulses)
    table = table.transpose(0, 2, 1, 3).reshape(2, members, sides * 2 * bins, 2 * pulses)
    block = (sides, elements // 2, 4 * bins, gates)
    anywhere = pl.BlockSpec(memory_space=pl.ANY)
    count = members if apart else 1
    shape = jax.ShapeDtypeStruct(block if apart else (members, *block), jnp.bfloat16)
    return pl.pallas_call(
        functools.partial(spectra_body, apart=apart),
        in_specs=[pl.BlockSpec(memory_space=pltpu.SMEM)] * 2 + [anywhere, anywhere],
        out_specs=[anywhere] * count,
        out_shape=[shape] * count,
        scratch_shapes=[
            pltpu.VMEM(table.shape[1:], jnp.bfloat16),
            pltpu.VMEM(echoes.shape, jnp.bfloat16),
            pltpu.VMEM((members, *block), jnp.bfloat16),
            pltpu.SemaphoreType.DMA(()),
            pltpu.SemaphoreType.DMA((steps,)),
            pltpu.SemaphoreType.DMA((members if apart else steps,)),
        ],
        compiler_params=pltpu.CompilerParams(vmem_limit_bytes=SPECTRA_VMEM),
        name="spectra",
    )(half, place, jnp.asarray(table), echoes)


def spread_body(weight_ref, out_ref, *, bins):
    beams = weight_ref.shape[1]
    elements = weight_ref.shape[2]
    own = out_ref.shape[2]
    group = 128
    width = group * 2 * bins
    lane = lax.broadcasted_iota(jnp.int32, (group, width), 1)
    row = lax.broadcasted_iota(jnp.int32, (group, width), 0)
    repeat = jnp.where(lane // (2 * bins) == row, 1.0, 0.0).astype(jnp.bfloat16)
    col = lax.broadcasted_iota(jnp.int32, (beams, width), 1)
    is_real = (col // bins) % 2 == 0
    for at in range(elements // group):
        span = slice(at * group, (at + 1) * group)
        real = jnp.dot(weight_ref[0, :, span], repeat, preferred_element_type=jnp.float32)
        imag = jnp.dot(weight_ref[1, :, span], repeat, preferred_element_type=jnp.float32)
        to_real = jnp.where(is_real, real, -imag).astype(jnp.bfloat16)
        to_imag = jnp.where(is_real, imag, real).astype(jnp.bfloat16)
        for n in range(width // own):
            out_ref[at * (width // own) + n, :beams] = to_real[:, n * own : (n + 1) * own]
            out_ref[at * (width // own) + n, beams:] = to_imag[:, n * own : (n + 1) * own]


def spread(beam_weights, bins, members):
    _, beams, elements = beam_weights.shape
    return pl.pallas_call(
        functools.partial(spread_body, bins=bins),
        in_specs=whole_vmem(1),
        out_specs=whole_vmem(1)[0],
        out_shape=jax.ShapeDtypeStruct((members, 2 * beams, elements // members * 2 * bins), jnp.bfloat16),
        compiler_params=pltpu.CompilerParams(vmem_limit_bytes=SMALL_VMEM),
        name="spread",
    )(beam_weights)


def beam_sums(blocks, weights, bins):
    received = jnp.concatenate(
        [
            jnp.concatenate([block[j].reshape(-1, block.shape[3]) for block in blocks], axis=0)
            for j in range(blocks[0].shape[0])
        ],
        axis=1,
    )
    weights = jnp.concatenate(weights, axis=1)
    own = lax.broadcasted_iota(jnp.int32, weights.shape, 1) % bins
    return [
        jnp.dot(
            jnp.where(own == d, weights, jnp.zeros_like(weights)),
            received,
            preferred_element_type=jnp.float32,
        )
        for d in range(bins)
    ]


def crossing_body(place_ref, side_ref, spread_ref, *refs):
    *block_refs, same_ref, other_ref = refs
    bins, _, gates = same_ref.shape
    place, first_side = place_ref[0], side_ref[0] == 0
    weights = [spread_ref[place ^ n] for n in far_first(len(block_refs))]
    for d, value in enumerate(beam_sums([ref[...] for ref in block_refs], weights, bins)):
        first, second = value[:, :gates], value[:, gates:]
        same_ref[d] = jnp.where(first_side, first, second).astype(same_ref.dtype)
        other_ref[d] = jnp.where(first_side, second, first).astype(other_ref.dtype)


def crossing_sums(place, side, blocks, spread_weights, bins):
    shape = jax.ShapeDtypeStruct((bins, spread_weights.shape[1], blocks[0].shape[3]), jnp.bfloat16)
    return pl.pallas_call(
        crossing_body,
        in_specs=[pl.BlockSpec(memory_space=pltpu.SMEM)] * 2 + whole_vmem(1 + len(blocks)),
        out_specs=whole_vmem(2),
        out_shape=[shape, shape],
        compiler_params=pltpu.CompilerParams(vmem_limit_bytes=BEAMS_VMEM),
        name="crossing_sums",
    )(place, side, spread_weights, *blocks)


def split(value):
    high = value.astype(jnp.bfloat16)
    return high, (value - high.astype(jnp.float32)).astype(jnp.bfloat16)


NT = (((1,), (1,)), ((), ()))


def c_mul(a, b):
    return a[0] * b[0] - a[1] * b[1], a[0] * b[1] + a[1] * b[0]
def c_mulc(a, b):
    return a[0] * b[0] + a[1] * b[1], a[1] * b[0] - a[0] * b[1]
def conj(a): return a[0], -a[1]
def c_add(a, b): return a[0] + b[0], a[1] + b[1]
def c_sub(a, b): return a[0] - b[0], a[1] - b[1]
def scale(a, r): return a[0] * r, a[1] * r

def inverse_pair(m):
    a, b, d = m
    r = 1.0 / (a * d - (b[0] * b[0] + b[1] * b[1]))
    return d * r, (-b[0] * r, -b[1] * r), a * r

def inverse_four(e):
    ea, eb, ed = inverse_pair((e[0][0][0], e[0][1], e[1][1][0]))
    f = [[e[0][2], e[0][3]], [e[1][2], e[1][3]]]
    t = [[None, None], [None, None]]
    for l in range(2):
        t[0][l] = c_add(scale(f[0][l], ea), c_mul(eb, f[1][l]))
        t[1][l] = c_add(c_mulc(f[0][l], eb), scale(f[1][l], ed))
    def herm(l, m):
        return c_add(c_mulc(t[0][m], f[0][l]), c_mulc(t[1][m], f[1][l]))
    def herm_re(l):
        return (t[0][l][0]*f[0][l][0] + t[0][l][1]*f[0][l][1]) + (t[1][l][0]*f[1][l][0] + t[1][l][1]*f[1][l][1])
    s = (e[2][2][0] - herm_re(0), c_sub(e[2][3], herm(0, 1)), e[3][3][0] - herm_re(1))
    sa, sb, sd = inverse_pair(s)
    u = [[None, None], [None, None]]
    for j in range(2):
        x = c_add(scale(t[j][0], sa), c_mulc(t[j][1], sb))
        y = c_add(c_mul(t[j][0], sb), scale(t[j][1], sd))
        u[j][0] = (-x[0], -x[1]); u[j][1] = (-y[0], -y[1])
    def corr(j, m):
        return c_add(c_mulc(u[j][0], t[m][0]), c_mulc(u[j][1], t[m][1]))
    zero = jnp.zeros_like(ea)
    p00 = ea - corr(0, 0)[0]; p11 = ed - corr(1, 1)[0]
    p01 = c_sub(eb, corr(0, 1))
    inv = [[None]*4 for _ in range(4)]
    inv[0][0] = (p00, None); inv[1][1] = (p11, None); inv[0][1] = p01
    inv[2][2] = (sa, None); inv[3][3] = (sd, None); inv[2][3] = sb
    for j in range(2):
        for l in range(2): inv[j][2+l] = u[j][l]
    for j in range(4):
        for l in range(j): inv[j][l] = conj(inv[l][j])
    return inv


def turn(x):
    half = x.shape[1] // 2
    lane = lax.broadcasted_iota(jnp.int32, x.shape, 1)
    y = pltpu.roll(x, half, 1)
    return jnp.where(lane < half, -y, y)


def sweep(rows, columns, updated):
    shape = rows[0].shape
    beams = shape[1] // 2
    lane = lax.broadcasted_iota(jnp.int32, shape, 1)
    upper = lax.broadcasted_iota(jnp.int32, shape, 0) < 4

    def col(x, k):
        return jnp.broadcast_to(x[:, k : k + 1], shape)

    first = lane < beams
    base = jnp.where(first, 0, beams)

    def pick(x, k):
        return jnp.take_along_axis(x, base + k, axis=1, mode="promise_in_bounds")

    for step, k in enumerate(columns):
        inside = ((lane >= k) & (lane < k + 4)) | ((lane >= beams + k) & (lane < beams + k + 4))
        pivot = []
        for q in (2 * step, 2 * step + 1):
            x = rows[q]
            y = pltpu.roll(x, 4, 0)
            pivot += [jnp.where(upper, x, y), jnp.where(upper, y, x)]
        entry = [[None] * 4 for _ in range(4)]
        for j in range(4):
            for l in range(j, 4):
                entry[j][l] = (col(pivot[j], k + l), col(pivot[j], beams + k + l) if l > j else None)
        inv = inverse_four(entry)
        unit = [jnp.where(lane == k + l, 1.0, jnp.where(inside, 0.0, pivot[l])) for l in range(4)]
        turned = [turn(x) for x in unit]
        b, bt = [], []
        for j in range(4):
            acc, tacc = unit[j] * inv[j][j][0], turned[j] * inv[j][j][0]
            for l in range(4):
                if l != j:
                    acc = acc + (unit[l] * inv[j][l][0] + turned[l] * inv[j][l][1])
                    tacc = tacc + (turned[l] * inv[j][l][0] - unit[l] * inv[j][l][1])
            b.append(acc)
            bt.append(tacc)
        same = [jnp.where(first, b[l], bt[l]) for l in range(4)]
        cross = [-jnp.where(first, bt[l], b[l]) for l in range(4)]
        for q in sorted(updated(step), key=lambda q: q // 2 != step + 1):
            x = rows[q]
            kept = jnp.where(inside, 0.0, x)
            if q // 2 == step + 1:
                for l in range(4):
                    kept = kept - (col(x, k + l) * b[l] + col(x, beams + k + l) * bt[l])
                rows[q] = kept
            else:
                both = [pick(x, k + l) for l in range(4)]
                straight = (both[0] * same[0] + both[1] * same[1]) + (both[2] * same[2] + both[3] * same[3])
                swapped = (both[0] * cross[0] + both[1] * cross[1]) + (both[2] * cross[2] + both[3] * cross[3])
                rows[q] = (kept - straight) - pltpu.roll(swapped, beams, 1)
        for q in (0, 1):
            rows[2 * step + q] = jnp.where(upper, b[2 * q], b[2 * q + 1])
    return rows


def eliminate(systems, sources, rows_ref, size=BLOCK):
    count = len(systems)
    beams = systems[0].shape[0]
    blocks = size // 2
    rest = [
        jnp.concatenate([systems[n], jnp.broadcast_to(sources[n], (8, 2 * beams))], axis=0) for n in range(count)
    ]
    for first in range(0, beams, size):
        base = count * first
        for n in range(count):
            rows_ref[pl.ds(base + n, size, stride=count), :] = rest[n][:size]
        rows = [rows_ref[base + 8 * q : base + 8 * q + 8] for q in range(blocks)]
        columns = range(first, first + size, 4)
        if first + size == beams:
            bottoms = [value[size : size + 1] for value in rest]
            rows.append(jnp.concatenate(bottoms + bottoms, axis=0))
            return sweep(rows, columns, lambda step: range(2 * step + 2, blocks + 1))[blocks]
        rows = sweep(rows, columns, lambda step: [q for q in range(blocks) if q // 2 != step])
        for q in range(blocks):
            rows_ref[base + 8 * q : base + 8 * q + 8] = rows[q]
        at = (lax.broadcasted_iota(jnp.int32, rest[0][size:].shape, 1) - first) % beams
        for n in range(count):
            top = rows_ref[pl.ds(base + n, size, stride=count), :]
            value = rest[n][size:]
            taken = jnp.dot(
                packed_left(value, at, size), packed_right(top, first), preferred_element_type=jnp.float32
            )
            rest[n] = jnp.where(at < size, 0.0, value) - taken


def packed_left(value, at, size):
    high, low = (part.astype(jnp.float32) for part in split(value))
    again = jnp.where(at < 2 * size, pltpu.roll(low, size, 1), pltpu.roll(high, 2 * size, 1))
    return jnp.where(at < size, high, again).astype(jnp.bfloat16)


def packed_right(top, first):
    size, width = top.shape
    count = width // size
    pieces = [jnp.zeros(top.shape, jnp.bfloat16)] * count
    for start, rows in ((first, top), (first + width // 2, turn(top))):
        high, low = split(rows)
        for step, piece in enumerate((high, high, low)):
            pieces[(start // size + step) % count] = piece
    return jnp.concatenate(pieces, axis=0)


def beams_body(
    side_ref, spectra_ref, spread_ref, same_ref, other_ref, pulse_ref, steer_ref, own_ref, send_ref, rows_ref
):
    bins, total, half = same_ref.shape
    beams = total // 2
    ranges = spectra_ref.shape[1]
    gates = ranges * half
    first_side = side_ref[0] == 0
    members = range(spectra_ref.shape[0])
    near = beam_sums([spectra_ref[n] for n in members], [spread_ref[n] for n in members], bins)
    sums = []
    for d in range(bins):
        same, other = same_ref[d].astype(jnp.float32), other_ref[d].astype(jnp.float32)
        far = [jnp.where(first_side, same, other), jnp.where(first_side, other, same)]
        sums.append(near[d] + jnp.concatenate(far, axis=1))
    high, low = split(
        jnp.concatenate(
            [
                jnp.concatenate(
                    [
                        value[part * beams : (part + 1) * beams, block * half : (block + 1) * half]
                        for block in range(ranges)
                        for part in range(2)
                    ],
                    axis=1,
                )
                for value in sums
            ],
            axis=0,
        )
    )
    formed = [0.0] * ranges
    for block in range(ranges):
        into = slice(block * 2 * half, (block + 1) * 2 * half)
        pulse = pulse_ref[block * 2 * half :, into]
        for piece in (high, low):
            formed[block] = formed[block] + jnp.dot(
                piece[:, block * 2 * half :], pulse, preferred_element_type=jnp.float32
            )
    sub = lax.broadcasted_iota(jnp.int32, (beams, 2 * beams), 0)
    lane = lax.broadcasted_iota(jnp.int32, (beams, 2 * beams), 1)
    both, systems = [], []
    for d in range(bins):
        mine = slice(d * beams, (d + 1) * beams)
        real = jnp.concatenate([value[mine, :half] for value in formed], axis=1)
        imag = jnp.concatenate([value[mine, half:] for value in formed], axis=1)
        top = jnp.concatenate([real, imag], axis=1)
        t_high, t_low = split(top)
        u_high, u_low = split(jnp.concatenate([-imag, real], axis=1))
        left = jnp.concatenate([t_high, t_low], axis=0)
        both.append(left)
        products = lax.dot_general(
            left, jnp.concatenate([t_high, u_high, t_low, u_low], axis=0), NT, preferred_element_type=jnp.float32
        )
        cov = (
            products[:beams, : 2 * beams] + products[:beams, 2 * beams :] + products[beams:, : 2 * beams]
        )
        cov = cov * (1.0 / gates)
        on_diagonal = sub == lane
        trace = jnp.sum(jnp.where(on_diagonal, cov, 0.0), axis=(0, 1), keepdims=True)
        loading = load_ratio * trace / beams + epsilon
        cov = jnp.where(on_diagonal, cov + loading, cov) * (1.0 / loading)
        systems.append(cov)
    steer = steer_ref[...]
    sources = [steer[d : d + 1] for d in range(bins)]
    conj = -eliminate(systems, sources, rows_ref)[:bins]
    response = jnp.sum(conj * steer, axis=1, keepdims=True)
    weight = conj / response
    part_of = lax.broadcasted_iota(jnp.int32, weight.shape, 1) < beams
    other = pltpu.roll(weight, beams, 1)
    pieces = []
    for twice in (jnp.where(part_of, weight, other), jnp.where(part_of, other, weight)):
        w_high, w_low = split(twice)
        pieces += [w_high, jnp.where(part_of, w_low, jnp.zeros_like(w_low))]
    left = jnp.concatenate(pieces, axis=0)
    row = lax.broadcasted_iota(jnp.int32, (bins, 2 * gates), 0)
    by_real = by_imag = jnp.zeros((bins, 2 * gates), jnp.float32)
    for d in range(bins):
        out = jnp.dot(left, both[d], preferred_element_type=jnp.float32)
        by_real = jnp.where(row == d, out[:bins] + out[bins : 2 * bins], by_real)
        by_imag = jnp.where(row == d, out[2 * bins : 3 * bins] + out[3 * bins :], by_imag)
    joined = (
        by_real[:, :gates] - by_imag[:, gates:],
        by_real[:, gates:] + by_imag[:, :gates],
    )
    nothing = jnp.zeros((bins, half), jnp.float32)
    for part in range(2):
        first, second = joined[part][:, :half], joined[part][:, half:]
        own_ref[part] = jnp.concatenate(
            [jnp.where(first_side, first, nothing), jnp.where(first_side, nothing, second)], axis=0
        )
        send_ref[part] = jnp.concatenate(
            [jnp.where(first_side, second, nothing), jnp.where(first_side, nothing, first)], axis=0
        )


def on_device_owned(echoes, replica, beam_weights, steering):
    elems, ranges = lax.axis_size("elem"), lax.axis_size("range")
    devices = elems * ranges
    _, own_elements, pulses, gate_count = echoes.shape
    bins = pulses // devices
    elements = beam_weights.shape[2]
    gates = gate_count * ranges
    side = lax.axis_index("range")
    half = lax.axis_index("elem") // (elems // 2)
    group = devices // 2
    members = elems // 2
    place, far_half, near_half, seat = (
        value.reshape(1).astype(jnp.int32)
        for value in (lax.axis_index("elem") % members, 1 - half, half, side)
    )
    here = lax.dynamic_slice_in_dim(beam_weights, half * (elements // 2), elements // 2, 2)
    spread_weights = spread(here, bins, members)
    blocks = spectra(far_half, place, echoes, members, ranges, True)
    blocks = [
        block if n == 0 else lax.ppermute(block, "elem", [(m, m ^ n) for m in range(elems)])
        for n, block in zip(far_first(members), blocks)
    ]
    pulse = pulse_kernel(replica, gates)[:, :, :gates]
    pulse = pulse.reshape(2, 2, ranges, gate_count, ranges, gate_count)
    pulse = pulse.transpose(2, 0, 3, 4, 1, 5).reshape(2 * gates, 2 * gates)
    own_steering = lax.dynamic_slice_in_dim(steering, side * bins, bins, 1)
    steer_row = jnp.concatenate([own_steering[0], -own_steering[1]], axis=1)
    (sent,) = spectra(near_half, place, echoes, members, ranges, False)
    sent, spread_weights, pulse, steer_row, *blocks[1:] = lax.optimization_barrier(
        (sent, spread_weights, pulse, steer_row, *blocks[1:])
    )
    same, other = crossing_sums(place, seat, blocks, spread_weights, bins)
    across = [(n + group) % devices for n in range(devices)]
    same = lax.ppermute(same, ("elem", "range"), list(enumerate(across)))
    other = lax.ppermute(other, ("elem", "range"), [(n, to ^ 1) for n, to in enumerate(across)])
    near = lax.all_to_all(
        sent.reshape(group, *sent.shape[2:]),
        ("elem", "range"),
        0,
        0,
        tiled=True,
        axis_index_groups=[list(range(group)), list(range(group, devices))],
    )
    near = near.reshape(members, ranges, own_elements // 2, 4 * bins, gate_count)
    shape = jax.ShapeDtypeStruct((2, 2 * bins, gate_count), jnp.float32)
    own, send = pl.pallas_call(
        beams_body,
        in_specs=[pl.BlockSpec(memory_space=pltpu.SMEM)] + whole_vmem(6),
        out_specs=whole_vmem(2),
        out_shape=[shape, shape],
        scratch_shapes=[pltpu.VMEM((bins * beam_weights.shape[1], 2 * beam_weights.shape[1]), jnp.float32)],
        compiler_params=pltpu.CompilerParams(vmem_limit_bytes=BEAMS_VMEM),
        name="beams",
    )(seat, near, spread_weights, same, other, pulse, steer_row)
    return own + lax.ppermute(send, "range", [(0, 1), (1, 0)])


def on_device(echoes, replica, beam_weights, steering):
    elems, ranges = lax.axis_size("elem"), lax.axis_size("range")
    pulses, gate_count = echoes.shape[2:]
    beams, elements = beam_weights.shape[1:]
    owned = (
        ranges == 2
        and pulses == 4 * elems * ranges
        and gate_count % 128 == 0
        and beams == 64
        and elems % 2 == 0
        and elems & (elems - 1) == 0
        and 128 % echoes.shape[1] == 0
        and elements % 256 == 0
        and echoes.shape[1] % 8 == 0
        and replica.shape[1] <= gate_count
    )
    run = on_device_owned if owned else on_device_general
    return run(echoes, replica, beam_weights, steering)


def solution(mesh):
    return jax.shard_map(
        on_device,
        mesh=mesh,
        in_specs=(P(None, "elem", None, "range"), P(), P(), P(None, "elem", None)),
        out_specs=P(None, "elem", "range"),
        check_vma=False,
    )
```

```python
import functools

import jax
import jax.numpy as jnp
import numpy as np
from jax import lax
from jax.experimental import pallas as pl
from jax.experimental.pallas import tpu as pltpu
from jax.sharding import PartitionSpec as P

load_ratio = 0.1
epsilon = 1e-06
SPECTRA_VMEM = 56 << 20
STEPS = 2
BLOCK = 16
SMALL_VMEM = 14 << 20
BEAMS_VMEM = 24 << 20


def shifted(value, axis, steps):
    count = lax.axis_size(axis)
    first, last = (max(0, -steps), min(count, count - steps))
    return lax.ppermute(value, axis, [(source, source + steps) for source in range(first, last)])


def correlation_matrix(tap_values, gate_count):
    tap_count = tap_values.shape[0]
    span_width = gate_count + tap_count - 1
    padded_taps = jnp.concatenate(
        [tap_values, jnp.zeros((span_width + 1 - tap_count,), tap_values.dtype)]
    )
    tiled_rows = jnp.tile(padded_taps, gate_count)[: gate_count * span_width].reshape(
        gate_count, span_width
    )
    return tiled_rows.T


def pulse_kernel(replica, gate_count):
    real_part = correlation_matrix(replica[0], gate_count)
    imag_part = correlation_matrix(replica[1], gate_count)
    return jnp.stack([jnp.stack([real_part, imag_part]), jnp.stack([-imag_part, real_part])])


def doppler_table(pulses):
    index = np.arange(pulses, dtype=np.int64)
    phase_index = (index[:, None] * index[None, :]) % pulses
    phase_angle = np.float32(2.0 * np.pi) * phase_index.astype(np.float32) / np.float32(pulses)
    scale = np.float32(1.0) / np.sqrt(np.float32(pulses))
    cosine = np.cos(phase_angle) * scale
    sine = np.sin(phase_angle) * scale
    table = np.stack([np.stack([cosine, -sine]), np.stack([sine, cosine])])
    return table.astype(jnp.bfloat16)


def beam_kernel(beam_weights):
    weight_re = beam_weights[0]
    weight_im = beam_weights[1]
    return jnp.stack([jnp.stack([weight_re, weight_im]), jnp.stack([-weight_im, weight_re])])


def adapt(gram_sum, steering, formed):
    beams = formed.shape[2]
    cov_re = gram_sum[:, :beams, :beams] + gram_sum[:, beams:, beams:]
    cov_im = gram_sum[:, beams:, :beams] - gram_sum[:, :beams, beams:]
    loading = load_ratio * jnp.trace(cov_re, axis1=1, axis2=2) / beams + epsilon
    upper = jnp.concatenate([cov_re, -cov_im], axis=2)
    lower = jnp.concatenate([cov_im, cov_re], axis=2)
    system = jnp.concatenate([upper, lower], axis=1)
    system = system + loading[:, None, None] * jnp.eye(2 * beams, dtype=jnp.float32)[None]
    factor = jnp.linalg.cholesky(system)
    right_side = jnp.concatenate([steering[0], steering[1]], axis=-1)
    solved = jax.scipy.linalg.cho_solve((factor, True), right_side[..., None])[..., 0]
    response = jnp.sum(right_side * solved, axis=-1)
    weights = solved / response[:, None]
    weight_re = weights[:, :beams]
    weight_im = weights[:, beams:]
    beam_re = formed[:, 0].astype(jnp.float32)
    beam_im = formed[:, 1].astype(jnp.float32)
    high = lax.Precision.HIGHEST
    out_re = jnp.einsum("db,dbr->dr", weight_re, beam_re, precision=high) + jnp.einsum(
        "db,dbr->dr", weight_im, beam_im, precision=high
    )
    out_im = jnp.einsum("db,dbr->dr", weight_re, beam_im, precision=high) - jnp.einsum(
        "db,dbr->dr", weight_im, beam_re, precision=high
    )
    return jnp.stack([out_re, out_im])


def on_device_general(echoes, replica, beam_weights, steering):
    pulses = echoes.shape[2]
    gate_count = echoes.shape[3]
    tap_count = replica.shape[1]
    following = shifted(echoes[:, :, :, : tap_count - 1], "range", -1)
    padded = jnp.concatenate([echoes, following], axis=3)
    compressed = jnp.einsum(
        "cepj,cojr->oepr",
        padded,
        pulse_kernel(replica, gate_count),
        preferred_element_type=jnp.float32,
    ).astype(jnp.bfloat16)
    doppler = jnp.einsum(
        "cepr,codp->oedr",
        compressed,
        jnp.asarray(doppler_table(pulses)),
        preferred_element_type=jnp.float32,
    ).astype(jnp.bfloat16)
    kernel_full = beam_kernel(beam_weights)
    own_bins = pulses // lax.axis_size("elem")
    beam_sums = jnp.einsum(
        "cedr,cobe->dobr",
        lax.all_to_all(doppler, "elem", split_axis=2, concat_axis=1, tiled=True),
        kernel_full,
        preferred_element_type=jnp.float32,
    )
    formed = beam_sums.astype(jnp.bfloat16)
    beams = formed.shape[2]
    stacked = formed.reshape(own_bins, 2 * beams, gate_count)
    partial_gram = jnp.einsum("dbr,dcr->dbc", stacked, stacked, preferred_element_type=jnp.float32)
    gram_sum = lax.psum(partial_gram, "range") / (gate_count * lax.axis_size("range"))
    return adapt(gram_sum, steering, formed)


def whole_vmem(count):
    return [pl.BlockSpec(memory_space=pltpu.VMEM)] * count


def far_first(members):
    return [0] + sorted(range(1, members), key=lambda n: (n & 1, -n))


def spectra_body(half_ref, place_ref, table_hbm, echo_hbm, *refs, apart):
    *out_hbm, table_ref, echo_ref, out_ref, table_sem, in_sem, out_sem = refs
    members = table_ref.shape[0]
    gates = echo_ref.shape[3]
    steps = in_sem.shape[0]
    block = echo_ref.shape[1] // steps
    pairs = block // 2
    fetch_table = pltpu.make_async_copy(table_hbm.at[half_ref[0]], table_ref, table_sem)
    fetches = [
        pltpu.make_async_copy(
            echo_hbm.at[:, pl.ds(step * block, block)],
            echo_ref.at[:, pl.ds(step * block, block)],
            in_sem.at[step],
        )
        for step in range(steps)
    ]
    if apart:
        stores = [
            pltpu.make_async_copy(out_ref.at[n], out_hbm[n], out_sem.at[n]) for n in range(members)
        ]
    else:
        stores = [
            pltpu.make_async_copy(
                out_ref.at[:, :, pl.ds(step * pairs, pairs)],
                out_hbm[0].at[:, :, pl.ds(step * pairs, pairs)],
                out_sem.at[step],
            )
            for step in range(steps)
        ]
    fetch_table.start()
    for fetch in fetches:
        fetch.start()
    fetch_table.wait()
    place = place_ref[0]
    table = jnp.concatenate([table_ref[place ^ n if apart else n] for n in (far_first(members) if apart else range(members))], axis=0)
    sides = out_ref.shape[1]
    for step in range(steps):
        fetches[step].wait()
        for pair in range(step * pairs, (step + 1) * pairs):
            even, odd = 2 * pair, 2 * pair + 1
            samples = jnp.concatenate(
                [
                    jnp.concatenate([echo_ref[0, even], echo_ref[0, odd]], axis=1),
                    jnp.concatenate([echo_ref[1, even], echo_ref[1, odd]], axis=1),
                ],
                axis=0,
            )
            bins = jnp.dot(table, samples, preferred_element_type=jnp.float32)
            bins = bins.reshape(members, sides, bins.shape[0] // (members * sides), 2 * gates)
            rows = jnp.concatenate([bins[..., :gates], bins[..., gates:]], axis=2)
            out_ref[:, :, pair] = rows.astype(jnp.bfloat16)
        if not apart:
            stores[step].start()
    if apart:
        for store in stores:
            store.start()
    for store in stores:
        store.wait()


def spectra(half, place, echoes, members, sides, apart, steps=STEPS):
    _, elements, pulses, gates = echoes.shape
    devices = 2 * members * sides
    bins = pulses // devices
    table = doppler_table(pulses)
    table = table.transpose(2, 1, 0, 3).reshape(devices, bins, 2, 2 * pulses)
    table = table.transpose(0, 2, 1, 3).reshape(2, members, sides * 2 * bins, 2 * pulses)
    block = (sides, elements // 2, 4 * bins, gates)
    anywhere = pl.BlockSpec(memory_space=pl.ANY)
    count = members if apart else 1
    shape = jax.ShapeDtypeStruct(block if apart else (members, *block), jnp.bfloat16)
    return pl.pallas_call(
        functools.partial(spectra_body, apart=apart),
        in_specs=[pl.BlockSpec(memory_space=pltpu.SMEM)] * 2 + [anywhere, anywhere],
        out_specs=[anywhere] * count,
        out_shape=[shape] * count,
        scratch_shapes=[
            pltpu.VMEM(table.shape[1:], jnp.bfloat16),
            pltpu.VMEM(echoes.shape, jnp.bfloat16),
            pltpu.VMEM((members, *block), jnp.bfloat16),
            pltpu.SemaphoreType.DMA(()),
            pltpu.SemaphoreType.DMA((steps,)),
            pltpu.SemaphoreType.DMA((members if apart else steps,)),
        ],
        compiler_params=pltpu.CompilerParams(vmem_limit_bytes=SPECTRA_VMEM),
        name="spectra",
    )(half, place, jnp.asarray(table), echoes)


def spread_body(weight_ref, out_ref, *, bins):
    beams = weight_ref.shape[1]
    elements = weight_ref.shape[2]
    own = out_ref.shape[2]
    group = 128
    width = group * 2 * bins
    lane = lax.broadcasted_iota(jnp.int32, (group, width), 1)
    row = lax.broadcasted_iota(jnp.int32, (group, width), 0)
    repeat = jnp.where(lane // (2 * bins) == row, 1.0, 0.0).astype(jnp.bfloat16)
    col = lax.broadcasted_iota(jnp.int32, (beams, width), 1)
    is_real = (col // bins) % 2 == 0
    for at in range(elements // group):
        span = slice(at * group, (at + 1) * group)
        real = jnp.dot(weight_ref[0, :, span], repeat, preferred_element_type=jnp.float32)
        imag = jnp.dot(weight_ref[1, :, span], repeat, preferred_element_type=jnp.float32)
        to_real = jnp.where(is_real, real, -imag).astype(jnp.bfloat16)
        to_imag = jnp.where(is_real, imag, real).astype(jnp.bfloat16)
        for n in range(width // own):
            out_ref[at * (width // own) + n, :beams] = to_real[:, n * own : (n + 1) * own]
            out_ref[at * (width // own) + n, beams:] = to_imag[:, n * own : (n + 1) * own]


def spread(beam_weights, bins, members):
    _, beams, elements = beam_weights.shape
    return pl.pallas_call(
        functools.partial(spread_body, bins=bins),
        in_specs=whole_vmem(1),
        out_specs=whole_vmem(1)[0],
        out_shape=jax.ShapeDtypeStruct((members, 2 * beams, elements // members * 2 * bins), jnp.bfloat16),
        compiler_params=pltpu.CompilerParams(vmem_limit_bytes=SMALL_VMEM),
        name="spread",
    )(beam_weights)


def beam_sums(blocks, weights, bins):
    received = jnp.concatenate(
        [
            jnp.concatenate([block[j].reshape(-1, block.shape[3]) for block in blocks], axis=0)
            for j in range(blocks[0].shape[0])
        ],
        axis=1,
    )
    weights = jnp.concatenate(weights, axis=1)
    own = lax.broadcasted_iota(jnp.int32, weights.shape, 1) % bins
    return [
        jnp.dot(
            jnp.where(own == d, weights, jnp.zeros_like(weights)),
            received,
            preferred_element_type=jnp.float32,
        )
        for d in range(bins)
    ]


def crossing_body(place_ref, side_ref, spread_ref, *refs):
    *block_refs, same_ref, other_ref = refs
    bins, _, gates = same_ref.shape
    place, first_side = place_ref[0], side_ref[0] == 0
    weights = [spread_ref[place ^ n] for n in far_first(len(block_refs))]
    for d, value in enumerate(beam_sums([ref[...] for ref in block_refs], weights, bins)):
        first, second = value[:, :gates], value[:, gates:]
        same_ref[d] = jnp.where(first_side, first, second).astype(same_ref.dtype)
        other_ref[d] = jnp.where(first_side, second, first).astype(other_ref.dtype)


def crossing_sums(place, side, blocks, spread_weights, bins):
    shape = jax.ShapeDtypeStruct((bins, spread_weights.shape[1], blocks[0].shape[3]), jnp.bfloat16)
    return pl.pallas_call(
        crossing_body,
        in_specs=[pl.BlockSpec(memory_space=pltpu.SMEM)] * 2 + whole_vmem(1 + len(blocks)),
        out_specs=whole_vmem(2),
        out_shape=[shape, shape],
        compiler_params=pltpu.CompilerParams(vmem_limit_bytes=BEAMS_VMEM),
        name="crossing_sums",
    )(place, side, spread_weights, *blocks)


def split(value):
    high = value.astype(jnp.bfloat16)
    return high, (value - high.astype(jnp.float32)).astype(jnp.bfloat16)


NT = (((1,), (1,)), ((), ()))


def c_mul(a, b):
    return a[0] * b[0] - a[1] * b[1], a[0] * b[1] + a[1] * b[0]
def c_mulc(a, b):
    return a[0] * b[0] + a[1] * b[1], a[1] * b[0] - a[0] * b[1]
def conj(a): return a[0], -a[1]
def c_add(a, b): return a[0] + b[0], a[1] + b[1]
def c_sub(a, b): return a[0] - b[0], a[1] - b[1]
def scale(a, r): return a[0] * r, a[1] * r

def inverse_pair(m):
    a, b, d = m
    r = 1.0 / (a * d - (b[0] * b[0] + b[1] * b[1]))
    return d * r, (-b[0] * r, -b[1] * r), a * r

def inverse_four(e):
    ea, eb, ed = inverse_pair((e[0][0][0], e[0][1], e[1][1][0]))
    f = [[e[0][2], e[0][3]], [e[1][2], e[1][3]]]
    t = [[None, None], [None, None]]
    for l in range(2):
        t[0][l] = c_add(scale(f[0][l], ea), c_mul(eb, f[1][l]))
        t[1][l] = c_add(c_mulc(f[0][l], eb), scale(f[1][l], ed))
    def herm(l, m):
        return c_add(c_mulc(t[0][m], f[0][l]), c_mulc(t[1][m], f[1][l]))
    def herm_re(l):
        return (t[0][l][0]*f[0][l][0] + t[0][l][1]*f[0][l][1]) + (t[1][l][0]*f[1][l][0] + t[1][l][1]*f[1][l][1])
    s = (e[2][2][0] - herm_re(0), c_sub(e[2][3], herm(0, 1)), e[3][3][0] - herm_re(1))
    sa, sb, sd = inverse_pair(s)
    u = [[None, None], [None, None]]
    for j in range(2):
        x = c_add(scale(t[j][0], sa), c_mulc(t[j][1], sb))
        y = c_add(c_mul(t[j][0], sb), scale(t[j][1], sd))
        u[j][0] = (-x[0], -x[1]); u[j][1] = (-y[0], -y[1])
    def corr(j, m):
        return c_add(c_mulc(u[j][0], t[m][0]), c_mulc(u[j][1], t[m][1]))
    zero = jnp.zeros_like(ea)
    p00 = ea - corr(0, 0)[0]; p11 = ed - corr(1, 1)[0]
    p01 = c_sub(eb, corr(0, 1))
    inv = [[None]*4 for _ in range(4)]
    inv[0][0] = (p00, None); inv[1][1] = (p11, None); inv[0][1] = p01
    inv[2][2] = (sa, None); inv[3][3] = (sd, None); inv[2][3] = sb
    for j in range(2):
        for l in range(2): inv[j][2+l] = u[j][l]
    for j in range(4):
        for l in range(j): inv[j][l] = conj(inv[l][j])
    return inv


def turn(x):
    half = x.shape[1] // 2
    lane = lax.broadcasted_iota(jnp.int32, x.shape, 1)
    y = pltpu.roll(x, half, 1)
    return jnp.where(lane < half, -y, y)


def sweep(rows, columns, updated):
    shape = rows[0].shape
    beams = shape[1] // 2
    lane = lax.broadcasted_iota(jnp.int32, shape, 1)
    upper = lax.broadcasted_iota(jnp.int32, shape, 0) < 4

    def col(x, k):
        return jnp.broadcast_to(x[:, k : k + 1], shape)

    first = lane < beams
    base = jnp.where(first, 0, beams)

    def pick(x, k):
        return jnp.take_along_axis(x, base + k, axis=1, mode="promise_in_bounds")

    for step, k in enumerate(columns):
        inside = ((lane >= k) & (lane < k + 4)) | ((lane >= beams + k) & (lane < beams + k + 4))
        pivot = []
        for q in (2 * step, 2 * step + 1):
            x = rows[q]
            y = pltpu.roll(x, 4, 0)
            pivot += [jnp.where(upper, x, y), jnp.where(upper, y, x)]
        entry = [[None] * 4 for _ in range(4)]
        for j in range(4):
            for l in range(j, 4):
                entry[j][l] = (col(pivot[j], k + l), col(pivot[j], beams + k + l) if l > j else None)
        inv = inverse_four(entry)
        unit = [jnp.where(lane == k + l, 1.0, jnp.where(inside, 0.0, pivot[l])) for l in range(4)]
        turned = [turn(x) for x in unit]
        b, bt = [], []
        for j in range(4):
            acc, tacc = unit[j] * inv[j][j][0], turned[j] * inv[j][j][0]
            for l in range(4):
                if l != j:
                    acc = acc + (unit[l] * inv[j][l][0] + turned[l] * inv[j][l][1])
                    tacc = tacc + (turned[l] * inv[j][l][0] - unit[l] * inv[j][l][1])
            b.append(acc)
            bt.append(tacc)
        same = [jnp.where(first, b[l], bt[l]) for l in range(4)]
        cross = [-jnp.where(first, bt[l], b[l]) for l in range(4)]
        for q in sorted(updated(step), key=lambda q: q // 2 != step + 1):
            x = rows[q]
            kept = jnp.where(inside, 0.0, x)
            if q // 2 == step + 1:
                for l in range(4):
                    kept = kept - (col(x, k + l) * b[l] + col(x, beams + k + l) * bt[l])
                rows[q] = kept
            else:
                both = [pick(x, k + l) for l in range(4)]
                straight = (both[0] * same[0] + both[1] * same[1]) + (both[2] * same[2] + both[3] * same[3])
                swapped = (both[0] * cross[0] + both[1] * cross[1]) + (both[2] * cross[2] + both[3] * cross[3])
                rows[q] = (kept - straight) - pltpu.roll(swapped, beams, 1)
        for q in (0, 1):
            rows[2 * step + q] = jnp.where(upper, b[2 * q], b[2 * q + 1])
    return rows


def eliminate(systems, sources, rows_ref, size=BLOCK):
    count = len(systems)
    beams = systems[0].shape[0]
    blocks = size // 2
    rest = [
        jnp.concatenate([systems[n], jnp.broadcast_to(sources[n], (8, 2 * beams))], axis=0) for n in range(count)
    ]
    for first in range(0, beams, size):
        base = count * first
        for n in range(count):
            rows_ref[pl.ds(base + n, size, stride=count), :] = rest[n][:size]
        rows = [rows_ref[base + 8 * q : base + 8 * q + 8] for q in range(blocks)]
        columns = range(first, first + size, 4)
        if first + size == beams:
            bottoms = [value[size : size + 1] for value in rest]
            rows.append(jnp.concatenate(bottoms + bottoms, axis=0))
            return sweep(rows, columns, lambda step: range(2 * step + 2, blocks + 1))[blocks]
        rows = sweep(rows, columns, lambda step: [q for q in range(blocks) if q // 2 != step])
        for q in range(blocks):
            rows_ref[base + 8 * q : base + 8 * q + 8] = rows[q]
        at = (lax.broadcasted_iota(jnp.int32, rest[0][size:].shape, 1) - first) % beams
        for n in range(count):
            top = rows_ref[pl.ds(base + n, size, stride=count), :]
            value = rest[n][size:]
            taken = jnp.dot(
                packed_left(value, at, size), packed_right(top, first), preferred_element_type=jnp.float32
            )
            rest[n] = jnp.where(at < size, 0.0, value) - taken


def packed_left(value, at, size):
    high, low = (part.astype(jnp.float32) for part in split(value))
    again = jnp.where(at < 2 * size, pltpu.roll(low, size, 1), pltpu.roll(high, 2 * size, 1))
    return jnp.where(at < size, high, again).astype(jnp.bfloat16)


def packed_right(top, first):
    size, width = top.shape
    count = width // size
    pieces = [jnp.zeros(top.shape, jnp.bfloat16)] * count
    for start, rows in ((first, top), (first + width // 2, turn(top))):
        high, low = split(rows)
        for step, piece in enumerate((high, high, low)):
            pieces[(start // size + step) % count] = piece
    return jnp.concatenate(pieces, axis=0)


def beams_body(
    side_ref, spectra_ref, spread_ref, same_ref, other_ref, pulse_ref, steer_ref, own_ref, send_ref, rows_ref
):
    bins, total, half = same_ref.shape
    beams = total // 2
    ranges = spectra_ref.shape[1]
    gates = ranges * half
    first_side = side_ref[0] == 0
    members = range(spectra_ref.shape[0])
    near = beam_sums([spectra_ref[n] for n in members], [spread_ref[n] for n in members], bins)
    sums = []
    for d in range(bins):
        same, other = same_ref[d].astype(jnp.float32), other_ref[d].astype(jnp.float32)
        far = [jnp.where(first_side, same, other), jnp.where(first_side, other, same)]
        sums.append(near[d] + jnp.concatenate(far, axis=1))
    high, low = split(
        jnp.concatenate(
            [
                jnp.concatenate(
                    [
                        value[part * beams : (part + 1) * beams, block * half : (block + 1) * half]
                        for block in range(ranges)
                        for part in range(2)
                    ],
                    axis=1,
                )
                for value in sums
            ],
            axis=0,
        )
    )
    formed = [0.0] * ranges
    for block in range(ranges):
        into = slice(block * 2 * half, (block + 1) * 2 * half)
        pulse = pulse_ref[block * 2 * half :, into]
        for piece in (high, low):
            formed[block] = formed[block] + jnp.dot(
                piece[:, block * 2 * half :], pulse, preferred_element_type=jnp.float32
            )
    sub = lax.broadcasted_iota(jnp.int32, (beams, 2 * beams), 0)
    lane = lax.broadcasted_iota(jnp.int32, (beams, 2 * beams), 1)
    both, systems = [], []
    for d in range(bins):
        mine = slice(d * beams, (d + 1) * beams)
        real = jnp.concatenate([value[mine, :half] for value in formed], axis=1)
        imag = jnp.concatenate([value[mine, half:] for value in formed], axis=1)
        top = jnp.concatenate([real, imag], axis=1)
        t_high, t_low = split(top)
        u_high, u_low = split(jnp.concatenate([-imag, real], axis=1))
        left = jnp.concatenate([t_high, t_low], axis=0)
        both.append(left)
        products = lax.dot_general(
            left, jnp.concatenate([t_high, u_high, t_low, u_low], axis=0), NT, preferred_element_type=jnp.float32
        )
        cov = (
            products[:beams, : 2 * beams] + products[:beams, 2 * beams :] + products[beams:, : 2 * beams]
        )
        cov = cov * (1.0 / gates)
        on_diagonal = sub == lane
        trace = jnp.sum(jnp.where(on_diagonal, cov, 0.0), axis=(0, 1), keepdims=True)
        loading = load_ratio * trace / beams + epsilon
        cov = jnp.where(on_diagonal, cov + loading, cov) * (1.0 / loading)
        systems.append(cov)
    steer = steer_ref[...]
    sources = [steer[d : d + 1] for d in range(bins)]
    conj = -eliminate(systems, sources, rows_ref)[:bins]
    response = jnp.sum(conj * steer, axis=1, keepdims=True)
    weight = conj / response
    part_of = lax.broadcasted_iota(jnp.int32, weight.shape, 1) < beams
    other = pltpu.roll(weight, beams, 1)
    pieces = []
    for twice in (jnp.where(part_of, weight, other), jnp.where(part_of, other, weight)):
        w_high, w_low = split(twice)
        pieces += [w_high, jnp.where(part_of, w_low, jnp.zeros_like(w_low))]
    left = jnp.concatenate(pieces, axis=0)
    row = lax.broadcasted_iota(jnp.int32, (bins, 2 * gates), 0)
    by_real = by_imag = jnp.zeros((bins, 2 * gates), jnp.float32)
    for d in range(bins):
        out = jnp.dot(left, both[d], preferred_element_type=jnp.float32)
        by_real = jnp.where(row == d, out[:bins] + out[bins : 2 * bins], by_real)
        by_imag = jnp.where(row == d, out[2 * bins : 3 * bins] + out[3 * bins :], by_imag)
    joined = (
        by_real[:, :gates] - by_imag[:, gates:],
        by_real[:, gates:] + by_imag[:, :gates],
    )
    nothing = jnp.zeros((bins, half), jnp.float32)
    for part in range(2):
        first, second = joined[part][:, :half], joined[part][:, half:]
        own_ref[part] = jnp.concatenate(
            [jnp.where(first_side, first, nothing), jnp.where(first_side, nothing, second)], axis=0
        )
        send_ref[part] = jnp.concatenate(
            [jnp.where(first_side, second, nothing), jnp.where(first_side, nothing, first)], axis=0
        )


def on_device_owned(echoes, replica, beam_weights, steering):
    elems, ranges = lax.axis_size("elem"), lax.axis_size("range")
    devices = elems * ranges
    _, own_elements, pulses, gate_count = echoes.shape
    bins = pulses // devices
    elements = beam_weights.shape[2]
    gates = gate_count * ranges
    side = lax.axis_index("range")
    half = lax.axis_index("elem") // (elems // 2)
    group = devices // 2
    members = elems // 2
    place, far_half, near_half, seat = (
        value.reshape(1).astype(jnp.int32)
        for value in (lax.axis_index("elem") % members, 1 - half, half, side)
    )
    here = lax.dynamic_slice_in_dim(beam_weights, half * (elements // 2), elements // 2, 2)
    spread_weights = spread(here, bins, members)
    blocks = spectra(far_half, place, echoes, members, ranges, True)
    blocks = [
        block if n == 0 else lax.ppermute(block, "elem", [(m, m ^ n) for m in range(elems)])
        for n, block in zip(far_first(members), blocks)
    ]
    (sent,) = spectra(near_half, place, echoes, members, ranges, False)
    sent, *blocks[1:] = lax.optimization_barrier((sent, *blocks[1:]))
    same, other = crossing_sums(place, seat, blocks, spread_weights, bins)
    across = [(n + group) % devices for n in range(devices)]
    same = lax.ppermute(same, ("elem", "range"), list(enumerate(across)))
    other = lax.ppermute(other, ("elem", "range"), [(n, to ^ 1) for n, to in enumerate(across)])
    near = lax.all_to_all(
        sent.reshape(group, *sent.shape[2:]),
        ("elem", "range"),
        0,
        0,
        tiled=True,
        axis_index_groups=[list(range(group)), list(range(group, devices))],
    )
    near = near.reshape(members, ranges, own_elements // 2, 4 * bins, gate_count)
    pulse = pulse_kernel(replica, gates)[:, :, :gates]
    pulse = pulse.reshape(2, 2, ranges, gate_count, ranges, gate_count)
    pulse = pulse.transpose(2, 0, 3, 4, 1, 5).reshape(2 * gates, 2 * gates)
    own_steering = lax.dynamic_slice_in_dim(steering, side * bins, bins, 1)
    steer_row = jnp.concatenate([own_steering[0], -own_steering[1]], axis=1)
    shape = jax.ShapeDtypeStruct((2, 2 * bins, gate_count), jnp.float32)
    own, send = pl.pallas_call(
        beams_body,
        in_specs=[pl.BlockSpec(memory_space=pltpu.SMEM)] + whole_vmem(6),
        out_specs=whole_vmem(2),
        out_shape=[shape, shape],
        scratch_shapes=[pltpu.VMEM((bins * beam_weights.shape[1], 2 * beam_weights.shape[1]), jnp.float32)],
        compiler_params=pltpu.CompilerParams(vmem_limit_bytes=BEAMS_VMEM),
        name="beams",
    )(seat, near, spread_weights, same, other, pulse, steer_row)
    return own + lax.ppermute(send, "range", [(0, 1), (1, 0)])


def on_device(echoes, replica, beam_weights, steering):
    elems, ranges = lax.axis_size("elem"), lax.axis_size("range")
    pulses, gate_count = echoes.shape[2:]
    beams, elements = beam_weights.shape[1:]
    owned = (
        ranges == 2
        and pulses == 4 * elems * ranges
        and gate_count % 128 == 0
        and beams == 64
        and elems % 2 == 0
        and elems & (elems - 1) == 0
        and 128 % echoes.shape[1] == 0
        and elements % 256 == 0
        and echoes.shape[1] % 8 == 0
        and replica.shape[1] <= gate_count
    )
    run = on_device_owned if owned else on_device_general
    return run(echoes, replica, beam_weights, steering)


def solution(mesh):
    return jax.shard_map(
        on_device,
        mesh=mesh,
        in_specs=(P(None, "elem", None, "range"), P(), P(), P(None, "elem", None)),
        out_specs=P(None, "elem", "range"),
        check_vma=False,
    )
```
